32 devices in a mesh: dp: 16 (over z, x, core), tensor: 2 (over y).
Axes of the slice: x: 2, y: 2, z: 4, core: 2. Of those that a mesh axis runs over, the one named last changes fastest.
Arguments:
- block_in: bfloat16 [16384, 1024], P('dp'), may hold values from -6 to 6
- cotangent: bfloat16 [16384, 1024], P('dp'), may hold values from -8 to 8
- lengths: int32 [16, 4], P('dp'), may hold values from 1 to 512, 1024 in all within a row
- pad_count: int32 [16], P('dp'), may hold values from 0 to 255
- norm_in_attn: float32 [1024], replicated, may hold values from 0.5 to 1.5
- w_query: bfloat16 [1024, 1024], P(None, 'tensor'), may hold values from -0.1875 to 0.1875
- w_key: bfloat16 [1024, 1024], P(None, 'tensor'), may hold values from -0.1875 to 0.1875
- w_value: bfloat16 [1024, 1024], P(None, 'tensor'), may hold values from -0.1875 to 0.1875
- w_out: bfloat16 [1024, 1024], P('tensor'), may hold values from -0.1875 to 0.1875
- norm_out_attn: float32 [1024], replicated, may hold values from 0.5 to 1.5
- norm_in_mlp: float32 [1024], replicated, may hold values from 0.5 to 1.5
- w_up: bfloat16 [1024, 4096], P(None, 'tensor'), may hold values from -0.1875 to 0.1875
- w_down: bfloat16 [4096, 1024], P('tensor'), may hold values from -0.09375 to 0.09375
- norm_out_mlp: float32 [1024], replicated, may hold values from 0.5 to 1.5
Outputs:
- block_out: bfloat16 [16384, 1024], P('dp')
- grad_in: float32 [16384, 1024], P('dp')
- grad_norm_in_attn: float32 [1024], P('dp')
- grad_query: float32 [1024, 1024], P('dp', 'tensor')
- grad_key: float32 [1024, 1024], P('dp', 'tensor')
- grad_value: float32 [1024, 1024], P('dp', 'tensor')
- grad_out_proj: float32 [1024, 1024], P('tensor', 'dp')
- grad_norm_out_attn: float32 [1024], P('dp')
- grad_norm_in_mlp: float32 [1024], P('dp')
- grad_up: float32 [1024, 4096], P('dp', 'tensor')
- grad_down: float32 [4096, 1024], P('tensor', 'dp')
- grad_norm_out_mlp: float32 [1024], P('dp')
The draws below stay inside these ranges and needn't reach their ends.
Inputs may be any that keep to these rules, and one draw needn't show every extreme that they name: Each row's 4 lengths sum to 1024, and the longest document of every row has exactly half of 1024 tokens. The last pad_count positions of a row are padding; they may cut into the last documents.
All inputs are finite; a program needn't handle non-finite values.
Results may differ from the reference program's by a relative error of at most 0.014.
Values sent between devices are 32-bit elements; how exact they have to be, the bound alone decides.
No kernel may reach another device: no remote copies, remote signals or barrier semaphores. Data moves between devices by JAX's collectives and lax.ppermute only.
A program may use at most 192 MiB of HBM per device.

```python
import math
import jax
import jax.numpy as jnp
import numpy as np
from jax import lax

D = 1024
HEADS = 16
HEAD_DIM = 64
FF = 4096
ROW_LEN = 1024
DOCS = 4
ROWS = 16
TOKENS = 16384


def plant(values, stream_key, smallest, high):
    longest = values.shape.index(max(values.shape))
    spots = []
    for shift in (0, 1):
        where = [jax.random.randint(jax.random.fold_in(stream_key, axis), (), 0, length) for axis, length in enumerate(values.shape)]
        where[longest] = (where[longest] + shift) % values.shape[longest]
        spots.append(tuple(where))
    return values.at[spots[0]].set(smallest).at[spots[1]].set(high)


def spiked(array, key, source, target, shards_of, factor):
    owner, partner = [(jnp.arange(array.shape[dim]) // (array.shape[dim] // shards_of)).reshape([-1 if axis == dim else 1 for axis in range(array.ndim)]) for dim in (source, target)]
    chosen = jax.random.permutation(key, shards_of)[partner]
    strong = (owner == chosen) | (owner == (partner + shards_of // 2) % shards_of)
    return jnp.where(strong, factor * array, array)


def level_of(stream_key, extent, cuts, smallest, top_value):
    loudness = 1.0
    for dim, blocks in cuts:
        steps = jax.random.uniform(jax.random.fold_in(jax.random.fold_in(stream_key, 6), dim), (blocks,), jnp.float32, smallest / len(cuts), top_value / len(cuts))
        loudness = loudness * jnp.repeat(jnp.exp(steps), extent[dim] // blocks).reshape((-1,) + (1,) * (len(extent) - 1 - dim))
    return loudness


def length_profile(number_of, total, limit, skew):
    portions = [(1 << 20) // math.isqrt(grade ** skew) + 1 for grade in range(2, number_of + 1)]
    rest, given = total - limit - (number_of - 1), [1] * (number_of - 1)
    while rest > 0:
        candidates = [i for i in range(number_of - 1) if given[i] < limit]
        mass, left = sum([portions[i] for i in candidates]), rest
        for i in candidates:
            more = min(limit - given[i], max(1, left * portions[i] // mass), rest)
            given[i] = given[i] + more
            rest = rest - more
    return np.array([limit] + given)


def ragged(key, number_of, total, bound, skew):
    if number_of == 2:
        one = jax.random.randint(key, (), max(1, total - bound), min(bound, total - 1) + 1)
        return jnp.stack([one, total - one])
    tallies = jnp.asarray(length_profile(number_of, total, bound, skew), jnp.int32)
    couples = (number_of - 1) // 2
    donor, receiver = tallies[1:1 + 2 * couples:2], tallies[2:2 + 2 * couples:2]
    margin = jnp.minimum(donor - 1, bound - receiver)
    passed = jax.random.randint(jax.random.fold_in(key, 1), (couples,), 0, 1 << 20) % (margin + 1)
    tallies = tallies.at[1:1 + 2 * couples:2].set(donor - passed).at[2:2 + 2 * couples:2].set(receiver + passed)
    return tallies[jax.random.permutation(jax.random.fold_in(key, 2), number_of)]


def scatter_about(own_key, extent, spread, limit, cuts=(), held_as=jnp.bfloat16):
    drawn = jax.random.normal(own_key, extent, jnp.float32) * spread
    if len(cuts) > 0:
        drawn = level_of(own_key, extent, cuts, -0.22, 0.18) * drawn
    return jnp.clip(drawn, min=-limit, max=limit).astype(held_as)


def heavy_noise(stream_key, dims, deviation, bound, pieces, heavy, kind=jnp.bfloat16):
    values = deviation * jax.random.normal(stream_key, dims, jnp.float32)
    if pieces:
        values = values * level_of(stream_key, dims, pieces, -0.22, 0.18)
    return jnp.clip(spiked(values, jax.random.fold_in(stream_key, 3), *heavy), -bound, bound).astype(kind)


def setup_inputs(seed: int = 0) -> dict:
    streams_of = jax.random.split(jax.random.key(seed), 15)
    block_in = scatter_about(streams_of[0], (TOKENS, D), 1.0, 6.0, ((0, 16),))
    cotangent = heavy_noise(streams_of[1], (TOKENS, D), 1.0, 8.0, ((0, 16),), (0, 1, 16, 2.0))
    lengths = jax.vmap(lambda own: ragged(own, DOCS, ROW_LEN, ROW_LEN // 2, 2))(jax.random.split(streams_of[2], ROWS)).reshape((ROWS, DOCS)).astype(jnp.int32)
    pad_count = plant(jax.random.randint(streams_of[3], (ROWS,), 0, ROW_LEN // 4), jax.random.fold_in(streams_of[3], 1), 0, (ROW_LEN // 4) - 1).astype(jnp.int32)
    norm_in_attn = jnp.clip(1.0 + 0.1 * jax.random.normal(streams_of[4], (D,), jnp.float32), 0.5, 1.5)
    w_query = scatter_about(streams_of[5], (D, D), D ** -0.5, 0.1875, ((1, 2),))
    w_key = scatter_about(streams_of[6], (D, D), D ** -0.5, 0.1875, ((1, 2),))
    w_value = scatter_about(streams_of[7], (D, D), D ** -0.5, 0.1875, ((1, 2),))
    w_out = scatter_about(streams_of[8], (D, D), D ** -0.5, 0.1875, ((0, 2),))
    norm_out_attn = jnp.clip(1.0 + 0.1 * jax.random.normal(streams_of[9], (D,), jnp.float32), 0.5, 1.5)
    norm_in_mlp = jnp.clip(1.0 + 0.1 * jax.random.normal(streams_of[10], (D,), jnp.float32), 0.5, 1.5)
    w_up = scatter_about(streams_of[11], (D, FF), D ** -0.5, 0.1875, ((1, 2),))
    w_down = scatter_about(streams_of[12], (FF, D), FF ** -0.5, 0.09375, ((0, 2),))
    norm_out_mlp = jnp.clip(1.0 + 0.1 * jax.random.normal(streams_of[13], (D,), jnp.float32), 0.5, 1.5)
    return {"block_in": block_in, "cotangent": cotangent, "lengths": lengths, "pad_count": pad_count, "norm_in_attn": norm_in_attn, "w_query": w_query, "w_key": w_key, "w_value": w_value, "w_out": w_out, "norm_out_attn": norm_out_attn, "norm_in_mlp": norm_in_mlp, "w_up": w_up, "w_down": w_down, "norm_out_mlp": norm_out_mlp}


@jax.custom_vjp
def low(v):
    return lax.optimization_barrier(v.astype(jnp.bfloat16)).astype(jnp.float32)

@jax.custom_vjp
def low_back(v):
    return v

def low_keep(v):
    return (low(v), None)

def low_pass(kept, grad):
    return (grad,)

def back_keep(v):
    return (v, None)

def back_low(kept, grad):
    return (low(grad),)
low.defvjp(low_keep, low_pass)
low_back.defvjp(back_keep, back_low)

def layer_norm(values, gain):
    average = lax.optimization_barrier(jnp.mean(values, axis=-1, keepdims=True))
    centered = values - average
    variance = lax.optimization_barrier(jnp.mean(centered * centered, axis=-1, keepdims=True))
    return centered * lax.rsqrt(variance + 1e-05) * gain

def product(left, right):
    return jnp.dot(left, right, precision=lax.Precision.HIGHEST, preferred_element_type=jnp.float32)

def row_layout(lengths, pad_count, row_len):
    doc_ends = jnp.cumsum(lengths, axis=-1)
    doc_starts = doc_ends - lengths
    indices = jnp.arange(row_len, dtype=jnp.int32)
    segment = lax.optimization_barrier(jnp.sum((indices[None, :, None] >= doc_ends[:, None, :]).astype(jnp.int32), axis=-1))
    labels = jnp.arange(lengths.shape[-1], dtype=jnp.int32)
    offset = lax.optimization_barrier(jnp.sum(jnp.where(segment[:, :, None] == labels[None, None, :], doc_starts[:, None, :], 0), axis=-1))
    position = indices[None, :] - offset
    padded = indices[None, :] >= (row_len - pad_count)[:, None]
    return (segment, position, padded)

def rotate(values, position, direction):
    head_dim = values.shape[-1]
    half_dim = head_dim // 2
    frequency = 10000.0 ** (-2.0 * jnp.arange(half_dim, dtype=jnp.float32) / head_dim)
    angles = position.astype(jnp.float32)[..., None] * frequency
    cosine = jnp.cos(angles)[..., None, :]
    sine_part = direction * jnp.sin(angles)[..., None, :]
    first = values[..., :half_dim]
    second = values[..., half_dim:]
    return jnp.concatenate([first * cosine - second * sine_part, second * cosine + first * sine_part], axis=-1)

def row_attention(inputs):
    query_rows, key_rows, value_rows, segment, padded = inputs
    row_len = segment.shape[0]
    indices = jnp.arange(row_len, dtype=jnp.int32)
    allowed = (segment[:, None] == segment[None, :]) & (indices[None, :] <= indices[:, None])
    allowed = allowed & jnp.logical_not(padded[None, :]) & jnp.logical_not(padded[:, None])
    allowed = allowed | (indices[None, :] == indices[:, None])
    scores = jnp.einsum('qhd,khd->hqk', query_rows, key_rows, precision=lax.Precision.HIGHEST) * (1.0 / math.sqrt(HEAD_DIM))
    scores = low_back(scores)
    scores = jnp.where(allowed[None], scores, -1e+30)
    highest = lax.optimization_barrier(jnp.max(scores, axis=-1, keepdims=True))
    log_total = highest + jnp.log(lax.optimization_barrier(jnp.sum(jnp.exp(scores - highest), axis=-1, keepdims=True)))
    weights = low(jnp.exp(scores - log_total))
    return jnp.einsum('hqk,khd->qhd', weights, value_rows, precision=lax.Precision.HIGHEST)

def reference(block_in, cotangent, lengths, pad_count, norm_in_attn, w_query, w_key, w_value, w_out, norm_out_attn, norm_in_mlp, w_up, w_down, norm_out_mlp):
    row_count = lengths.shape[0]
    row_len = block_in.shape[0] // row_count
    segment, position, padded = row_layout(lengths, pad_count, row_len)

    def forward(inputs, gain_first, query_weight, key_weight, value_weight, out_weight, gain_second, gain_third, up_weight, down_weight, gain_fourth):
        attn_in = low(layer_norm(inputs, gain_first))

        def project(weight):
            return low_back(product(attn_in, weight)).reshape(row_count, row_len, HEADS, HEAD_DIM)
        query_rows = low(rotate(project(query_weight), position, 1.0))
        key_rows = low(rotate(project(key_weight), position, 1.0))
        value_rows = low(project(value_weight))
        attended = lax.map(jax.checkpoint(row_attention), (query_rows, key_rows, value_rows, segment, padded))
        attended = low(low_back(attended.reshape(inputs.shape[0], HEADS * HEAD_DIM)))
        attn_total = low_back(product(attended, out_weight))
        hidden_res = inputs + layer_norm(attn_total, gain_second)
        mlp_in = low(layer_norm(hidden_res, gain_third))
        up_pre = low_back(product(mlp_in, up_weight))
        activated = low(jax.nn.gelu(up_pre, approximate=True))
        mlp_total = low_back(product(activated, down_weight))
        return hidden_res + layer_norm(mlp_total, gain_fourth)
    floats = (block_in.astype(jnp.float32), norm_in_attn, w_query.astype(jnp.float32), w_key.astype(jnp.float32), w_value.astype(jnp.float32), w_out.astype(jnp.float32), norm_out_attn, norm_in_mlp, w_up.astype(jnp.float32), w_down.astype(jnp.float32), norm_out_mlp)
    result, pullback = jax.vjp(forward, *floats)
    grads = pullback(cotangent.astype(jnp.float32))
    return (result.astype(jnp.bfloat16), grads[0], grads[1], grads[2], grads[3], grads[4], grads[5], grads[6], grads[7], grads[8], grads[9], grads[10])
```

```python
from functools import partial
import math

import jax
import jax.numpy as jnp
from jax import lax
from jax.sharding import PartitionSpec as P

HEAD_DIM = 64


def norm_parts(values):
    average = jnp.mean(values, axis=-1, keepdims=True)
    centered = values - average
    inverse = lax.rsqrt(jnp.mean(centered * centered, axis=-1, keepdims=True) + 1e-05)
    return (centered * inverse, inverse)


def norm_back(grad_output, gain, normed, inverse):
    scaled = grad_output * gain
    mean_scaled = jnp.mean(scaled, axis=-1, keepdims=True)
    mean_cross = jnp.mean(scaled * normed, axis=-1, keepdims=True)
    return (
        inverse * (scaled - mean_scaled - normed * mean_cross),
        jnp.sum(grad_output * normed, axis=0),
    )


def row_layout(lengths, pad_count, row_len):
    ends = [lengths[:, 0]]
    for number in range(1, lengths.shape[-1]):
        ends.append(ends[-1] + lengths[:, number])
    doc_ends = jnp.stack(ends, axis=-1)
    doc_starts = doc_ends - lengths
    indices = jnp.arange(row_len, dtype=jnp.int32)
    segment = jnp.sum((indices[None, :, None] >= doc_ends[:, None, :]).astype(jnp.int32), axis=-1)
    labels = jnp.arange(lengths.shape[-1], dtype=jnp.int32)
    offset = jnp.sum(
        jnp.where(segment[:, :, None] == labels[None, None, :], doc_starts[:, None, :], 0), axis=-1
    )
    position = indices[None, :] - offset
    padded = indices[None, :] >= (row_len - pad_count)[:, None]
    return (segment, position, padded)


def rotate(values, position, direction):
    head_dim = values.shape[-1]
    half_dim = head_dim // 2
    frequency = 10000.0 ** (-2.0 * jnp.arange(half_dim, dtype=jnp.float32) / head_dim)
    angles = position.astype(jnp.float32)[..., None] * frequency
    cosine = jnp.cos(angles)[..., None, :]
    sine_part = direction * jnp.sin(angles)[..., None, :]
    first = values[..., :half_dim]
    second = values[..., half_dim:]
    return jnp.concatenate(
        [first * cosine - second * sine_part, second * cosine + first * sine_part], axis=-1
    )


def allowed_block(segment, padded, row_start, query_count, key_count):
    query_index = row_start + jnp.arange(query_count, dtype=jnp.int32)
    key_index = jnp.arange(key_count, dtype=jnp.int32)
    query_segment = segment[:, row_start : row_start + query_count]
    allowed = (query_segment[:, :, None] == segment[:, None, :key_count]) & (
        key_index[None, None, :] <= query_index[None, :, None]
    )
    allowed = (
        allowed
        & jnp.logical_not(padded[:, None, :key_count])
        & jnp.logical_not(padded[:, row_start : row_start + query_count, None])
    )
    allowed = allowed | (key_index[None, None, :] == query_index[None, :, None])
    return allowed[:, None]


def masked_scores(query_block, key_block, allowed, scale):
    scores = (
        jnp.einsum("rqhd,rkhd->rhqk", query_block, key_block, preferred_element_type=jnp.float32)
        * scale
    )
    return jnp.where(allowed, scores, -1e30)


def pair_sum(values):
    return values + lax.ppermute(values, "tensor", [(0, 1), (1, 0)])


def body(
    block_in,
    cotangent,
    lengths,
    pad_count,
    norm_in_attn,
    w_query,
    w_key,
    w_value,
    w_out,
    norm_out_attn,
    norm_in_mlp,
    w_up,
    w_down,
    norm_out_mlp,
):
    row_count = lengths.shape[0]
    tokens_here = block_in.shape[0]
    row_len = tokens_here // row_count
    head_dim = HEAD_DIM
    local_heads = w_query.shape[1] // head_dim
    scale = 1.0 / math.sqrt(head_dim)
    block_rows = min(512, row_len)
    block_count = row_len // block_rows
    segment, position, padded = row_layout(lengths, pad_count, row_len)
    allowed_list = [
        allowed_block(segment, padded, number * block_rows, block_rows, (number + 1) * block_rows)
        for number in range(block_count)
    ]
    inputs = block_in.astype(jnp.float32)
    input_hat, input_inv = norm_parts(inputs)
    attn_in = (input_hat * norm_in_attn).astype(jnp.bfloat16)

    def project(weight):
        return jnp.dot(attn_in, weight, preferred_element_type=jnp.float32).reshape(
            row_count, row_len, local_heads, head_dim
        )

    query_rows = rotate(project(w_query), position, 1.0).astype(jnp.bfloat16)
    key_rows = rotate(project(w_key), position, 1.0).astype(jnp.bfloat16)
    value_rows = project(w_value).astype(jnp.bfloat16)
    log_totals = []
    head_outputs = []
    for number in range(block_count):
        row_start = number * block_rows
        row_stop = row_start + block_rows
        scores = masked_scores(
            query_rows[:, row_start:row_stop], key_rows[:, :row_stop], allowed_list[number], scale
        )
        highest = jnp.max(scores, axis=-1, keepdims=True)
        log_total = highest + jnp.log(jnp.sum(jnp.exp(scores - highest), axis=-1, keepdims=True))
        softmax_block = jnp.exp(scores - log_total)
        log_totals.append(log_total)
        head_outputs.append(
            jnp.einsum(
                "rhqk,rkhd->rqhd",
                softmax_block.astype(jnp.bfloat16),
                value_rows[:, :row_stop],
                preferred_element_type=jnp.float32,
            )
        )
    attended = (
        jnp.concatenate(head_outputs, axis=1)
        .reshape(tokens_here, local_heads * head_dim)
        .astype(jnp.bfloat16)
    )
    attn_part = jnp.dot(attended, w_out, preferred_element_type=jnp.float32)
    attn_total = pair_sum(attn_part)
    attn_hat, attn_inv = norm_parts(attn_total)
    hidden_res = inputs + attn_hat * norm_out_attn
    mlp_hat, mlp_inv = norm_parts(hidden_res)
    mlp_in = (mlp_hat * norm_in_mlp).astype(jnp.bfloat16)
    up_pre = jnp.dot(mlp_in, w_up, preferred_element_type=jnp.float32)
    activated = jax.nn.gelu(up_pre, approximate=True).astype(jnp.bfloat16)
    mlp_part = jnp.dot(activated, w_down, preferred_element_type=jnp.float32)
    mlp_total = pair_sum(mlp_part)
    out_hat, out_inv = norm_parts(mlp_total)
    block_out = (hidden_res + out_hat * norm_out_mlp).astype(jnp.bfloat16)
    grad_output = cotangent.astype(jnp.float32)
    grad_mlp, gain_out_mlp = norm_back(grad_output, norm_out_mlp, out_hat, out_inv)
    grad_mlp_low = grad_mlp.astype(jnp.bfloat16)
    grad_act = jnp.einsum("td,fd->tf", grad_mlp_low, w_down, preferred_element_type=jnp.float32)
    gelu_value, gelu_pull = jax.vjp(partial(jax.nn.gelu, approximate=True), up_pre)
    grad_up_pre = gelu_pull(grad_act)[0].astype(jnp.bfloat16)
    weight_down = jnp.einsum(
        "tf,td->df", activated, grad_mlp_low, preferred_element_type=jnp.float32
    )
    weight_up = jnp.einsum("td,tf->df", mlp_in, grad_up_pre, preferred_element_type=jnp.float32)
    grad_mlp_part = jnp.einsum("tf,df->td", grad_up_pre, w_up, preferred_element_type=jnp.float32)
    grad_mlp_in = pair_sum(grad_mlp_part)
    grad_res_extra, gain_in_mlp = norm_back(grad_mlp_in, norm_in_mlp, mlp_hat, mlp_inv)
    grad_res = grad_output + grad_res_extra
    grad_attn, gain_out_attn = norm_back(grad_res, norm_out_attn, attn_hat, attn_inv)
    grad_attn_low = grad_attn.astype(jnp.bfloat16)
    weight_out = jnp.einsum(
        "te,td->de", attended, grad_attn_low, preferred_element_type=jnp.float32
    )
    grad_heads = jnp.einsum("td,ed->te", grad_attn_low, w_out, preferred_element_type=jnp.float32)
    grad_heads = grad_heads.astype(jnp.bfloat16).reshape(row_count, row_len, local_heads, head_dim)
    grad_query_blocks = []
    grad_key_total = jnp.zeros((row_count, row_len, local_heads, head_dim), jnp.float32)
    grad_value_total = jnp.zeros((row_count, row_len, local_heads, head_dim), jnp.float32)
    for number in range(block_count):
        row_start = number * block_rows
        row_stop = row_start + block_rows
        scores = masked_scores(
            query_rows[:, row_start:row_stop], key_rows[:, :row_stop], allowed_list[number], scale
        )
        softmax_block = jnp.exp(scores - log_totals[number])
        grad_block = grad_heads[:, row_start:row_stop]
        grad_soft = jnp.einsum(
            "rqhd,rkhd->rhqk",
            grad_block,
            value_rows[:, :row_stop],
            preferred_element_type=jnp.float32,
        )
        grad_scores = softmax_block * (
            grad_soft - jnp.sum(grad_soft * softmax_block, axis=-1, keepdims=True)
        )
        grad_scores = grad_scores.astype(jnp.bfloat16)
        grad_query_blocks.append(
            jnp.einsum(
                "rhqk,rkhd->rqhd",
                grad_scores,
                key_rows[:, :row_stop],
                preferred_element_type=jnp.float32,
            )
            * scale
        )
        key_term = (
            jnp.einsum(
                "rhqk,rqhd->rkhd",
                grad_scores,
                query_rows[:, row_start:row_stop],
                preferred_element_type=jnp.float32,
            )
            * scale
        )
        grad_key_total = grad_key_total.at[:, :row_stop].add(key_term)
        value_term = jnp.einsum(
            "rhqk,rqhd->rkhd",
            softmax_block.astype(jnp.bfloat16),
            grad_block,
            preferred_element_type=jnp.float32,
        )
        grad_value_total = grad_value_total.at[:, :row_stop].add(value_term)
    width_here = local_heads * head_dim
    grad_q = (
        rotate(jnp.concatenate(grad_query_blocks, axis=1), position, -1.0)
        .reshape(tokens_here, width_here)
        .astype(jnp.bfloat16)
    )
    grad_k = (
        rotate(grad_key_total, position, -1.0).reshape(tokens_here, width_here).astype(jnp.bfloat16)
    )
    grad_v = grad_value_total.reshape(tokens_here, width_here).astype(jnp.bfloat16)
    weight_query = jnp.einsum("td,te->de", attn_in, grad_q, preferred_element_type=jnp.float32)
    weight_key = jnp.einsum("td,te->de", attn_in, grad_k, preferred_element_type=jnp.float32)
    weight_value = jnp.einsum("td,te->de", attn_in, grad_v, preferred_element_type=jnp.float32)
    grad_attn_part = jnp.einsum("te,de->td", grad_q, w_query, preferred_element_type=jnp.float32)
    grad_attn_part = grad_attn_part + jnp.einsum(
        "te,de->td", grad_k, w_key, preferred_element_type=jnp.float32
    )
    grad_attn_part = grad_attn_part + jnp.einsum(
        "te,de->td", grad_v, w_value, preferred_element_type=jnp.float32
    )
    grad_attn_in = pair_sum(grad_attn_part)
    grad_in_extra, gain_in_attn = norm_back(grad_attn_in, norm_in_attn, input_hat, input_inv)
    grad_in = grad_res + grad_in_extra
    wide = w_query.shape[1]
    hidden = w_up.shape[1]
    gains = jnp.stack([gain_in_attn, gain_out_attn, gain_in_mlp, gain_out_mlp], axis=1)
    mlp_grads = lax.psum_scatter(
        jnp.concatenate([weight_up, weight_down], axis=1), "dp", scatter_dimension=0, tiled=True
    )
    attn_grads = lax.psum_scatter(
        jnp.concatenate([weight_query, weight_key, weight_value, weight_out, jnp.pad(gains, ((0, 0), (0, 124)))], axis=1),
        "dp",
        scatter_dimension=0,
        tiled=True,
    )
    gain_sums = attn_grads[:, 4 * wide :]
    summed = (
        attn_grads[:, :wide],
        attn_grads[:, wide : 2 * wide],
        attn_grads[:, 2 * wide : 3 * wide],
        attn_grads[:, 3 * wide : 4 * wide].T,
        mlp_grads[:, :hidden],
        mlp_grads[:, hidden:].T,
        gain_sums[:, 0],
        gain_sums[:, 1],
        gain_sums[:, 2],
        gain_sums[:, 3],
    )
    return (
        block_out,
        grad_in,
        summed[6],
        summed[0],
        summed[1],
        summed[2],
        summed[3],
        summed[7],
        summed[8],
        summed[4],
        summed[5],
        summed[9],
    )


def solution(mesh):
    placed = (
        P("dp", None),
        P("dp", None),
        P("dp", None),
        P("dp"),
        P(),
        P(None, "tensor"),
        P(None, "tensor"),
        P(None, "tensor"),
        P("tensor", None),
        P(),
        P(),
        P(None, "tensor"),
        P("tensor", None),
        P(),
    )
    return jax.shard_map(
        body,
        mesh=mesh,
        in_specs=placed,
        out_specs=(
            P("dp", None),
            P("dp", None),
            P("dp"),
            P("dp", "tensor"),
            P("dp", "tensor"),
            P("dp", "tensor"),
            P("tensor", "dp"),
            P("dp"),
            P("dp"),
            P("dp", "tensor"),
            P("tensor", "dp"),
            P("dp"),
        ),
        check_vma=False,
    )
```

```python
from functools import partial
import math

import jax
import jax.numpy as jnp
from jax import lax
from jax.experimental import pallas as pl
from jax.experimental.pallas import tpu as pltpu
from jax.sharding import PartitionSpec as P
import numpy as np

HEAD_DIM = 64


def half_columns(values, which, size):
    return lax.dynamic_slice_in_dim(values, which * size, size, axis=1)


def flat_pairs(count, target):
    pairs = []
    for row in range(count):
        for side in range(2):
            goal = target(row, row % 2, side)
            if goal is not None:
                pairs.append((row * 2 + side, goal[0] * 2 + goal[1]))
    return pairs


def send(values, pairs):
    return lax.ppermute(values, ("dp", "tensor"), pairs)


def half_of(values, which, size):
    return lax.dynamic_slice_in_dim(values, which * size, size, axis=0)


BLOCK = 256
LANES = 128
VMEM_LIMIT = 56 * 1024 * 1024


def doc_ends(lengths_ref, docs):
    ends = [lengths_ref[0, 0]]
    for number in range(1, docs):
        ends.append(ends[-1] + lengths_ref[0, number])
    return ends


def doc_start(index, ends):
    start = jnp.zeros_like(index)
    for end in ends:
        start = jnp.where(index >= end, end, start)
    return start


def first_key(index, ends, real):
    return jnp.where(index >= real, index, doc_start(index, ends))


def rope_tables(ends, row_len, freq_ref, cos_ref, sin_ref):
    index = lax.broadcasted_iota(jnp.int32, (1, row_len), 1)
    position = (index - doc_start(index, ends)).astype(jnp.float32)
    angles = freq_ref[...] * position
    cosine, sine = jnp.cos(angles), jnp.sin(angles)
    cos_ref[...] = jnp.concatenate([cosine] * 4, axis=0).T
    sin_ref[...] = jnp.concatenate([-sine, sine] * 2, axis=0).T


def turned(values, cosine, sine, low_half):
    ahead = pltpu.roll(values, LANES - HEAD_DIM // 2, 1)
    behind = pltpu.roll(values, HEAD_DIM // 2, 1)
    return values * cosine + jnp.where(low_half, ahead, behind) * sine


def normed(values):
    average = jnp.mean(values, axis=-1, keepdims=True)
    centered = values - average
    return centered * lax.rsqrt(jnp.mean(centered * centered, axis=-1, keepdims=True) + 1e-05)


def contract(left, right, left_dim, right_dim):
    return lax.dot_general(
        left, right, (((left_dim,), (right_dim,)), ((), ())), preferred_element_type=jnp.float32
    )


def prepare(docs, lengths_ref, freq_ref, rows_of, gain_ref, attn_in_ref, cos_ref, sin_ref):
    row_len = attn_in_ref.shape[0]

    @pl.when(pl.program_id(0) == 0)
    def _():
        rope_tables(doc_ends(lengths_ref, docs), row_len, freq_ref, cos_ref, sin_ref)
        for number in range(row_len // BLOCK):
            rows = pl.ds(number * BLOCK, BLOCK)
            attn_in_ref[rows, :] = (
                normed(rows_of(rows)) * gain_ref[...]
            ).astype(jnp.bfloat16)


def head_masks():
    lane = lax.broadcasted_iota(jnp.int32, (1, LANES), 1)
    return (lax.rem(lane, HEAD_DIM) < HEAD_DIM // 2, lane < HEAD_DIM)


def forward_kernel(docs, first, lengths_ref, pad_ref, freq_ref, gain_ref, *refs):
    if first:
        x_ref, wq_ref, wk_ref, wv_ref, out_ref, attn_in_ref, cos_ref, sin_ref, q_ref, k_ref, v_ref = refs
        row_len = x_ref.shape[0]
        prepare(
            docs, lengths_ref, freq_ref, lambda rows: x_ref[rows, :].astype(jnp.float32), gain_ref, attn_in_ref, cos_ref, sin_ref
        )
    else:
        attn_in_ref, cos_ref, sin_ref, wq_ref, wk_ref, wv_ref, out_ref, q_ref, k_ref, v_ref = refs
        row_len = attn_in_ref.shape[0]
    low_half, even = head_masks()
    group = wq_ref.shape[1]
    scale = 1.0 / math.sqrt(HEAD_DIM)
    for number in range(row_len // BLOCK):
        rows = pl.ds(number * BLOCK, BLOCK)
        block = attn_in_ref[rows, :]
        query = jnp.dot(block, wq_ref[...], preferred_element_type=jnp.float32)
        key = jnp.dot(block, wk_ref[...], preferred_element_type=jnp.float32)
        v_ref[rows, :] = jnp.dot(block, wv_ref[...], preferred_element_type=jnp.float32).astype(jnp.bfloat16)
        cosine, sine = cos_ref[rows, :], sin_ref[rows, :]
        for pair in range(group // LANES):
            cols = slice(pair * LANES, (pair + 1) * LANES)
            q_ref[rows, cols] = (turned(query[:, cols], cosine, sine, low_half) * scale).astype(jnp.bfloat16)
            k_ref[rows, cols] = turned(key[:, cols], cosine, sine, low_half).astype(jnp.bfloat16)
    ends = doc_ends(lengths_ref, docs)
    real = row_len - pad_ref[0]
    for number in range(row_len // BLOCK):
        rows = pl.ds(number * BLOCK, BLOCK)
        keys = (number + 1) * BLOCK
        query_index = number * BLOCK + lax.broadcasted_iota(jnp.int32, (BLOCK, 1), 0)
        start = first_key(query_index, ends, real)
        key_index = lax.broadcasted_iota(jnp.int32, (1, keys), 1)
        allowed = (key_index >= start) & (key_index <= query_index)
        for pair in range(group // LANES):
            cols = slice(pair * LANES, (pair + 1) * LANES)
            query = q_ref[rows, cols]
            key, value = k_ref[:keys, cols], v_ref[:keys, cols]
            results = []
            for chosen in (even, jnp.logical_not(even)):
                one = query * chosen.astype(jnp.bfloat16)
                scores = jnp.where(allowed, contract(one, key, 1, 1), -1e30)
                weights = jnp.exp(scores - jnp.max(scores, axis=-1, keepdims=True))
                total = jnp.sum(weights, axis=-1, keepdims=True)
                results.append(
                    jnp.dot(weights.astype(jnp.bfloat16), value, preferred_element_type=jnp.float32) / total
                )
            out_ref[rows, cols] = jnp.where(even, results[0], results[1]).astype(jnp.bfloat16).astype(jnp.float32)


def ready_kernel(
    docs, where_ref, lengths_ref, pad_ref, freq_ref, here_ref, there_ref, gain_ref, wq_ref, wk_ref, wv_ref,
    q_ref, k_ref, v_ref, log_ref, attn_in_ref, cos_ref, sin_ref,
):
    row_len = here_ref.shape[0]
    flag = where_ref[1]
    prepare(
        docs,
        lengths_ref,
        freq_ref,
        lambda rows: jnp.where(flag != 0, here_ref[rows, :].astype(jnp.float32), there_ref[rows, :]),
        gain_ref,
        attn_in_ref,
        cos_ref,
        sin_ref,
    )
    low_half, even = head_masks()
    group = wq_ref.shape[1]
    scale = 1.0 / math.sqrt(HEAD_DIM)
    for number in range(row_len // BLOCK):
        rows = pl.ds(number * BLOCK, BLOCK)
        block = attn_in_ref[rows, :]
        query = jnp.dot(block, wq_ref[...], preferred_element_type=jnp.float32)
        key = jnp.dot(block, wk_ref[...], preferred_element_type=jnp.float32)
        v_ref[rows, :] = jnp.dot(block, wv_ref[...], preferred_element_type=jnp.float32).astype(jnp.bfloat16)
        cosine, sine = cos_ref[rows, :], sin_ref[rows, :]
        for pair in range(group // LANES):
            cols = slice(pair * LANES, (pair + 1) * LANES)
            q_ref[rows, cols] = (turned(query[:, cols], cosine, sine, low_half) * scale).astype(jnp.bfloat16)
            k_ref[rows, cols] = turned(key[:, cols], cosine, sine, low_half).astype(jnp.bfloat16)
    ends = doc_ends(lengths_ref, docs)
    real = row_len - pad_ref[0]
    for number in range(row_len // BLOCK):
        rows = pl.ds(number * BLOCK, BLOCK)
        keys = (number + 1) * BLOCK
        query_index = number * BLOCK + lax.broadcasted_iota(jnp.int32, (1, BLOCK), 1)
        start = first_key(query_index, ends, real)
        key_index = lax.broadcasted_iota(jnp.int32, (keys, 1), 0)
        allowed = (key_index >= start) & (key_index <= query_index)
        for pair in range(group // LANES):
            cols = slice(pair * LANES, (pair + 1) * LANES)
            query, key = q_ref[rows, cols], k_ref[:keys, cols]
            for side, chosen in enumerate((even, jnp.logical_not(even))):
                one = query * chosen.astype(jnp.bfloat16)
                scores = jnp.where(allowed, contract(key, one, 1, 1), -1e30)
                highest = jnp.max(scores, axis=0, keepdims=True)
                total = jnp.sum(jnp.exp(scores - highest), axis=0, keepdims=True)
                head = pair * 2 + side
                log_ref[0, head : head + 1, rows] = highest + jnp.log(total)


def backward_kernel(
    docs, lengths_ref, pad_ref, cos_ref, sin_ref, q_ref, k_ref, v_ref, log_ref, grad_ref,
    gq_ref, gk_ref, gv_ref, key_sum, value_sum,
):
    row_len = q_ref.shape[0]
    low_half, even = head_masks()
    scale = 1.0 / math.sqrt(HEAD_DIM)
    ends = doc_ends(lengths_ref, docs)
    real = row_len - pad_ref[0]
    blocks = row_len // BLOCK
    for number in range(blocks - 1, -1, -1):
        rows = pl.ds(number * BLOCK, BLOCK)
        keys = (number + 1) * BLOCK
        query_index = number * BLOCK + lax.broadcasted_iota(jnp.int32, (1, BLOCK), 1)
        start = first_key(query_index, ends, real)
        key_index = lax.broadcasted_iota(jnp.int32, (keys, 1), 0)
        allowed = (key_index >= start) & (key_index <= query_index)
        query, grad = q_ref[rows, :], grad_ref[rows, :]
        key, value = k_ref[:keys, :], v_ref[:keys, :]
        parts = []
        for side, chosen in enumerate((even, jnp.logical_not(even))):
            mask = chosen.astype(jnp.bfloat16)
            one_query, one_grad = query * mask, grad * mask
            scores = jnp.where(allowed, contract(key, one_query, 1, 1), -1e30)
            weights = jnp.exp(scores - log_ref[0, side : side + 1, rows])
            soft = contract(value, one_grad, 1, 1)
            cross = jnp.sum(soft * weights, axis=0, keepdims=True)
            grad_scores = (weights * (soft - cross)).astype(jnp.bfloat16)
            low_weights = weights.astype(jnp.bfloat16)
            parts.append((
                contract(grad_scores, key, 0, 0),
                jnp.dot(grad_scores, one_query, preferred_element_type=jnp.float32),
                jnp.dot(low_weights, one_grad, preferred_element_type=jnp.float32),
            ))
        grad_query = jnp.where(even, parts[0][0], parts[1][0]) * scale
        gq_ref[rows, :] = turned(grad_query, cos_ref[rows, :], -sin_ref[rows, :], low_half).astype(jnp.bfloat16)
        if number == blocks - 1:
            key_sum[...] = parts[0][1] + parts[1][1]
            value_sum[...] = parts[0][2] + parts[1][2]
        else:
            key_sum[:keys, :] += parts[0][1] + parts[1][1]
            value_sum[:keys, :] += parts[0][2] + parts[1][2]
    for number in range(blocks):
        rows = pl.ds(number * BLOCK, BLOCK)
        gk_ref[rows, :] = turned(
            key_sum[rows, :], cos_ref[rows, :], -sin_ref[rows, :], low_half
        ).astype(jnp.bfloat16)
        gv_ref[rows, :] = value_sum[rows, :].astype(jnp.bfloat16)


def smem():
    return pl.BlockSpec(memory_space=pltpu.SMEM)


def whole(shape):
    return pl.BlockSpec(shape, lambda step: (0,) * len(shape))


def frequencies():
    half_dim = HEAD_DIM // 2
    return (10000.0 ** (-2.0 * np.arange(half_dim) / HEAD_DIM)).astype(np.float32)[:, None]


def attention_forward(number, sources, lengths, pad_count, gain, w_query, w_key, w_value):
    row_len, width = sources[0].shape
    first = number == 0
    group = w_query.shape[1] // 2
    weight = pl.BlockSpec((width, group), lambda step: (0, number))
    table = jax.ShapeDtypeStruct((row_len, LANES), jnp.float32)
    outs = [jax.ShapeDtypeStruct((row_len, group), jnp.float32)]
    if first:
        outs += [jax.ShapeDtypeStruct((row_len, width), jnp.bfloat16), table, table]
    return pl.pallas_call(
        partial(forward_kernel, lengths.shape[1], first),
        grid=(1,),
        in_specs=[
            smem(), smem(), whole((HEAD_DIM // 2, 1)), whole((1, width)),
            *(whole(source.shape) for source in sources), weight, weight, weight,
        ],
        out_specs=[whole(out.shape) for out in outs],
        out_shape=outs,
        scratch_shapes=[pltpu.VMEM((row_len, group), jnp.bfloat16)] * 3,
        compiler_params=pltpu.CompilerParams(vmem_limit_bytes=VMEM_LIMIT),
        cost_estimate=pl.CostEstimate(
            flops=6 * row_len * width * group + 16 * row_len * row_len * group,
            bytes_accessed=4 * row_len * width + 6 * width * group,
            transcendentals=row_len * row_len * group // HEAD_DIM,
        ),
        name="attention_forward",
    )(lengths, pad_count, jnp.asarray(frequencies()), gain[None], *sources, w_query, w_key, w_value)


def attention_ready(where, block_in, there, lengths, pad_count, gain, weights):
    row_len, width = block_in.shape
    wide = weights.shape[1] // 3
    group = 2 * LANES
    heads = group // HEAD_DIM
    steps = wide // group
    weight = [pl.BlockSpec((width, group), lambda step, part=part: (0, part * steps + step)) for part in range(3)]
    part = pl.BlockSpec((row_len, group), lambda step: (0, step))
    table = jax.ShapeDtypeStruct((row_len, LANES), jnp.float32)
    rows = jax.ShapeDtypeStruct((row_len, wide), jnp.bfloat16)
    return pl.pallas_call(
        partial(ready_kernel, lengths.shape[1]),
        grid=(wide // group,),
        in_specs=[
            smem(), smem(), smem(), whole((HEAD_DIM // 2, 1)), whole((row_len, width)), whole((row_len, width)), whole((1, width)), *weight,
        ],
        out_specs=[
            part, part, part,
            pl.BlockSpec((1, heads, row_len), lambda step: (step, 0, 0)),
            whole((row_len, width)), whole((row_len, LANES)), whole((row_len, LANES)),
        ],
        out_shape=[
            rows, rows, rows,
            jax.ShapeDtypeStruct((wide // group, heads, row_len), jnp.float32),
            jax.ShapeDtypeStruct((row_len, width), jnp.bfloat16), table, table,
        ],
        compiler_params=pltpu.CompilerParams(vmem_limit_bytes=VMEM_LIMIT),
        cost_estimate=pl.CostEstimate(
            flops=6 * row_len * width * wide + 8 * row_len * row_len * wide,
            bytes_accessed=6 * row_len * width + 6 * width * wide + 6 * row_len * wide,
            transcendentals=row_len * row_len * wide // HEAD_DIM,
        ),
        name="attention_ready",
    )(where, lengths, pad_count, jnp.asarray(frequencies()), block_in, there, gain[None], weights, weights, weights)


def attention_backward(ready, lengths, pad_count, grad_heads):
    query, key, value, logs, _, cosine, sine = ready
    row_len, wide = query.shape
    pairs = wide // LANES
    logs = logs.reshape(pairs, LANES // HEAD_DIM, row_len)
    part = pl.BlockSpec((row_len, LANES), lambda step: (0, step))
    rows = jax.ShapeDtypeStruct((row_len, wide), jnp.bfloat16)
    return pl.pallas_call(
        partial(backward_kernel, lengths.shape[1]),
        grid=(pairs,),
        in_specs=[
            smem(), smem(), whole((row_len, LANES)), whole((row_len, LANES)), part, part, part,
            pl.BlockSpec((1, LANES // HEAD_DIM, row_len), lambda step: (step, 0, 0)), part,
        ],
        out_specs=[part, part, part],
        out_shape=[rows, rows, rows],
        scratch_shapes=[pltpu.VMEM((row_len, LANES), jnp.float32), pltpu.VMEM((row_len, LANES), jnp.float32)],
        compiler_params=pltpu.CompilerParams(vmem_limit_bytes=VMEM_LIMIT),
        cost_estimate=pl.CostEstimate(
            flops=40 * row_len * row_len * wide,
            bytes_accessed=14 * row_len * wide,
            transcendentals=row_len * row_len * wide // HEAD_DIM,
        ),
        name="attention_backward",
    )(lengths, pad_count, cosine, sine, query, key, value, logs, grad_heads)


FF_STEPS = 4
PARTS = 2
TILE = 64


def chosen_rows(flag, here_ref, there_ref):
    return jnp.where(flag != 0, here_ref[...].astype(jnp.float32), there_ref[...])


def norm_stats(values):
    average = jnp.mean(values, axis=-1, keepdims=True)
    centered = values - average
    inverse = lax.rsqrt(jnp.mean(centered * centered, axis=-1, keepdims=True) + 1e-05)
    return (centered * inverse, inverse)


def norm_pull(grad, gain, hat, inverse):
    scaled = grad * gain
    mean_scaled = jnp.mean(scaled, axis=-1, keepdims=True)
    mean_cross = jnp.mean(scaled * hat, axis=-1, keepdims=True)
    return inverse * (scaled - mean_scaled - hat * mean_cross)


def add_gain(ref, step, row, value):
    @pl.when(step == 0)
    def _():
        ref[row : row + 1, :] = value

    @pl.when(step != 0)
    def _():
        ref[row : row + 1, :] += value


def hidden_kernel(where_ref, low_ref, high_ref, w_out_ref, arrived_ref, here_ref, there_ref, gain_ref, hidden_ref, total_ref):
    group = low_ref.shape[1]
    total = jnp.dot(low_ref[...], w_out_ref[:group, :], preferred_element_type=jnp.float32) + arrived_ref[...]
    total += jnp.dot(high_ref[...], w_out_ref[group:, :], preferred_element_type=jnp.float32)
    total_ref[...] = total
    hat, _ = norm_stats(total)
    hidden_ref[...] = chosen_rows(where_ref[1], here_ref, there_ref) + hat * gain_ref[...]


def mlp_forward_kernel(hidden_ref, gain_ref, up_ref, down_ref, *refs):
    mlp_in_ref, act_ref, slope_ref, part_ref = refs[-4:]
    step = pl.program_id(0)

    @pl.when(step == 0)
    def _():
        hat, _ = norm_stats(hidden_ref[...])
        mlp_in_ref[...] = (hat * gain_ref[...]).astype(jnp.bfloat16)

    factor = math.sqrt(2.0 / math.pi)
    size = up_ref.shape[1] // PARTS
    part = None
    for number in range(PARTS):
        cols = slice(number * size, (number + 1) * size)
        pre = jnp.dot(mlp_in_ref[...], up_ref[:, cols], preferred_element_type=jnp.float32)
        squared = pre * pre
        bent = jnp.tanh(factor * pre * (1.0 + 0.044715 * squared))
        gate = 0.5 * (1.0 + bent)
        act = (pre * gate).astype(jnp.bfloat16)
        act_ref[:, cols] = act
        slope_ref[:, cols] = gate + 0.5 * pre * (1.0 - bent * bent) * (factor + (3.0 * 0.044715 * factor) * squared)
        piece = jnp.dot(act, down_ref[cols, :], preferred_element_type=jnp.float32)
        part = piece if part is None else part + piece

    @pl.when(step == 0)
    def _():
        part_ref[...] = part

    @pl.when(step != 0)
    def _():
        part_ref[...] += part


def mlp_backward_kernel(
    where_ref, hidden_ref, total_ref, here_ref, there_ref, gain_ref, down_ref, up_ref, slope_ref, *refs
):
    block_ref, low_ref, gain_sum_ref, grad_up_ref, part_ref = refs[-5:]
    step = pl.program_id(0)

    @pl.when(step == 0)
    def _():
        hat, inverse = norm_stats(total_ref[...])
        cot = chosen_rows(where_ref[1], here_ref, there_ref)
        block_ref[...] = hidden_ref[...] + hat * gain_ref[...]
        low_ref[...] = norm_pull(cot, gain_ref[...], hat, inverse).astype(jnp.bfloat16)
        gain_sum_ref[...] = jnp.broadcast_to(jnp.sum(cot * hat, axis=0, keepdims=True), gain_sum_ref.shape)

    size = up_ref.shape[1] // PARTS
    part = None
    for number in range(PARTS):
        cols = slice(number * size, (number + 1) * size)
        grad_act = contract(low_ref[...], down_ref[cols, :], 1, 1)
        grad_up = (grad_act * slope_ref[:, cols]).astype(jnp.bfloat16)
        grad_up_ref[:, cols] = grad_up
        piece = contract(grad_up, up_ref[:, cols], 1, 1)
        part = piece if part is None else part + piece

    @pl.when(step == 0)
    def _():
        part_ref[...] = part

    @pl.when(step != 0)
    def _():
        part_ref[...] += part


def residual_kernel(
    where_ref, part_ref, arrived_ref, hidden_ref, attn_ref, here_ref, there_ref, gain_mlp_ref, gain_attn_ref, *refs
):
    res_ref, attn_grad_ref, gains_ref = refs[-3:]
    step = pl.program_id(0)
    grad = part_ref[...] + arrived_ref[...]
    hat, inverse = norm_stats(hidden_ref[...])
    cot = chosen_rows(where_ref[1], here_ref, there_ref)
    res = cot + norm_pull(grad, gain_mlp_ref[...], hat, inverse)
    res_ref[...] = res
    add_gain(gains_ref, step, 0, jnp.sum(grad * hat, axis=0, keepdims=True))
    hat, inverse = norm_stats(attn_ref[...])
    attn_grad_ref[...] = norm_pull(res, gain_attn_ref[...], hat, inverse)
    add_gain(gains_ref, step, 1, jnp.sum(res * hat, axis=0, keepdims=True))


def other_kernel(where_ref, grad_ref, weight_ref, out_ref):
    piece = contract(grad_ref[...], weight_ref[...], 1, 1)

    @pl.when(pl.program_id(0) == 0)
    def _():
        out_ref[...] = piece

    @pl.when(pl.program_id(0) != 0)
    def _():
        out_ref[...] += piece


def input_kernel(
    where_ref, grad_ref, weight_ref, arrived_ref, here_ref, there_ref, res_ref, gain_ref, out_ref, gain_sum_ref, sum_ref
):
    step = pl.program_id(0)
    piece = contract(grad_ref[...], weight_ref[...], 1, 1)

    @pl.when(step == 0)
    def _():
        sum_ref[...] = piece + arrived_ref[...]

    @pl.when(step != 0)
    def _():
        sum_ref[...] += piece

    @pl.when(step == pl.num_programs(0) - 1)
    def _():
        grad = sum_ref[...]
        hat, inverse = norm_stats(chosen_rows(where_ref[1], here_ref, there_ref))
        out_ref[...] = res_ref[...] + norm_pull(grad, gain_ref[...], hat, inverse)
        gain_sum_ref[...] = jnp.broadcast_to(jnp.sum(grad * hat, axis=0, keepdims=True), gain_sum_ref.shape)


def pack_kernel(where_ref, x_ref, cot_ref, out_ref):
    step = pl.program_id(0)

    @pl.when(step < 2)
    def _():
        out_ref[...] = x_ref[...].astype(jnp.float32)

    @pl.when(step == 2)
    def _():
        out_ref[...] = cot_ref[...].astype(jnp.float32)


def call(kernel, name, steps, where, arrays, specs, outs, aliases, flops):
    moved = sum(array.size * array.dtype.itemsize for array in arrays)
    return pl.pallas_call(
        kernel,
        grid_spec=pltpu.PrefetchScalarGridSpec(
            num_scalar_prefetch=0 if where is None else 1,
            grid=(steps,),
            in_specs=specs,
            out_specs=[spec for _, spec in outs],
        ),
        out_shape=[shape for shape, _ in outs],
        input_output_aliases=aliases,
        compiler_params=pltpu.CompilerParams(vmem_limit_bytes=VMEM_LIMIT),
        cost_estimate=pl.CostEstimate(flops=flops, bytes_accessed=moved, transcendentals=0),
        name=name,
    )(*(() if where is None else (where,)), *arrays)


def rows_spec(rows, width, place):
    return pl.BlockSpec((rows, width), lambda step, *where: (place(step, *where), 0))


def fixed_spec(shape):
    return pl.BlockSpec(shape, lambda *args: (0,) * len(shape))


def hidden_chunk(where, number, attended, w_out, arrived, block_in, there, gain):
    row_len, group = attended[0].shape
    width = w_out.shape[1]
    rows = row_len // 4
    mine = rows_spec(rows, width, lambda step, where: where[0] * 2 + number)
    mine_attended = rows_spec(rows, group, lambda step, where: where[0] * 2 + number)
    shape = jax.ShapeDtypeStruct((rows, width), jnp.float32)
    return call(
        hidden_kernel, "hidden", 1, where,
        (*attended, w_out, arrived, block_in, there, gain[None]),
        [
            mine_attended, mine_attended, fixed_spec(w_out.shape),
            rows_spec(rows, width, lambda step, where: number), mine, mine, fixed_spec((1, width)),
        ],
        [(shape, fixed_spec((rows, width))), (shape, fixed_spec((rows, width)))],
        {}, 4 * rows * group * width,
    )


def mlp_forward(number, hidden, gain, w_up, w_down, buffers):
    rows, width = hidden.shape
    inner = w_up.shape[1]
    size = inner // FF_STEPS
    spare = [pl.BlockSpec(memory_space=pl.ANY)] * len(buffers)
    return call(
        mlp_forward_kernel, "mlp_forward", FF_STEPS, None,
        (hidden, gain[None], w_up, w_down, *buffers),
        [
            fixed_spec((rows, width)), fixed_spec((1, width)),
            pl.BlockSpec((width, size), lambda step: (0, step)),
            pl.BlockSpec((size, width), lambda step: (step, 0)),
            *spare,
        ],
        [
            (jax.ShapeDtypeStruct((4 * rows, width), jnp.bfloat16), pl.BlockSpec((rows, width), lambda step: (number, 0))),
            (jax.ShapeDtypeStruct((4 * rows, inner), jnp.bfloat16), pl.BlockSpec((rows, size), lambda step: (number, step))),
            (jax.ShapeDtypeStruct((rows, inner), jnp.float32), pl.BlockSpec((rows, size), lambda step: (0, step))),
            (jax.ShapeDtypeStruct((rows, width), jnp.float32), fixed_spec((rows, width))),
        ],
        {4 + index: index for index in range(len(buffers))}, 4 * rows * width * inner,
    )


def mlp_backward(where, number, hidden, total, cotangent, there, gain, w_down, w_up, slope, buffers):
    rows, width = hidden.shape
    inner = w_up.shape[1]
    size = inner // FF_STEPS
    part = number % 2
    spare = [pl.BlockSpec(memory_space=pl.ANY)] * len(buffers)
    return call(
        mlp_backward_kernel, "mlp_backward", FF_STEPS, where,
        (hidden, total, cotangent, there, gain[None], w_down, w_up, slope, *buffers),
        [
            fixed_spec((rows, width)), fixed_spec((rows, width)),
            rows_spec(rows, width, lambda step, where: where[0] * 2 + part),
            rows_spec(rows, width, lambda step, where: 4 + part),
            fixed_spec((1, width)),
            pl.BlockSpec((size, width), lambda step, where: (step, 0)),
            pl.BlockSpec((width, size), lambda step, where: (0, step)),
            pl.BlockSpec((rows, size), lambda step, where: (0, step)),
            *spare,
        ],
        [
            (jax.ShapeDtypeStruct((rows, width), jnp.float32), fixed_spec((rows, width))),
            (jax.ShapeDtypeStruct((4 * rows, width), jnp.bfloat16), pl.BlockSpec((rows, width), lambda step, where: (number, 0))),
            (jax.ShapeDtypeStruct((8, width), jnp.float32), fixed_spec((8, width))),
            (jax.ShapeDtypeStruct((4 * rows, inner), jnp.bfloat16), pl.BlockSpec((rows, size), lambda step, where: (number, step))),
            (jax.ShapeDtypeStruct((rows, width), jnp.float32), fixed_spec((rows, width))),
        ],
        {9 + index: 1 + 2 * index for index in range(len(buffers))}, 4 * rows * width * inner,
    )


def residual_chunk(where, number, part, arrived, hidden, attn_total, cotangent, there, gain_mlp, gain_attn, buffers):
    rows, width = part.shape
    steps = rows // TILE
    local = rows_spec(TILE, width, lambda step, where: step)
    spare = [pl.BlockSpec(memory_space=pl.ANY)] * len(buffers)
    whole_half = jax.ShapeDtypeStruct((2 * rows, width), jnp.float32)
    place = rows_spec(TILE, width, lambda step, where: number * steps + step)
    return call(
        residual_kernel, "residual", steps, where,
        (part, arrived, hidden, attn_total, cotangent, there, gain_mlp[None], gain_attn[None], *buffers),
        [
            local, local, local, local,
            rows_spec(TILE, width, lambda step, where: (where[0] * 2 + number) * steps + step),
            rows_spec(TILE, width, lambda step, where: (4 + number) * steps + step),
            fixed_spec((1, width)), fixed_spec((1, width)),
            *spare,
        ],
        [(whole_half, place), (whole_half, place), (jax.ShapeDtypeStruct((8, width), jnp.float32), fixed_spec((8, width)))],
        {9 + index: index for index in range(len(buffers))}, 20 * rows * width,
    )


def packed(where, block_in, cotangent):
    row_len, width = block_in.shape
    half = row_len // 2
    return call(
        pack_kernel, "packed", 3, where, (block_in, cotangent),
        [
            rows_spec(half, width, lambda step, where: jnp.minimum(step, 1)),
            rows_spec(half, width, lambda step, where: 1 - where[0]),
        ],
        [(jax.ShapeDtypeStruct((3 * half, width), jnp.float32), rows_spec(half, width, lambda step, where: step))],
        {}, 0,
    )[0]


def input_specs(grads, weights, other):
    row_len, wide = grads.shape[0], grads.shape[1] // 3
    width = weights.shape[0]
    half = row_len // 2
    return [
        pl.BlockSpec((half, wide), lambda step, where: (1 - where[0] if other else where[0], step)),
        pl.BlockSpec((width, wide), lambda step, where: (0, step)),
    ], (half, width)


def input_other(where, grads, weights):
    specs, shape = input_specs(grads, weights, True)
    return call(
        other_kernel, "input_other", 3, where, (grads, weights), specs,
        [(jax.ShapeDtypeStruct(shape, jnp.float32), fixed_spec(shape))], {}, 2 * shape[0] * weights.size,
    )[0]


def input_own(where, grads, weights, arrived, block_in, there, res, gain):
    specs, shape = input_specs(grads, weights, False)
    mine = rows_spec(*shape, lambda step, where: where[0])
    moved = sum(array.size * array.dtype.itemsize for array in (grads, weights, arrived, block_in, there, res))
    return pl.pallas_call(
        input_kernel,
        grid_spec=pltpu.PrefetchScalarGridSpec(
            num_scalar_prefetch=1,
            grid=(3,),
            in_specs=specs + [fixed_spec(shape), mine, mine, fixed_spec(shape), fixed_spec((1, shape[1]))],
            out_specs=[fixed_spec(shape), fixed_spec((8, shape[1]))],
            scratch_shapes=[pltpu.VMEM(shape, jnp.float32)],
        ),
        out_shape=[jax.ShapeDtypeStruct(shape, jnp.float32), jax.ShapeDtypeStruct((8, shape[1]), jnp.float32)],
        compiler_params=pltpu.CompilerParams(vmem_limit_bytes=VMEM_LIMIT),
        cost_estimate=pl.CostEstimate(flops=2 * shape[0] * weights.size, bytes_accessed=moved, transcendentals=0),
        name="input_own",
    )(where, grads, weights, arrived, block_in, there, res, gain[None])


def after(values, *others):
    return lax.optimization_barrier((values, others))[0]


def ordered(mine, other, bit, axis):
    low = jnp.where(bit == 0, mine, other)
    high = jnp.where(bit == 0, other, mine)
    return jnp.concatenate([low, high], axis=axis)


def body(
    dp_size,
    block_in,
    cotangent,
    lengths,
    pad_count,
    norm_in_attn,
    w_query,
    w_key,
    w_value,
    w_out,
    norm_out_attn,
    norm_in_mlp,
    w_up,
    w_down,
    norm_out_mlp,
):
    f32, bf16 = jnp.float32, jnp.bfloat16
    place = lax.axis_index("dp")
    core = lax.rem(place, 2)
    chip = lax.div(place, 2)
    side = lax.axis_index("tensor")
    same = core == side
    keep = same.astype(f32)
    first = (core == 0).astype(f32)
    chips = dp_size // 2
    levels = chips.bit_length() - 1
    bits = [lax.rem(lax.div(chip, 1 << level), 2) for level in range(levels)]
    swap = flat_pairs(dp_size, lambda d, c, t: (d ^ 1, 1 - t) if c != t else None)
    cross = flat_pairs(dp_size, lambda d, c, t: (d ^ 1, t))
    over = flat_pairs(dp_size, lambda d, c, t: (d, 1 - t))
    flips = [flat_pairs(dp_size, lambda d, c, t: (d ^ (2 << level), t)) for level in range(levels)]
    row_len, width = block_in.shape
    half = row_len // 2
    chunk = half // 2
    wide = w_query.shape[1]
    hidden = w_up.shape[1]

    shares = min(2, levels)
    near = [flat_pairs(dp_size, lambda d, c, t: (d ^ (2 << level), t) if c != t else None) for level in range(shares)]

    where_own = jnp.stack([core, same.astype(jnp.int32)])
    where_peer = jnp.stack([core, 1 - same.astype(jnp.int32)])
    out_rows = wide // 2
    w_out_sent = send(half_of(w_out, bits[0], out_rows).astype(f32), swap)
    attended_low, *sources = attention_forward(0, (block_in,), lengths, pad_count, norm_in_attn, w_query, w_key, w_value)
    low_sent = send(attended_low, swap)
    sources = after(sources, w_out_sent)
    w_out_sent = ordered(w_out_sent, send(w_out_sent, near[0]), bits[0], 0)
    [attended_high] = attention_forward(1, sources, lengths, pad_count, norm_in_attn, w_query, w_key, w_value)
    high_sent = send(attended_high, swap)
    block_late, cot_late, facts = after((block_in, cotangent, jnp.pad(lengths, ((0, 0), (0, 1)))), attended_high)
    facts = facts.astype(f32) + jnp.pad(pad_count.astype(f32)[:, None], ((0, 0), (lengths.shape[1], 0)))
    there = send(packed(where_own, block_late, cot_late), cross)
    facts_there = send(facts, cross)
    low_sent = after(low_sent, attended_high)
    attended = [(attended_low * keep + low_sent).astype(bf16), (attended_high * keep + high_sent).astype(bf16)]
    weights_here = jnp.concatenate([w_query, w_key, w_value], axis=1)
    part_rows = width >> shares
    which = sum(bits[level] << level for level in range(shares))
    weights_sent = send(half_of(after(weights_here, attended[1]), which, part_rows).astype(f32), swap)
    w_out_mine = (w_out.astype(f32) * keep + w_out_sent).astype(bf16)
    facts_row = jnp.where(same, facts, facts_there).astype(jnp.int32)
    docs = lengths.shape[1]
    lengths_row, pad_row = facts_row[:, :docs], facts_row[:, docs]
    part_other = sum(
        jnp.dot(half_of(values, 1 - core, half), w_out_mine[start : start + out_rows], preferred_element_type=f32)
        for values, start in zip(attended, (0, out_rows))
    )
    arrived = send(part_other, cross)
    hidden_own, attn_total, hidden_peer = [], [], []
    for number in range(2):
        one, total = hidden_chunk(where_own, number, attended, w_out_mine, arrived, block_in, there, norm_out_attn)
        hidden_own.append(one)
        attn_total.append(total)
        hidden_peer.append(send(one, over))

    buffers, slopes, parts, sums_own = (), [], [], []
    for number in range(4):
        piece = hidden_own[number] if number < 2 else hidden_peer[number - 2]
        if number == 3:
            piece = after(piece, parts[2], weights_sent)
        *buffers, slope, part = mlp_forward(number, piece, norm_in_mlp, w_up, w_down, buffers)
        slopes.append(slope)
        parts.append(part)
        if number >= 2:
            sums_own.append(send(part, over))
            if number - 2 < shares:
                weights_sent = after(weights_sent, part)
                weights_sent = ordered(weights_sent, send(weights_sent, near[number - 2]), bits[number - 2], 0)
    mlp_in_all, activated_all = buffers
    weights_late = after(weights_sent, parts[3])
    weights_mine = (weights_here.astype(f32) * keep + weights_late).astype(bf16)
    ready = attention_ready(where_own, block_in, there, lengths_row, pad_row, norm_in_attn, weights_mine)
    totals, blocks, back_parts, gain_out_mlp = [], [], [], []
    buffers = ()
    for number in range(4):
        if number < 2:
            total = parts[number] + (sums_own[0] if number == 0 else after(sums_own[1], back_parts[0]))
            totals.append(total)
            totals_peer = send(total, over)
            totals.append(totals_peer)
        total = totals[2 * number] if number < 2 else totals[2 * (number - 2) + 1]
        if number >= 2:
            total = after(total, back_parts[number - 1], ready)
        hidden_piece = hidden_own[number] if number < 2 else hidden_peer[number - 2]
        block, low_all, gain_sum, up_all, part = mlp_backward(
            where_own if number < 2 else where_peer,
            number,
            hidden_piece,
            total,
            cotangent,
            there,
            norm_out_mlp,
            w_down,
            w_up,
            slopes[number],
            buffers,
        )
        buffers = (low_all, up_all)
        blocks.append(block)
        back_parts.append(part)
        gain_out_mlp.append(gain_sum[0])
    grad_low_all, grad_up_all = buffers
    sums_own = [send(part, over) for part in back_parts[2:]]

    small = width // chips // 2

    def halved(held, arrived, level):
        group = (-1, 2, width // chips, held.shape[-1])
        parts = [held.reshape(group)] + ([] if arrived is None else [arrived.reshape(group)])
        results = []
        for which in (bits[level], 1 - bits[level]):
            results.append(sum(lax.dynamic_index_in_dim(part, which, 1, keepdims=False) for part in parts))
        return results

    def to_chip(held, arrived, level, gate=None):
        for number in range(level, levels):
            held, leaving = halved(held, arrived, number)
            arrived = send(leaving, flips[number])
        return (held + arrived).reshape(width // chips, -1)

    def to_core(held):
        arrived = send(half_of(held, 1 - core, small), cross)
        return ordered(half_of(held, core, small), arrived, core, 1)

    def weight_part(left, right, columns):
        return jnp.einsum("td,tf->df", left, half_columns(right, columns, hidden // 2), preferred_element_type=f32)

    down_sent = send(weight_part(grad_low_all, activated_all, 1 - core), cross)
    weight_up = jnp.einsum("td,tf->df", mlp_in_all, grad_up_all, preferred_element_type=f32)
    grad_up = lax.psum_scatter(weight_up, "dp", scatter_dimension=0, tiled=True)
    down_kept = weight_part(grad_low_all, activated_all, core)
    down_held, down_leaving = halved(down_kept, down_sent, 0)
    down_arrived = send(down_leaving, flips[0])
    sums_own = after(sums_own, down_leaving, weight_up)

    def to_output(values_own, values_peer):
        stay = jnp.where(same, values_own, values_peer)
        leave = jnp.where(same, values_peer, values_own)
        arrived = send(leave, cross)
        low = stay * first + arrived * (1.0 - first)
        high = arrived * first + stay * (1.0 - first)
        return jnp.concatenate([low, high], axis=0)

    buffers, gain_sums = (), []
    for number in range(2):
        *buffers, gain_sum = residual_chunk(
            where_own,
            number,
            back_parts[number],
            sums_own[number],
            hidden_own[number],
            attn_total[number],
            cotangent,
            there,
            norm_in_mlp,
            norm_out_attn,
            buffers,
        )
        gain_sums.append(gain_sum)
    grad_res, grad_attn = buffers
    gain_in_mlp = gain_sums[0][0] + gain_sums[1][0]
    gain_out_attn = gain_sums[0][1] + gain_sums[1][1]
    gain_out_mlp = gain_out_mlp[0] + gain_out_mlp[1]
    grad_attn_other = send(grad_attn, cross)
    grad_attn_low = jnp.concatenate(
        [
            grad_attn * first + grad_attn_other * (1.0 - first),
            grad_attn_other * first + grad_attn * (1.0 - first),
        ],
        axis=0,
    ).astype(bf16)
    grad_heads = jnp.einsum("td,ed->te", grad_attn_low, w_out_mine, preferred_element_type=f32).astype(bf16)
    weight_out = jnp.concatenate(
        [jnp.einsum("td,te->de", grad_attn_low, values, preferred_element_type=f32) for values in attended], axis=1
    )
    weight_out_sent = send(weight_out, swap)
    down_held, down_leaving = halved(down_held, down_arrived, 1)
    down_arrived = send(down_leaving, flips[1])
    grad_heads = after(grad_heads, down_leaving, weight_out)
    grads = attention_backward(ready, lengths_row, pad_row, grad_heads)
    down_held, down_leaving = halved(down_held, down_arrived, 2)
    down_arrived = send(down_leaving, flips[2])
    grads = jnp.concatenate(after(grads, down_leaving), axis=1)
    other_sent = send(input_other(where_own, grads, weights_mine), cross)
    pair = jnp.einsum("td,te->de", ready[4], grads[:, : 2 * wide], preferred_element_type=f32)
    pair_held, pair_leaving = halved(pair, None, 0)
    pair_arrived = send(pair_leaving, flips[0])
    value = jnp.einsum("td,te->de", ready[4], grads[:, 2 * wide :], preferred_element_type=f32)
    value_held, value_leaving = halved(value, None, 0)
    value_arrived = send(value_leaving, flips[0])
    other_sent = after(other_sent, value_leaving)
    grad_in_own, gain_in_attn = input_own(
        where_own, grads, weights_mine, other_sent, block_in, there, grad_res, norm_in_attn
    )
    grad_in = to_output(grad_in_own, send(grad_in_own, over))
    grad_down = to_core(to_chip(down_held, down_arrived, 3)).T
    gains = jnp.stack([gain_in_attn[0], gain_out_attn, gain_in_mlp, gain_out_mlp], axis=1)
    weight_out_sent, gains, pair_arrived = after((weight_out_sent, gains, pair_arrived), grad_up, grad_down)
    others = lax.psum_scatter(
        jnp.concatenate([weight_out * keep + weight_out_sent, jnp.pad(gains, ((0, 0), (0, LANES - 4)))], axis=1),
        "dp",
        scatter_dimension=0,
        tiled=True,
    )
    held = jnp.concatenate([to_chip(pair_held, pair_arrived, 1), to_chip(value_held, value_arrived, 1)], axis=1)
    for_core = half_of(held, core, small)
    for_other = half_of(held, 1 - core, small)
    straight = send(for_core, flat_pairs(dp_size, lambda d, c, t: (d, 1 - t) if c != t else None))
    diagonal = send(for_other, swap)
    beside = send(for_other, flat_pairs(dp_size, lambda d, c, t: (d ^ 1, t) if c == t else None))
    heads = jnp.where(same, for_core + straight, beside + diagonal)
    gains = others[:, wide:]
    gains = gains + send(gains, over)
    block_out = to_output(jnp.concatenate(blocks[:2], axis=0), jnp.concatenate(blocks[2:], axis=0)).astype(bf16)
    return (
        block_out,
        grad_in,
        gains[:, 0],
        heads[:, :wide],
        heads[:, wide : 2 * wide],
        heads[:, 2 * wide : 3 * wide],
        others[:, :wide].T,
        gains[:, 1],
        gains[:, 2],
        grad_up,
        grad_down,
        gains[:, 3],
    )


def solution(mesh):
    placed = (
        P("dp", None),
        P("dp", None),
        P("dp", None),
        P("dp"),
        P(),
        P(None, "tensor"),
        P(None, "tensor"),
        P(None, "tensor"),
        P("tensor", None),
        P(),
        P(),
        P(None, "tensor"),
        P("tensor", None),
        P(),
    )
    return jax.shard_map(
        partial(body, mesh.shape["dp"]),
        mesh=mesh,
        in_specs=placed,
        out_specs=(
            P("dp", None),
            P("dp", None),
            P("dp"),
            P("dp", "tensor"),
            P("dp", "tensor"),
            P("dp", "tensor"),
            P("tensor", "dp"),
            P("dp"),
            P("dp"),
            P("dp", "tensor"),
            P("tensor", "dp"),
            P("dp"),
        ),
        check_vma=False,
    )
```

```python
from functools import partial
import math

import jax
import jax.numpy as jnp
from jax import lax
from jax.experimental import pallas as pl
from jax.experimental.pallas import tpu as pltpu
from jax.sharding import PartitionSpec as P
import numpy as np

HEAD_DIM = 64


def half_columns(values, which, size):
    return lax.dynamic_slice_in_dim(values, which * size, size, axis=1)


def flat_pairs(count, target):
    pairs = []
    for row in range(count):
        for side in range(2):
            goal = target(row, row % 2, side)
            if goal is not None:
                pairs.append((row * 2 + side, goal[0] * 2 + goal[1]))
    return pairs


def send(values, pairs):
    return lax.ppermute(values, ("dp", "tensor"), pairs)


def half_of(values, which, size):
    return lax.dynamic_slice_in_dim(values, which * size, size, axis=0)


BLOCK = 256
LANES = 128
VMEM_LIMIT = 56 * 1024 * 1024
SMALL = pl.CostEstimate(flops=1, bytes_accessed=1, transcendentals=0)


def doc_ends(lengths_ref, docs):
    ends = [lengths_ref[0, 0]]
    for number in range(1, docs):
        ends.append(ends[-1] + lengths_ref[0, number])
    return ends


def doc_start(index, ends):
    start = jnp.zeros_like(index)
    for end in ends:
        start = jnp.where(index >= end, end, start)
    return start


def first_key(index, ends, real):
    return jnp.where(index >= real, index, doc_start(index, ends))


def rope_tables(ends, row_len, freq_ref, cos_ref, sin_ref):
    index = lax.broadcasted_iota(jnp.int32, (1, row_len), 1)
    position = (index - doc_start(index, ends)).astype(jnp.float32)
    angles = freq_ref[...] * position
    cosine, sine = jnp.cos(angles), jnp.sin(angles)
    cos_ref[...] = jnp.concatenate([cosine] * 4, axis=0).T
    sin_ref[...] = jnp.concatenate([-sine, sine] * 2, axis=0).T


def turned(values, cosine, sine, low_half):
    ahead = pltpu.roll(values, LANES - HEAD_DIM // 2, 1)
    behind = pltpu.roll(values, HEAD_DIM // 2, 1)
    return values * cosine + jnp.where(low_half, ahead, behind) * sine


def normed(values):
    average = jnp.mean(values, axis=-1, keepdims=True)
    centered = values - average
    return centered * lax.rsqrt(jnp.mean(centered * centered, axis=-1, keepdims=True) + 1e-05)


def contract(left, right, left_dim, right_dim):
    return lax.dot_general(
        left, right, (((left_dim,), (right_dim,)), ((), ())), preferred_element_type=jnp.float32
    )


def prepare(docs, lengths_ref, freq_ref, rows_of, gain_ref, attn_in_ref, cos_ref, sin_ref):
    row_len = attn_in_ref.shape[0]

    @pl.when(pl.program_id(0) == 0)
    def _():
        rope_tables(doc_ends(lengths_ref, docs), row_len, freq_ref, cos_ref, sin_ref)
        for number in range(row_len // BLOCK):
            rows = pl.ds(number * BLOCK, BLOCK)
            attn_in_ref[rows, :] = (
                normed(rows_of(rows)) * gain_ref[...]
            ).astype(jnp.bfloat16)


def head_masks():
    lane = lax.broadcasted_iota(jnp.int32, (1, LANES), 1)
    return (lax.rem(lane, HEAD_DIM) < HEAD_DIM // 2, lane < HEAD_DIM)


def forward_kernel(docs, first, lengths_ref, pad_ref, freq_ref, gain_ref, *refs):
    if first:
        x_ref, wq_ref, wk_ref, wv_ref, out_ref, attn_in_ref, cos_ref, sin_ref, q_ref, k_ref, v_ref = refs
        row_len = x_ref.shape[0]
        prepare(
            docs, lengths_ref, freq_ref, lambda rows: x_ref[rows, :].astype(jnp.float32), gain_ref, attn_in_ref, cos_ref, sin_ref
        )
    else:
        attn_in_ref, cos_ref, sin_ref, wq_ref, wk_ref, wv_ref, out_ref, q_ref, k_ref, v_ref = refs
        row_len = attn_in_ref.shape[0]
    low_half, even = head_masks()
    group = wq_ref.shape[1]
    scale = 1.0 / math.sqrt(HEAD_DIM)
    for number in range(row_len // BLOCK):
        rows = pl.ds(number * BLOCK, BLOCK)
        block = attn_in_ref[rows, :]
        query = jnp.dot(block, wq_ref[...], preferred_element_type=jnp.float32)
        key = jnp.dot(block, wk_ref[...], preferred_element_type=jnp.float32)
        v_ref[rows, :] = jnp.dot(block, wv_ref[...], preferred_element_type=jnp.float32).astype(jnp.bfloat16)
        cosine, sine = cos_ref[rows, :], sin_ref[rows, :]
        for pair in range(group // LANES):
            cols = slice(pair * LANES, (pair + 1) * LANES)
            q_ref[rows, cols] = (turned(query[:, cols], cosine, sine, low_half) * scale).astype(jnp.bfloat16)
            k_ref[rows, cols] = turned(key[:, cols], cosine, sine, low_half).astype(jnp.bfloat16)
    ends = doc_ends(lengths_ref, docs)
    real = row_len - pad_ref[0]
    for number in range(row_len // BLOCK):
        rows = pl.ds(number * BLOCK, BLOCK)
        keys = (number + 1) * BLOCK
        query_index = number * BLOCK + lax.broadcasted_iota(jnp.int32, (BLOCK, 1), 0)
        start = first_key(query_index, ends, real)
        key_index = lax.broadcasted_iota(jnp.int32, (1, keys), 1)
        allowed = (key_index >= start) & (key_index <= query_index)
        for pair in range(group // LANES):
            cols = slice(pair * LANES, (pair + 1) * LANES)
            query = q_ref[rows, cols]
            key, value = k_ref[:keys, cols], v_ref[:keys, cols]
            results = []
            for chosen in (even, jnp.logical_not(even)):
                one = query * chosen.astype(jnp.bfloat16)
                scores = jnp.where(allowed, contract(one, key, 1, 1), -1e30)
                weights = jnp.exp(scores - jnp.max(scores, axis=-1, keepdims=True))
                total = jnp.sum(weights, axis=-1, keepdims=True)
                results.append(
                    jnp.dot(weights.astype(jnp.bfloat16), value, preferred_element_type=jnp.float32) / total
                )
            out_ref[rows, cols] = jnp.where(even, results[0], results[1]).astype(jnp.bfloat16).astype(jnp.float32)


def ready_kernel(
    docs, where_ref, lengths_ref, pad_ref, freq_ref, here_ref, there_ref, gain_ref, wq_ref, wk_ref, wv_ref,
    q_ref, k_ref, v_ref, log_ref, attn_in_ref, cos_ref, sin_ref,
):
    row_len = here_ref.shape[0]
    flag = where_ref[1]
    prepare(
        docs,
        lengths_ref,
        freq_ref,
        lambda rows: jnp.where(flag != 0, here_ref[rows, :].astype(jnp.float32), there_ref[rows, :]),
        gain_ref,
        attn_in_ref,
        cos_ref,
        sin_ref,
    )
    low_half, even = head_masks()
    group = wq_ref.shape[1]
    scale = 1.0 / math.sqrt(HEAD_DIM)
    for number in range(row_len // BLOCK):
        rows = pl.ds(number * BLOCK, BLOCK)
        block = attn_in_ref[rows, :]
        query = jnp.dot(block, wq_ref[...], preferred_element_type=jnp.float32)
        key = jnp.dot(block, wk_ref[...], preferred_element_type=jnp.float32)
        v_ref[rows, :] = jnp.dot(block, wv_ref[...], preferred_element_type=jnp.float32).astype(jnp.bfloat16)
        cosine, sine = cos_ref[rows, :], sin_ref[rows, :]
        for pair in range(group // LANES):
            cols = slice(pair * LANES, (pair + 1) * LANES)
            q_ref[rows, cols] = (turned(query[:, cols], cosine, sine, low_half) * scale).astype(jnp.bfloat16)
            k_ref[rows, cols] = turned(key[:, cols], cosine, sine, low_half).astype(jnp.bfloat16)
    ends = doc_ends(lengths_ref, docs)
    real = row_len - pad_ref[0]
    for number in range(row_len // BLOCK):
        rows = pl.ds(number * BLOCK, BLOCK)
        keys = (number + 1) * BLOCK
        query_index = number * BLOCK + lax.broadcasted_iota(jnp.int32, (1, BLOCK), 1)
        start = first_key(query_index, ends, real)
        key_index = lax.broadcasted_iota(jnp.int32, (keys, 1), 0)
        allowed = (key_index >= start) & (key_index <= query_index)
        for pair in range(group // LANES):
            cols = slice(pair * LANES, (pair + 1) * LANES)
            query, key = q_ref[rows, cols], k_ref[:keys, cols]
            for side, chosen in enumerate((even, jnp.logical_not(even))):
                one = query * chosen.astype(jnp.bfloat16)
                scores = jnp.where(allowed, contract(key, one, 1, 1), -1e30)
                highest = jnp.max(scores, axis=0, keepdims=True)
                total = jnp.sum(jnp.exp(scores - highest), axis=0, keepdims=True)
                head = pair * 2 + side
                log_ref[0, head : head + 1, rows] = highest + jnp.log(total)


def backward_kernel(
    docs, lengths_ref, pad_ref, cos_ref, sin_ref, q_ref, k_ref, v_ref, log_ref, grad_ref,
    gq_ref, gk_ref, gv_ref, key_sum, value_sum,
):
    row_len = q_ref.shape[0]
    low_half, even = head_masks()
    scale = 1.0 / math.sqrt(HEAD_DIM)
    ends = doc_ends(lengths_ref, docs)
    real = row_len - pad_ref[0]
    blocks = row_len // BLOCK
    for number in range(blocks - 1, -1, -1):
        rows = pl.ds(number * BLOCK, BLOCK)
        keys = (number + 1) * BLOCK
        query_index = number * BLOCK + lax.broadcasted_iota(jnp.int32, (1, BLOCK), 1)
        start = first_key(query_index, ends, real)
        key_index = lax.broadcasted_iota(jnp.int32, (keys, 1), 0)
        allowed = (key_index >= start) & (key_index <= query_index)
        query, grad = q_ref[rows, :], grad_ref[rows, :]
        key, value = k_ref[:keys, :], v_ref[:keys, :]
        parts = []
        for side, chosen in enumerate((even, jnp.logical_not(even))):
            mask = chosen.astype(jnp.bfloat16)
            one_query, one_grad = query * mask, grad * mask
            scores = jnp.where(allowed, contract(key, one_query, 1, 1), -1e30)
            weights = jnp.exp(scores - log_ref[0, side : side + 1, rows])
            soft = contract(value, one_grad, 1, 1)
            cross = jnp.sum(soft * weights, axis=0, keepdims=True)
            grad_scores = (weights * (soft - cross)).astype(jnp.bfloat16)
            low_weights = weights.astype(jnp.bfloat16)
            parts.append((
                contract(grad_scores, key, 0, 0),
                jnp.dot(grad_scores, one_query, preferred_element_type=jnp.float32),
                jnp.dot(low_weights, one_grad, preferred_element_type=jnp.float32),
            ))
        grad_query = jnp.where(even, parts[0][0], parts[1][0]) * scale
        gq_ref[rows, :] = turned(grad_query, cos_ref[rows, :], -sin_ref[rows, :], low_half).astype(jnp.bfloat16)
        if number == blocks - 1:
            key_sum[...] = parts[0][1] + parts[1][1]
            value_sum[...] = parts[0][2] + parts[1][2]
        else:
            key_sum[:keys, :] += parts[0][1] + parts[1][1]
            value_sum[:keys, :] += parts[0][2] + parts[1][2]
    for number in range(blocks):
        rows = pl.ds(number * BLOCK, BLOCK)
        gk_ref[rows, :] = turned(
            key_sum[rows, :], cos_ref[rows, :], -sin_ref[rows, :], low_half
        ).astype(jnp.bfloat16)
        gv_ref[rows, :] = value_sum[rows, :].astype(jnp.bfloat16)


def smem():
    return pl.BlockSpec(memory_space=pltpu.SMEM)


def whole(shape):
    return pl.BlockSpec(shape, lambda step: (0,) * len(shape))


def frequencies():
    half_dim = HEAD_DIM // 2
    return (10000.0 ** (-2.0 * np.arange(half_dim) / HEAD_DIM)).astype(np.float32)[:, None]


def attention_forward(number, sources, lengths, pad_count, gain, w_query, w_key, w_value):
    row_len, width = sources[0].shape
    first = number == 0
    group = w_query.shape[1] // 2
    weight = pl.BlockSpec((width, group), lambda step: (0, number))
    table = jax.ShapeDtypeStruct((row_len, LANES), jnp.float32)
    outs = [jax.ShapeDtypeStruct((row_len, group), jnp.float32)]
    if first:
        outs += [jax.ShapeDtypeStruct((row_len, width), jnp.bfloat16), table, table]
    return pl.pallas_call(
        partial(forward_kernel, lengths.shape[1], first),
        grid=(1,),
        in_specs=[
            smem(), smem(), whole((HEAD_DIM // 2, 1)), whole((1, width)),
            *(whole(source.shape) for source in sources), weight, weight, weight,
        ],
        out_specs=[whole(out.shape) for out in outs],
        out_shape=outs,
        scratch_shapes=[pltpu.VMEM((row_len, group), jnp.bfloat16)] * 3,
        compiler_params=pltpu.CompilerParams(vmem_limit_bytes=VMEM_LIMIT),
        cost_estimate=SMALL,
        name="attention_forward",
    )(lengths, pad_count, jnp.asarray(frequencies()), gain[None], *sources, w_query, w_key, w_value)


def attention_ready(where, block_in, there, lengths, pad_count, gain, weights):
    row_len, width = block_in.shape
    wide = weights.shape[1] // 3
    group = 2 * LANES
    heads = group // HEAD_DIM
    steps = wide // group
    weight = [pl.BlockSpec((width, group), lambda step, part=part: (0, part * steps + step)) for part in range(3)]
    part = pl.BlockSpec((row_len, group), lambda step: (0, step))
    table = jax.ShapeDtypeStruct((row_len, LANES), jnp.float32)
    rows = jax.ShapeDtypeStruct((row_len, wide), jnp.bfloat16)
    return pl.pallas_call(
        partial(ready_kernel, lengths.shape[1]),
        grid=(wide // group,),
        in_specs=[
            smem(), smem(), smem(), whole((HEAD_DIM // 2, 1)), whole((row_len, width)), whole((row_len, width)), whole((1, width)), *weight,
        ],
        out_specs=[
            part, part, part,
            pl.BlockSpec((1, heads, row_len), lambda step: (step, 0, 0)),
            whole((row_len, width)), whole((row_len, LANES)), whole((row_len, LANES)),
        ],
        out_shape=[
            rows, rows, rows,
            jax.ShapeDtypeStruct((wide // group, heads, row_len), jnp.float32),
            jax.ShapeDtypeStruct((row_len, width), jnp.bfloat16), table, table,
        ],
        compiler_params=pltpu.CompilerParams(vmem_limit_bytes=VMEM_LIMIT),
        cost_estimate=SMALL,
        name="attention_ready",
    )(where, lengths, pad_count, jnp.asarray(frequencies()), block_in, there, gain[None], weights, weights, weights)


def attention_backward(ready, lengths, pad_count, grad_heads):
    query, key, value, logs, _, cosine, sine = ready
    row_len, wide = query.shape
    pairs = wide // LANES
    logs = logs.reshape(pairs, LANES // HEAD_DIM, row_len)
    part = pl.BlockSpec((row_len, LANES), lambda step: (0, step))
    rows = jax.ShapeDtypeStruct((row_len, wide), jnp.bfloat16)
    return pl.pallas_call(
        partial(backward_kernel, lengths.shape[1]),
        grid=(pairs,),
        in_specs=[
            smem(), smem(), whole((row_len, LANES)), whole((row_len, LANES)), part, part, part,
            pl.BlockSpec((1, LANES // HEAD_DIM, row_len), lambda step: (step, 0, 0)), part,
        ],
        out_specs=[part, part, part],
        out_shape=[rows, rows, rows],
        scratch_shapes=[pltpu.VMEM((row_len, LANES), jnp.float32), pltpu.VMEM((row_len, LANES), jnp.float32)],
        compiler_params=pltpu.CompilerParams(vmem_limit_bytes=VMEM_LIMIT),
        cost_estimate=SMALL,
        name="attention_backward",
    )(lengths, pad_count, cosine, sine, query, key, value, logs, grad_heads)


FF_STEPS = 4
PARTS = 2
TILE = 256


def chosen_rows(flag, here_ref, there_ref):
    return jnp.where(flag != 0, here_ref[...].astype(jnp.float32), there_ref[...])


def norm_stats(values):
    average = jnp.mean(values, axis=-1, keepdims=True)
    centered = values - average
    inverse = lax.rsqrt(jnp.mean(centered * centered, axis=-1, keepdims=True) + 1e-05)
    return (centered * inverse, inverse)


def norm_pull(grad, gain, hat, inverse):
    scaled = grad * gain
    mean_scaled = jnp.mean(scaled, axis=-1, keepdims=True)
    mean_cross = jnp.mean(scaled * hat, axis=-1, keepdims=True)
    return inverse * (scaled - mean_scaled - hat * mean_cross)


def add_gain(ref, step, row, value):
    @pl.when(step == 0)
    def _():
        ref[row : row + 1, :] = value

    @pl.when(step != 0)
    def _():
        ref[row : row + 1, :] += value


def hidden_kernel(where_ref, low_ref, high_ref, w_out_ref, arrived_ref, here_ref, there_ref, gain_ref, hidden_ref, total_ref):
    group = low_ref.shape[1]
    total = jnp.dot(low_ref[...], w_out_ref[:group, :], preferred_element_type=jnp.float32) + arrived_ref[...]
    total += jnp.dot(high_ref[...], w_out_ref[group:, :], preferred_element_type=jnp.float32)
    total_ref[...] = total
    hat, _ = norm_stats(total)
    hidden_ref[...] = chosen_rows(where_ref[1], here_ref, there_ref) + hat * gain_ref[...]


def mlp_forward_kernel(hidden_ref, gain_ref, up_ref, down_ref, *refs):
    mlp_in_ref, act_ref, slope_ref, part_ref = refs[-4:]
    step = pl.program_id(0)

    @pl.when(step == 0)
    def _():
        hat, _ = norm_stats(hidden_ref[...])
        mlp_in_ref[...] = (hat * gain_ref[...]).astype(jnp.bfloat16)

    factor = math.sqrt(2.0 / math.pi)
    size = up_ref.shape[1] // PARTS
    part = None
    for number in range(PARTS):
        cols = slice(number * size, (number + 1) * size)
        pre = jnp.dot(mlp_in_ref[...], up_ref[:, cols], preferred_element_type=jnp.float32)
        squared = pre * pre
        bent = jnp.tanh(factor * pre * (1.0 + 0.044715 * squared))
        gate = 0.5 * (1.0 + bent)
        act = (pre * gate).astype(jnp.bfloat16)
        act_ref[:, cols] = act
        slope_ref[:, cols] = gate + 0.5 * pre * (1.0 - bent * bent) * (factor + (3.0 * 0.044715 * factor) * squared)
        piece = jnp.dot(act, down_ref[cols, :], preferred_element_type=jnp.float32)
        part = piece if part is None else part + piece

    @pl.when(step == 0)
    def _():
        part_ref[...] = part

    @pl.when(step != 0)
    def _():
        part_ref[...] += part


def mlp_backward_kernel(
    where_ref, hidden_ref, total_ref, here_ref, there_ref, gain_ref, down_ref, up_ref, slope_ref, *refs
):
    block_ref, low_ref, gain_sum_ref, grad_up_ref, part_ref = refs[-5:]
    step = pl.program_id(0)

    @pl.when(step == 0)
    def _():
        hat, inverse = norm_stats(total_ref[...])
        cot = chosen_rows(where_ref[1], here_ref, there_ref)
        block_ref[...] = hidden_ref[...] + hat * gain_ref[...]
        low_ref[...] = norm_pull(cot, gain_ref[...], hat, inverse).astype(jnp.bfloat16)
        gain_sum_ref[...] = jnp.broadcast_to(jnp.sum(cot * hat, axis=0, keepdims=True), gain_sum_ref.shape)

    size = up_ref.shape[1] // PARTS
    part = None
    for number in range(PARTS):
        cols = slice(number * size, (number + 1) * size)
        grad_act = contract(low_ref[...], down_ref[cols, :], 1, 1)
        grad_up = (grad_act * slope_ref[:, cols]).astype(jnp.bfloat16)
        grad_up_ref[:, cols] = grad_up
        piece = contract(grad_up, up_ref[:, cols], 1, 1)
        part = piece if part is None else part + piece

    @pl.when(step == 0)
    def _():
        part_ref[...] = part

    @pl.when(step != 0)
    def _():
        part_ref[...] += part


def residual_kernel(
    where_ref, part_ref, arrived_ref, hidden_ref, attn_ref, here_ref, there_ref, gain_mlp_ref, gain_attn_ref, *refs
):
    res_ref, attn_grad_ref, gains_ref = refs[-3:]
    step = pl.program_id(0)
    grad = part_ref[...] + arrived_ref[...]
    hat, inverse = norm_stats(hidden_ref[...])
    cot = chosen_rows(where_ref[1], here_ref, there_ref)
    res = cot + norm_pull(grad, gain_mlp_ref[...], hat, inverse)
    res_ref[...] = res
    add_gain(gains_ref, step, 0, jnp.sum(grad * hat, axis=0, keepdims=True))
    hat, inverse = norm_stats(attn_ref[...])
    attn_grad_ref[...] = norm_pull(res, gain_attn_ref[...], hat, inverse)
    add_gain(gains_ref, step, 1, jnp.sum(res * hat, axis=0, keepdims=True))


def other_kernel(where_ref, grad_ref, weight_ref, out_ref):
    piece = contract(grad_ref[...], weight_ref[...], 1, 1)

    @pl.when(pl.program_id(0) == 0)
    def _():
        out_ref[...] = piece

    @pl.when(pl.program_id(0) != 0)
    def _():
        out_ref[...] += piece


def input_kernel(
    where_ref, grad_ref, weight_ref, arrived_ref, here_ref, there_ref, res_ref, gain_ref, out_ref, gain_sum_ref, sum_ref
):
    step = pl.program_id(0)
    piece = contract(grad_ref[...], weight_ref[...], 1, 1)

    @pl.when(step == 0)
    def _():
        sum_ref[...] = piece + arrived_ref[...]

    @pl.when(step != 0)
    def _():
        sum_ref[...] += piece

    @pl.when(step == pl.num_programs(0) - 1)
    def _():
        grad = sum_ref[...]
        hat, inverse = norm_stats(chosen_rows(where_ref[1], here_ref, there_ref))
        out_ref[...] = res_ref[...] + norm_pull(grad, gain_ref[...], hat, inverse)
        gain_sum_ref[...] = jnp.broadcast_to(jnp.sum(grad * hat, axis=0, keepdims=True), gain_sum_ref.shape)


def pack_kernel(where_ref, x_ref, cot_ref, out_ref):
    step = pl.program_id(0)

    @pl.when(step < 2)
    def _():
        out_ref[...] = x_ref[...].astype(jnp.float32)

    @pl.when(step == 2)
    def _():
        out_ref[...] = cot_ref[...].astype(jnp.float32)


def call(kernel, name, steps, where, arrays, specs, outs, aliases, flops):
    moved = sum(array.size * array.dtype.itemsize for array in arrays)
    return pl.pallas_call(
        kernel,
        grid_spec=pltpu.PrefetchScalarGridSpec(
            num_scalar_prefetch=0 if where is None else 1,
            grid=(steps,),
            in_specs=specs,
            out_specs=[spec for _, spec in outs],
        ),
        out_shape=[shape for shape, _ in outs],
        input_output_aliases=aliases,
        compiler_params=pltpu.CompilerParams(vmem_limit_bytes=VMEM_LIMIT),
        cost_estimate=SMALL,
        name=name,
    )(*(() if where is None else (where,)), *arrays)


def rows_spec(rows, width, place):
    return pl.BlockSpec((rows, width), lambda step, *where: (place(step, *where), 0))


def fixed_spec(shape):
    return pl.BlockSpec(shape, lambda *args: (0,) * len(shape))


def hidden_chunk(where, number, attended, w_out, arrived, block_in, there, gain):
    row_len, group = attended[0].shape
    width = w_out.shape[1]
    rows = row_len // 4
    mine = rows_spec(rows, width, lambda step, where: where[0] * 2 + number)
    mine_attended = rows_spec(rows, group, lambda step, where: where[0] * 2 + number)
    shape = jax.ShapeDtypeStruct((rows, width), jnp.float32)
    return call(
        hidden_kernel, "hidden", 1, where,
        (*attended, w_out, arrived, block_in, there, gain[None]),
        [
            mine_attended, mine_attended, fixed_spec(w_out.shape),
            rows_spec(rows, width, lambda step, where: number), mine, mine, fixed_spec((1, width)),
        ],
        [(shape, fixed_spec((rows, width))), (shape, fixed_spec((rows, width)))],
        {}, 4 * rows * group * width,
    )


def mlp_forward(number, hidden, gain, w_up, w_down, buffers):
    rows, width = hidden.shape
    inner = w_up.shape[1]
    size = inner // FF_STEPS
    spare = [pl.BlockSpec(memory_space=pl.ANY)] * len(buffers)
    return call(
        mlp_forward_kernel, "mlp_forward", FF_STEPS, None,
        (hidden, gain[None], w_up, w_down, *buffers),
        [
            fixed_spec((rows, width)), fixed_spec((1, width)),
            pl.BlockSpec((width, size), lambda step: (0, step)),
            pl.BlockSpec((size, width), lambda step: (step, 0)),
            *spare,
        ],
        [
            (jax.ShapeDtypeStruct((4 * rows, width), jnp.bfloat16), pl.BlockSpec((rows, width), lambda step: (number, 0))),
            (jax.ShapeDtypeStruct((4 * rows, inner), jnp.bfloat16), pl.BlockSpec((rows, size), lambda step: (number, step))),
            (jax.ShapeDtypeStruct((rows, inner), jnp.float32), pl.BlockSpec((rows, size), lambda step: (0, step))),
            (jax.ShapeDtypeStruct((rows, width), jnp.float32), fixed_spec((rows, width))),
        ],
        {4 + index: index for index in range(len(buffers))}, 4 * rows * width * inner,
    )


def mlp_backward(where, number, hidden, total, cotangent, there, gain, w_down, w_up, slope, buffers):
    rows, width = hidden.shape
    inner = w_up.shape[1]
    size = inner // FF_STEPS
    part = number % 2
    spare = [pl.BlockSpec(memory_space=pl.ANY)] * len(buffers)
    return call(
        mlp_backward_kernel, "mlp_backward", FF_STEPS, where,
        (hidden, total, cotangent, there, gain[None], w_down, w_up, slope, *buffers),
        [
            fixed_spec((rows, width)), fixed_spec((rows, width)),
            rows_spec(rows, width, lambda step, where: where[0] * 2 + part),
            rows_spec(rows, width, lambda step, where: 4 + part),
            fixed_spec((1, width)),
            pl.BlockSpec((size, width), lambda step, where: (step, 0)),
            pl.BlockSpec((width, size), lambda step, where: (0, step)),
            pl.BlockSpec((rows, size), lambda step, where: (0, step)),
            *spare,
        ],
        [
            (jax.ShapeDtypeStruct((rows, width), jnp.float32), fixed_spec((rows, width))),
            (jax.ShapeDtypeStruct((4 * rows, width), jnp.bfloat16), pl.BlockSpec((rows, width), lambda step, where: (number, 0))),
            (jax.ShapeDtypeStruct((8, width), jnp.float32), fixed_spec((8, width))),
            (jax.ShapeDtypeStruct((4 * rows, inner), jnp.bfloat16), pl.BlockSpec((rows, size), lambda step, where: (number, step))),
            (jax.ShapeDtypeStruct((rows, width), jnp.float32), fixed_spec((rows, width))),
        ],
        {9 + index: 1 + 2 * index for index in range(len(buffers))}, 4 * rows * width * inner,
    )


def residual_chunk(where, number, part, arrived, hidden, attn_total, cotangent, there, gain_mlp, gain_attn, buffers):
    rows, width = part.shape
    steps = rows // TILE
    local = rows_spec(TILE, width, lambda step, where: step)
    spare = [pl.BlockSpec(memory_space=pl.ANY)] * len(buffers)
    whole_half = jax.ShapeDtypeStruct((2 * rows, width), jnp.float32)
    place = rows_spec(TILE, width, lambda step, where: number * steps + step)
    return call(
        residual_kernel, "residual", steps, where,
        (part, arrived, hidden, attn_total, cotangent, there, gain_mlp[None], gain_attn[None], *buffers),
        [
            local, local, local, local,
            rows_spec(TILE, width, lambda step, where: (where[0] * 2 + number) * steps + step),
            rows_spec(TILE, width, lambda step, where: (4 + number) * steps + step),
            fixed_spec((1, width)), fixed_spec((1, width)),
            *spare,
        ],
        [(whole_half, place), (whole_half, place), (jax.ShapeDtypeStruct((8, width), jnp.float32), fixed_spec((8, width)))],
        {9 + index: index for index in range(len(buffers))}, 20 * rows * width,
    )


def packed(where, block_in, cotangent):
    row_len, width = block_in.shape
    half = row_len // 2
    return call(
        pack_kernel, "packed", 3, where, (block_in, cotangent),
        [
            rows_spec(half, width, lambda step, where: jnp.minimum(step, 1)),
            rows_spec(half, width, lambda step, where: 1 - where[0]),
        ],
        [(jax.ShapeDtypeStruct((3 * half, width), jnp.float32), rows_spec(half, width, lambda step, where: step))],
        {}, 0,
    )[0]


def outer_kernel(where_ref, left_ref, right_ref, out_ref, turned_ref):
    @pl.when(pl.program_id(0) == 0)
    def _():
        turned_ref[...] = left_ref[...].T

    out_ref[...] = jnp.dot(turned_ref[...], right_ref[...], preferred_element_type=jnp.float32)


def outer(where, left, right, pick, columns):
    tokens, width = left.shape
    size = min(512, columns)
    steps = columns // size
    return pl.pallas_call(
        outer_kernel,
        grid_spec=pltpu.PrefetchScalarGridSpec(
            num_scalar_prefetch=1,
            grid=(steps,),
            in_specs=[
                fixed_spec((tokens, width)),
                pl.BlockSpec((tokens, size), lambda step, where: (0, pick(where) * steps + step)),
            ],
            out_specs=pl.BlockSpec((width, size), lambda step, where: (0, step)),
            scratch_shapes=[pltpu.VMEM((width, tokens), left.dtype)],
        ),
        out_shape=jax.ShapeDtypeStruct((width, columns), jnp.float32),
        compiler_params=pltpu.CompilerParams(vmem_limit_bytes=VMEM_LIMIT),
        cost_estimate=SMALL,
        name="outer",
    )(where, left, right)


def halves_kernel(count, sources, where_ref, *refs):
    stays, leaves = refs[:count], refs[count : 2 * count]
    outs = refs[-count - 1 : -1]
    leaving_ref = refs[-1]
    start = 0
    for stay_ref, leave_ref, out_ref, source in zip(stays, leaves, outs, sources):
        columns = stay_ref.shape[-1]
        stay, leave = stay_ref[0], leave_ref[0]
        if source is not None:
            number, first = source
            stay += refs[2 * count + 2 * number][0, :, first : first + columns]
            leave += refs[2 * count + 2 * number + 1][0, :, first : first + columns]
        out_ref[0] = stay
        leaving_ref[0, :, start : start + columns] = leave
        start += columns


def halves(where, step, held, arrived, sources):
    blocks, rows = held[0].shape[0] // 2, held[0].shape[1]
    widths = [part.shape[2] for part in held]

    def spec(width, stays):
        def place(index, where):
            low, bit = where[2 + 2 * step], where[3 + 2 * step]
            bit = bit if stays else 1 - bit
            high = lax.shift_right_logical(index, low)
            return (lax.shift_left(2 * high + bit, low) + index - lax.shift_left(high, low), 0, 0)

        return pl.BlockSpec((1, rows, width), place)

    arrays = list(held) * 2
    specs = [spec(width, stays) for stays in (True, False) for width in widths]
    for array in arrived:
        arrays += [array] * 2
        specs += [spec(array.shape[2], stays) for stays in (True, False)]
    outs = [*widths, sum(widths)]
    *staying, leaving = pl.pallas_call(
        partial(halves_kernel, len(held), sources),
        grid_spec=pltpu.PrefetchScalarGridSpec(
            num_scalar_prefetch=1,
            grid=(blocks,),
            in_specs=specs,
            out_specs=[pl.BlockSpec((1, rows, width), lambda index, where: (index, 0, 0)) for width in outs],
        ),
        out_shape=[jax.ShapeDtypeStruct((blocks, rows, width), jnp.float32) for width in outs],
        compiler_params=pltpu.CompilerParams(vmem_limit_bytes=VMEM_LIMIT),
        cost_estimate=SMALL,
        name="halves",
    )(where, *arrays)
    return staying, leaving


def input_specs(grads, weights, other):
    row_len, wide = grads.shape[0], grads.shape[1] // 3
    width = weights.shape[0]
    half = row_len // 2
    return [
        pl.BlockSpec((half, wide), lambda step, where: (1 - where[0] if other else where[0], step)),
        pl.BlockSpec((width, wide), lambda step, where: (0, step)),
    ], (half, width)


def input_other(where, grads, weights):
    specs, shape = input_specs(grads, weights, True)
    return call(
        other_kernel, "input_other", 3, where, (grads, weights), specs,
        [(jax.ShapeDtypeStruct(shape, jnp.float32), fixed_spec(shape))], {}, 2 * shape[0] * weights.size,
    )[0]


def input_own(where, grads, weights, arrived, block_in, there, res, gain):
    specs, shape = input_specs(grads, weights, False)
    mine = rows_spec(*shape, lambda step, where: where[0])
    moved = sum(array.size * array.dtype.itemsize for array in (grads, weights, arrived, block_in, there, res))
    return pl.pallas_call(
        input_kernel,
        grid_spec=pltpu.PrefetchScalarGridSpec(
            num_scalar_prefetch=1,
            grid=(3,),
            in_specs=specs + [fixed_spec(shape), mine, mine, fixed_spec(shape), fixed_spec((1, shape[1]))],
            out_specs=[fixed_spec(shape), fixed_spec((8, shape[1]))],
            scratch_shapes=[pltpu.VMEM(shape, jnp.float32)],
        ),
        out_shape=[jax.ShapeDtypeStruct(shape, jnp.float32), jax.ShapeDtypeStruct((8, shape[1]), jnp.float32)],
        compiler_params=pltpu.CompilerParams(vmem_limit_bytes=VMEM_LIMIT),
        cost_estimate=SMALL,
        name="input_own",
    )(where, grads, weights, arrived, block_in, there, res, gain[None])


def after(values, *others):
    return lax.optimization_barrier((values, others))[0]


def ordered(mine, other, bit, axis):
    low = jnp.where(bit == 0, mine, other)
    high = jnp.where(bit == 0, other, mine)
    return jnp.concatenate([low, high], axis=axis)


def body(
    dp_size,
    block_in,
    cotangent,
    lengths,
    pad_count,
    norm_in_attn,
    w_query,
    w_key,
    w_value,
    w_out,
    norm_out_attn,
    norm_in_mlp,
    w_up,
    w_down,
    norm_out_mlp,
):
    f32, bf16 = jnp.float32, jnp.bfloat16
    place = lax.axis_index("dp")
    core = lax.rem(place, 2)
    chip = lax.div(place, 2)
    side = lax.axis_index("tensor")
    same = core == side
    keep = same.astype(f32)
    first = (core == 0).astype(f32)
    chips = dp_size // 2
    levels = chips.bit_length() - 1
    bits = [lax.rem(lax.div(chip, 1 << level), 2) for level in range(levels)]
    swap = flat_pairs(dp_size, lambda d, c, t: (d ^ 1, 1 - t) if c != t else None)
    cross = flat_pairs(dp_size, lambda d, c, t: (d ^ 1, t))
    over = flat_pairs(dp_size, lambda d, c, t: (d, 1 - t))
    flips = [flat_pairs(dp_size, lambda d, c, t: (d ^ (2 << level), t)) for level in range(levels)]
    row_len, width = block_in.shape
    half = row_len // 2
    chunk = half // 2
    wide = w_query.shape[1]
    hidden = w_up.shape[1]

    shares = min(2, levels)
    near = flat_pairs(dp_size, lambda d, c, t: (d ^ 2, t) if c != t else None)

    orders = (list(range(levels)), [*range(1, levels), 0])
    hop_facts = []
    for step in range(levels):
        places = [sum(1 for later in order[step + 1 :] if later < order[step]) for order in orders]
        hop_facts.append(jnp.where(core == 0, places[0], places[1]))
        hop_facts.append(jnp.where(core == 0, bits[orders[0][step]], bits[orders[1][step]]))
    hops = [flat_pairs(dp_size, lambda d, c, t: (d ^ (2 << orders[c][step]), t)) for step in range(levels)]
    where_own = jnp.stack([core, same.astype(jnp.int32), *hop_facts])
    where_peer = jnp.stack([core, 1 - same.astype(jnp.int32)])
    out_rows = wide // 2
    weights_here = (w_query, w_key, w_value)
    part_rows = width >> shares
    which = sum(bits[level] << level for level in range(shares))
    parts_here = jnp.concatenate([half_of(weight, which, part_rows) for weight in weights_here], axis=1)
    w_out_sent = send(half_of(w_out, bits[0], out_rows).astype(f32), swap)
    attended_low, *sources = attention_forward(0, (block_in,), lengths, pad_count, norm_in_attn, w_query, w_key, w_value)
    low_sent = send(attended_low, swap)
    sources = after(sources, w_out_sent)
    w_out_sent = ordered(w_out_sent, send(w_out_sent, near), bits[0], 0)
    [attended_high] = attention_forward(1, sources, lengths, pad_count, norm_in_attn, w_query, w_key, w_value)
    high_sent = send(attended_high, swap)
    block_late, cot_late, facts = after((block_in, cotangent, jnp.pad(lengths, ((0, 0), (0, 1)))), low_sent, attended_high)
    facts = facts.astype(f32) + jnp.pad(pad_count.astype(f32)[:, None], ((0, 0), (lengths.shape[1], 0)))
    there = send(packed(where_own, block_late, cot_late), cross)
    facts_there = send(facts, cross)
    low_sent = after(low_sent, attended_high)
    attended = [(attended_low * keep + low_sent).astype(bf16), (attended_high * keep + high_sent).astype(bf16)]
    w_out_mine = (w_out.astype(f32) * keep + w_out_sent).astype(bf16)
    parts_sent = send(after(parts_here, attended[0]).astype(f32), swap)
    facts_row = jnp.where(same, facts, facts_there).astype(jnp.int32)
    docs = lengths.shape[1]
    lengths_row, pad_row = facts_row[:, :docs], facts_row[:, docs]
    part_other = sum(
        jnp.dot(half_of(values, 1 - core, half), w_out_mine[start : start + out_rows], preferred_element_type=f32)
        for values, start in zip(attended, (0, out_rows))
    )
    arrived = send(part_other, cross)
    hidden_own, attn_total, hidden_peer = [], [], []
    for number in range(2):
        one, total = hidden_chunk(where_own, number, attended, w_out_mine, arrived, block_in, there, norm_out_attn)
        hidden_own.append(one)
        attn_total.append(total)
        hidden_peer.append(send(one, over))

    gathered = 1 << shares
    groups = [
        [base + 2 * near_chip + one for near_chip in range(gathered)]
        for base in range(0, dp_size, 2 * gathered)
        for one in range(2)
    ]
    weights_sent = lax.all_gather(after(parts_sent, hidden_own[0]), "dp", axis=0, tiled=True, axis_index_groups=groups)

    buffers, slopes, parts, sums_own = (), [], [], []
    for number in range(4):
        piece = hidden_own[number] if number < 2 else hidden_peer[number - 2]
        if number > 1:
            piece = after(piece, parts[number - 1])
        *buffers, slope, part = mlp_forward(number, piece, norm_in_mlp, w_up, w_down, buffers)
        slopes.append(slope)
        parts.append(part)
        if number >= 2:
            sums_own.append(send(part, over))
    mlp_in_all, activated_all = buffers
    totals, blocks, back_parts, gain_out_mlp = [None] * 4, [None] * 4, [None] * 4, [None] * 4
    buffers = ()

    def add_up(number, gate):
        totals[number] = parts[number] + after(sums_own[number], gate)
        totals[number + 2] = send(totals[number], over)

    add_up(0, parts[3])
    gate = totals[0]
    for number in range(4):
        block, low_all, gain_sum, up_all, part = mlp_backward(
            where_own if number < 2 else where_peer,
            number,
            hidden_own[number] if number < 2 else hidden_peer[number - 2],
            after(totals[number], gate),
            cotangent,
            there,
            norm_out_mlp,
            w_down,
            w_up,
            slopes[number],
            buffers,
        )
        buffers = (low_all, up_all)
        blocks[number], back_parts[number], gain_out_mlp[number] = block, part, gain_sum[0]
        gate = part
        if number == 0:
            add_up(1, part)
            gate = totals[1]
    grad_low_all, grad_up_all = buffers
    sums_own = [send(part, over) for part in back_parts[2:]]

    def residual(number, arrived, buffers):
        return residual_chunk(
            where_own,
            number,
            back_parts[number],
            arrived,
            hidden_own[number],
            attn_total[number],
            cotangent,
            there,
            norm_in_mlp,
            norm_out_attn,
            buffers,
        )

    chip_rows = width // chips
    small = chip_rows // 2

    class Sum:
        def __init__(self, held, arrived):
            self.held = [part.reshape(chips, chip_rows, -1) for part in held]
            self.arrived = [] if arrived is None else [arrived.reshape(chips, chip_rows, -1)]
            self.sources = [None if arrived is None else (0, 0)] * len(held)
            self.step = 0

        def hop(self, *gates):
            arrived = [after(array, *gates) for array in self.arrived]
            self.held, leaving = halves(where_own, self.step, self.held, arrived, tuple(self.sources))
            self.arrived = [send(leaving, hops[self.step])]
            starts = np.cumsum([0, *(part.shape[2] for part in self.held)])
            self.sources = [(0, int(start)) for start in starts[:-1]]
            self.step += 1
            return leaving

        def result(self, *gates):
            while self.step < levels:
                gates = (self.hop(*gates),)
            arrived = [after(array, *gates) for array in self.arrived]
            return [
                (part + arrived[number][:, :, start : start + part.shape[2]]).reshape(chip_rows, -1)
                for part, (number, start) in zip(self.held, self.sources)
            ]

    down_other = outer(where_own, grad_low_all, activated_all, lambda where: 1 - where[0], hidden // 2)
    down_kept = outer(where_own, grad_low_all, activated_all, lambda where: where[0], hidden // 2)
    early = Sum([down_kept], send(down_other, cross))
    mlp_in_all, grad_up_all = after((mlp_in_all, grad_up_all), early.hop(down_kept))
    weight_up = outer(where_own, mlp_in_all, grad_up_all, lambda where: 0, hidden)
    grad_up = lax.psum_scatter(weight_up, "dp", scatter_dimension=0, tiled=True)
    weights_late = after(weights_sent, weight_up)
    weights_mine = (jnp.concatenate(weights_here, axis=1).astype(f32) * keep + weights_late).astype(bf16)
    ready = attention_ready(where_own, block_in, there, lengths_row, pad_row, norm_in_attn, weights_mine)
    *buffers, gain_sum = residual(0, after(sums_own[0], ready[0]), ())
    gain_sums = [gain_sum]
    *buffers, gain_sum = residual(1, after(sums_own[1], gain_sum), buffers)
    gain_sums.append(gain_sum)
    grad_res, grad_attn = buffers
    gain_in_mlp = gain_sums[0][0] + gain_sums[1][0]
    gain_out_attn = gain_sums[0][1] + gain_sums[1][1]
    gain_out_mlp = gain_out_mlp[0] + gain_out_mlp[1]

    def to_output(values_own, values_peer):
        stay = jnp.where(same, values_own, values_peer)
        leave = jnp.where(same, values_peer, values_own)
        arrived = send(leave, cross)
        low = stay * first + arrived * (1.0 - first)
        high = arrived * first + stay * (1.0 - first)
        return jnp.concatenate([low, high], axis=0)

    grad_attn_other = send(grad_attn, cross)
    gate = early.hop(gain_sum)
    grad_attn_low = jnp.concatenate(
        [
            grad_attn * first + grad_attn_other * (1.0 - first),
            grad_attn_other * first + grad_attn * (1.0 - first),
        ],
        axis=0,
    ).astype(bf16)
    grad_heads = jnp.einsum("td,ed->te", grad_attn_low, w_out_mine, preferred_element_type=f32).astype(bf16)
    grads = attention_backward(ready, lengths_row, pad_row, after(grad_heads, gate))
    grads = jnp.concatenate(after(grads, early.hop(grads)), axis=1)
    late = Sum([jnp.einsum("td,te->de", ready[4], grads, preferred_element_type=f32)], None)
    gate = late.hop()
    other = input_other(where_own, after(grads, gate), weights_mine)
    other_sent = send(other, cross)
    attended_all = after(jnp.concatenate(attended, axis=1), other)
    weight_out = jnp.einsum("td,te->de", grad_attn_low, attended_all, preferred_element_type=f32)
    weight_out_sent = send(weight_out, swap)
    gate = weight_out
    grad_in_own, gain_in_attn = input_own(
        where_own, grads, weights_mine, after(other_sent, gate), block_in, there, grad_res, norm_in_attn
    )
    grad_in_sent = send(grad_in_own, over)
    gains = jnp.stack([gain_in_attn[0], gain_out_attn, gain_in_mlp, gain_out_mlp], axis=1)
    weight_out_sent, gains = after((weight_out_sent, gains), grad_up)
    others = jnp.concatenate(
        [weight_out * keep + weight_out_sent, jnp.pad(gains, ((0, 0), (0, LANES - gains.shape[1])))], axis=1
    )
    gate = late.hop(grad_in_own, others)
    others = lax.psum_scatter(others, "dp", scatter_dimension=0, tiled=True)
    gate = late.hop(gate)
    [grad_down] = early.result(gate)
    [held] = late.result(gate)

    def to_core(held):
        arrived = send(half_of(held, 1 - core, small), cross)
        return ordered(half_of(held, core, small), arrived, core, 1)

    def to_output(values_own, values_peer):
        stay = jnp.where(same, values_own, values_peer)
        leave = jnp.where(same, values_peer, values_own)
        arrived = send(leave, cross)
        low = stay * first + arrived * (1.0 - first)
        high = arrived * first + stay * (1.0 - first)
        return jnp.concatenate([low, high], axis=0)

    grad_down = to_core(grad_down).T
    grad_in = to_output(grad_in_own, after(grad_in_sent, gate))
    for_core = half_of(held, core, small)
    for_other = half_of(held, 1 - core, small)
    diagonal = send(for_other, swap)
    straight = send(
        jnp.where(same, for_other, for_core),
        flat_pairs(dp_size, lambda d, c, t: (d, 1 - t) if c != t else (d ^ 1, t)),
    )
    heads = straight + jnp.where(same, for_core, diagonal)
    gains = others[:, wide:].T
    gains = gains + send(gains, over)
    block_out = to_output(jnp.concatenate(blocks[:2], axis=0), jnp.concatenate(blocks[2:], axis=0)).astype(bf16)
    return (
        block_out,
        grad_in,
        gains[0],
        heads[:, :wide],
        heads[:, wide : 2 * wide],
        heads[:, 2 * wide : 3 * wide],
        others[:, :wide].T,
        gains[1],
        gains[2],
        grad_up,
        grad_down,
        gains[3],
    )


def solution(mesh):
    placed = (
        P("dp", None),
        P("dp", None),
        P("dp", None),
        P("dp"),
        P(),
        P(None, "tensor"),
        P(None, "tensor"),
        P(None, "tensor"),
        P("tensor", None),
        P(),
        P(),
        P(None, "tensor"),
        P("tensor", None),
        P(),
    )
    return jax.shard_map(
        partial(body, mesh.shape["dp"]),
        mesh=mesh,
        in_specs=placed,
        out_specs=(
            P("dp", None),
            P("dp", None),
            P("dp"),
            P("dp", "tensor"),
            P("dp", "tensor"),
            P("dp", "tensor"),
            P("tensor", "dp"),
            P("dp"),
            P("dp"),
            P("dp", "tensor"),
            P("tensor", "dp"),
            P("dp"),
        ),
        check_vma=False,
    )
```

```python
from functools import partial
import math

import jax
import jax.numpy as jnp
from jax import lax
from jax.experimental import pallas as pl
from jax.experimental.pallas import tpu as pltpu
from jax.sharding import PartitionSpec as P
import numpy as np

HEAD_DIM = 64


def half_columns(values, which, size):
    return lax.dynamic_slice_in_dim(values, which * size, size, axis=1)


def flat_pairs(count, target):
    pairs = []
    for row in range(count):
        for side in range(2):
            goal = target(row, row % 2, side)
            if goal is not None:
                pairs.append((row * 2 + side, goal[0] * 2 + goal[1]))
    return pairs


def send(values, pairs):
    return lax.ppermute(values, ("dp", "tensor"), pairs)


def half_of(values, which, size):
    return lax.dynamic_slice_in_dim(values, which * size, size, axis=0)


BLOCK = 256
LANES = 128
VMEM_LIMIT = 56 * 1024 * 1024
SMALL = pl.CostEstimate(flops=1, bytes_accessed=1, transcendentals=0)


def doc_ends(lengths_ref, docs):
    ends = [lengths_ref[0, 0]]
    for number in range(1, docs):
        ends.append(ends[-1] + lengths_ref[0, number])
    return ends


def doc_start(index, ends):
    start = jnp.zeros_like(index)
    for end in ends:
        start = jnp.where(index >= end, end, start)
    return start


def first_key(index, ends, real):
    return jnp.where(index >= real, index, doc_start(index, ends))


def rope_tables(ends, row_len, freq_ref, cos_ref, sin_ref):
    index = lax.broadcasted_iota(jnp.int32, (1, row_len), 1)
    position = (index - doc_start(index, ends)).astype(jnp.float32)
    angles = freq_ref[...] * position
    cosine, sine = jnp.cos(angles), jnp.sin(angles)
    cos_ref[...] = jnp.concatenate([cosine] * 4, axis=0).T
    sin_ref[...] = jnp.concatenate([-sine, sine] * 2, axis=0).T


def turned(values, cosine, sine, low_half):
    ahead = pltpu.roll(values, LANES - HEAD_DIM // 2, 1)
    behind = pltpu.roll(values, HEAD_DIM // 2, 1)
    return values * cosine + jnp.where(low_half, ahead, behind) * sine


def normed(values):
    average = jnp.mean(values, axis=-1, keepdims=True)
    centered = values - average
    return centered * lax.rsqrt(jnp.mean(centered * centered, axis=-1, keepdims=True) + 1e-05)


def contract(left, right, left_dim, right_dim):
    return lax.dot_general(
        left, right, (((left_dim,), (right_dim,)), ((), ())), preferred_element_type=jnp.float32
    )


def prepare(docs, lengths_ref, freq_ref, rows_of, gain_ref, attn_in_ref, cos_ref, sin_ref):
    row_len = attn_in_ref.shape[0]

    @pl.when(pl.program_id(0) == 0)
    def _():
        rope_tables(doc_ends(lengths_ref, docs), row_len, freq_ref, cos_ref, sin_ref)
        for number in range(row_len // BLOCK):
            rows = pl.ds(number * BLOCK, BLOCK)
            attn_in_ref[rows, :] = (
                normed(rows_of(rows)) * gain_ref[...]
            ).astype(jnp.bfloat16)


def head_masks():
    lane = lax.broadcasted_iota(jnp.int32, (1, LANES), 1)
    return (lax.rem(lane, HEAD_DIM) < HEAD_DIM // 2, lane < HEAD_DIM)


def forward_kernel(docs, first, lengths_ref, pad_ref, freq_ref, gain_ref, *refs):
    if first:
        x_ref, wq_ref, wk_ref, wv_ref, out_ref, attn_in_ref, cos_ref, sin_ref, q_ref, k_ref, v_ref = refs
        row_len = x_ref.shape[0]
        prepare(
            docs, lengths_ref, freq_ref, lambda rows: x_ref[rows, :].astype(jnp.float32), gain_ref, attn_in_ref, cos_ref, sin_ref
        )
    else:
        attn_in_ref, cos_ref, sin_ref, wq_ref, wk_ref, wv_ref, out_ref, q_ref, k_ref, v_ref = refs
        row_len = attn_in_ref.shape[0]
    low_half, even = head_masks()
    group = wq_ref.shape[1]
    scale = 1.0 / math.sqrt(HEAD_DIM)
    for number in range(row_len // BLOCK):
        rows = pl.ds(number * BLOCK, BLOCK)
        block = attn_in_ref[rows, :]
        query = jnp.dot(block, wq_ref[...], preferred_element_type=jnp.float32)
        key = jnp.dot(block, wk_ref[...], preferred_element_type=jnp.float32)
        v_ref[rows, :] = jnp.dot(block, wv_ref[...], preferred_element_type=jnp.float32).astype(jnp.bfloat16)
        cosine, sine = cos_ref[rows, :], sin_ref[rows, :]
        for pair in range(group // LANES):
            cols = slice(pair * LANES, (pair + 1) * LANES)
            q_ref[rows, cols] = (turned(query[:, cols], cosine, sine, low_half) * scale).astype(jnp.bfloat16)
            k_ref[rows, cols] = turned(key[:, cols], cosine, sine, low_half).astype(jnp.bfloat16)
    ends = doc_ends(lengths_ref, docs)
    real = row_len - pad_ref[0]
    for number in range(row_len // BLOCK):
        rows = pl.ds(number * BLOCK, BLOCK)
        keys = (number + 1) * BLOCK
        query_index = number * BLOCK + lax.broadcasted_iota(jnp.int32, (BLOCK, 1), 0)
        start = first_key(query_index, ends, real)
        key_index = lax.broadcasted_iota(jnp.int32, (1, keys), 1)
        allowed = (key_index >= start) & (key_index <= query_index)
        for pair in range(group // LANES):
            cols = slice(pair * LANES, (pair + 1) * LANES)
            query = q_ref[rows, cols]
            key, value = k_ref[:keys, cols], v_ref[:keys, cols]
            results = []
            for chosen in (even, jnp.logical_not(even)):
                one = query * chosen.astype(jnp.bfloat16)
                scores = jnp.where(allowed, contract(one, key, 1, 1), -1e30)
                weights = jnp.exp(scores - jnp.max(scores, axis=-1, keepdims=True))
                total = jnp.sum(weights, axis=-1, keepdims=True)
                results.append(
                    jnp.dot(weights.astype(jnp.bfloat16), value, preferred_element_type=jnp.float32) / total
                )
            out_ref[rows, cols] = jnp.where(even, results[0], results[1]).astype(jnp.bfloat16).astype(jnp.float32)


def ready_kernel(
    docs, where_ref, lengths_ref, pad_ref, freq_ref, here_ref, there_ref, gain_ref, wq_ref, wk_ref, wv_ref,
    q_ref, k_ref, v_ref, log_ref, attn_in_ref, cos_ref, sin_ref,
):
    row_len = here_ref.shape[0]
    flag = where_ref[1]
    prepare(
        docs,
        lengths_ref,
        freq_ref,
        lambda rows: jnp.where(flag != 0, here_ref[rows, :].astype(jnp.float32), there_ref[rows, :]),
        gain_ref,
        attn_in_ref,
        cos_ref,
        sin_ref,
    )
    low_half, even = head_masks()
    group = wq_ref.shape[1]
    scale = 1.0 / math.sqrt(HEAD_DIM)
    for number in range(row_len // BLOCK):
        rows = pl.ds(number * BLOCK, BLOCK)
        block = attn_in_ref[rows, :]
        query = jnp.dot(block, wq_ref[...], preferred_element_type=jnp.float32)
        key = jnp.dot(block, wk_ref[...], preferred_element_type=jnp.float32)
        v_ref[rows, :] = jnp.dot(block, wv_ref[...], preferred_element_type=jnp.float32).astype(jnp.bfloat16)
        cosine, sine = cos_ref[rows, :], sin_ref[rows, :]
        for pair in range(group // LANES):
            cols = slice(pair * LANES, (pair + 1) * LANES)
            q_ref[rows, cols] = (turned(query[:, cols], cosine, sine, low_half) * scale).astype(jnp.bfloat16)
            k_ref[rows, cols] = turned(key[:, cols], cosine, sine, low_half).astype(jnp.bfloat16)
    ends = doc_ends(lengths_ref, docs)
    real = row_len - pad_ref[0]
    for number in range(row_len // BLOCK):
        rows = pl.ds(number * BLOCK, BLOCK)
        keys = (number + 1) * BLOCK
        query_index = number * BLOCK + lax.broadcasted_iota(jnp.int32, (1, BLOCK), 1)
        start = first_key(query_index, ends, real)
        key_index = lax.broadcasted_iota(jnp.int32, (keys, 1), 0)
        allowed = (key_index >= start) & (key_index <= query_index)
        for pair in range(group // LANES):
            cols = slice(pair * LANES, (pair + 1) * LANES)
            query, key = q_ref[rows, cols], k_ref[:keys, cols]
            for side, chosen in enumerate((even, jnp.logical_not(even))):
                one = query * chosen.astype(jnp.bfloat16)
                scores = jnp.where(allowed, contract(key, one, 1, 1), -1e30)
                highest = jnp.max(scores, axis=0, keepdims=True)
                total = jnp.sum(jnp.exp(scores - highest), axis=0, keepdims=True)
                head = pair * 2 + side
                log_ref[0, head : head + 1, rows] = highest + jnp.log(total)


def backward_kernel(
    docs, lengths_ref, pad_ref, cos_ref, sin_ref, q_ref, k_ref, v_ref, log_ref, grad_ref,
    gq_ref, gk_ref, gv_ref, key_sum, value_sum,
):
    row_len = q_ref.shape[0]
    low_half, even = head_masks()
    scale = 1.0 / math.sqrt(HEAD_DIM)
    ends = doc_ends(lengths_ref, docs)
    real = row_len - pad_ref[0]
    blocks = row_len // BLOCK
    for number in range(blocks - 1, -1, -1):
        rows = pl.ds(number * BLOCK, BLOCK)
        keys = (number + 1) * BLOCK
        query_index = number * BLOCK + lax.broadcasted_iota(jnp.int32, (1, BLOCK), 1)
        start = first_key(query_index, ends, real)
        key_index = lax.broadcasted_iota(jnp.int32, (keys, 1), 0)
        allowed = (key_index >= start) & (key_index <= query_index)
        query, grad = q_ref[rows, :], grad_ref[rows, :]
        key, value = k_ref[:keys, :], v_ref[:keys, :]
        parts = []
        for side, chosen in enumerate((even, jnp.logical_not(even))):
            mask = chosen.astype(jnp.bfloat16)
            one_query, one_grad = query * mask, grad * mask
            scores = jnp.where(allowed, contract(key, one_query, 1, 1), -1e30)
            weights = jnp.exp(scores - log_ref[0, side : side + 1, rows])
            soft = contract(value, one_grad, 1, 1)
            cross = jnp.sum(soft * weights, axis=0, keepdims=True)
            grad_scores = (weights * (soft - cross)).astype(jnp.bfloat16)
            low_weights = weights.astype(jnp.bfloat16)
            parts.append((
                contract(grad_scores, key, 0, 0),
                jnp.dot(grad_scores, one_query, preferred_element_type=jnp.float32),
                jnp.dot(low_weights, one_grad, preferred_element_type=jnp.float32),
            ))
        grad_query = jnp.where(even, parts[0][0], parts[1][0]) * scale
        gq_ref[rows, :] = turned(grad_query, cos_ref[rows, :], -sin_ref[rows, :], low_half).astype(jnp.bfloat16)
        if number == blocks - 1:
            key_sum[...] = parts[0][1] + parts[1][1]
            value_sum[...] = parts[0][2] + parts[1][2]
        else:
            key_sum[:keys, :] += parts[0][1] + parts[1][1]
            value_sum[:keys, :] += parts[0][2] + parts[1][2]
    for number in range(blocks):
        rows = pl.ds(number * BLOCK, BLOCK)
        gk_ref[rows, :] = turned(
            key_sum[rows, :], cos_ref[rows, :], -sin_ref[rows, :], low_half
        ).astype(jnp.bfloat16)
        gv_ref[rows, :] = value_sum[rows, :].astype(jnp.bfloat16)


def smem():
    return pl.BlockSpec(memory_space=pltpu.SMEM)


def whole(shape):
    return pl.BlockSpec(shape, lambda step: (0,) * len(shape))


def frequencies():
    half_dim = HEAD_DIM // 2
    return (10000.0 ** (-2.0 * np.arange(half_dim) / HEAD_DIM)).astype(np.float32)[:, None]


def attention_forward(number, sources, lengths, pad_count, gain, w_query, w_key, w_value):
    row_len, width = sources[0].shape
    first = number == 0
    group = w_query.shape[1] // 2
    weight = pl.BlockSpec((width, group), lambda step: (0, number))
    table = jax.ShapeDtypeStruct((row_len, LANES), jnp.float32)
    outs = [jax.ShapeDtypeStruct((row_len, group), jnp.float32)]
    if first:
        outs += [jax.ShapeDtypeStruct((row_len, width), jnp.bfloat16), table, table]
    return pl.pallas_call(
        partial(forward_kernel, lengths.shape[1], first),
        grid=(1,),
        in_specs=[
            smem(), smem(), whole((HEAD_DIM // 2, 1)), whole((1, width)),
            *(whole(source.shape) for source in sources), weight, weight, weight,
        ],
        out_specs=[whole(out.shape) for out in outs],
        out_shape=outs,
        scratch_shapes=[pltpu.VMEM((row_len, group), jnp.bfloat16)] * 3,
        compiler_params=pltpu.CompilerParams(vmem_limit_bytes=VMEM_LIMIT),
        cost_estimate=SMALL,
        name="attention_forward",
    )(lengths, pad_count, jnp.asarray(frequencies()), gain[None], *sources, w_query, w_key, w_value)


def attention_ready(where, block_in, there, lengths, pad_count, gain, weights):
    row_len, width = block_in.shape
    wide = weights.shape[1] // 3
    group = 2 * LANES
    heads = group // HEAD_DIM
    steps = wide // group
    weight = [pl.BlockSpec((width, group), lambda step, part=part: (0, part * steps + step)) for part in range(3)]
    part = pl.BlockSpec((row_len, group), lambda step: (0, step))
    table = jax.ShapeDtypeStruct((row_len, LANES), jnp.float32)
    rows = jax.ShapeDtypeStruct((row_len, wide), jnp.bfloat16)
    return pl.pallas_call(
        partial(ready_kernel, lengths.shape[1]),
        grid=(wide // group,),
        in_specs=[
            smem(), smem(), smem(), whole((HEAD_DIM // 2, 1)), whole((row_len, width)), whole((row_len, width)), whole((1, width)), *weight,
        ],
        out_specs=[
            part, part, part,
            pl.BlockSpec((1, heads, row_len), lambda step: (step, 0, 0)),
            whole((row_len, width)), whole((row_len, LANES)), whole((row_len, LANES)),
        ],
        out_shape=[
            rows, rows, rows,
            jax.ShapeDtypeStruct((wide // group, heads, row_len), jnp.float32),
            jax.ShapeDtypeStruct((row_len, width), jnp.bfloat16), table, table,
        ],
        compiler_params=pltpu.CompilerParams(vmem_limit_bytes=VMEM_LIMIT),
        cost_estimate=SMALL,
        name="attention_ready",
    )(where, lengths, pad_count, jnp.asarray(frequencies()), block_in, there, gain[None], weights, weights, weights)


def attention_backward(ready, lengths, pad_count, grad_heads):
    query, key, value, logs, _, cosine, sine = ready
    row_len, wide = query.shape
    pairs = wide // LANES
    logs = logs.reshape(pairs, LANES // HEAD_DIM, row_len)
    part = pl.BlockSpec((row_len, LANES), lambda step: (0, step))
    rows = jax.ShapeDtypeStruct((row_len, wide), jnp.bfloat16)
    return pl.pallas_call(
        partial(backward_kernel, lengths.shape[1]),
        grid=(pairs,),
        in_specs=[
            smem(), smem(), whole((row_len, LANES)), whole((row_len, LANES)), part, part, part,
            pl.BlockSpec((1, LANES // HEAD_DIM, row_len), lambda step: (step, 0, 0)), part,
        ],
        out_specs=[part, part, part],
        out_shape=[rows, rows, rows],
        scratch_shapes=[pltpu.VMEM((row_len, LANES), jnp.float32), pltpu.VMEM((row_len, LANES), jnp.float32)],
        compiler_params=pltpu.CompilerParams(vmem_limit_bytes=VMEM_LIMIT),
        cost_estimate=SMALL,
        name="attention_backward",
    )(lengths, pad_count, cosine, sine, query, key, value, logs, grad_heads)


FF_STEPS = 4
PARTS = 2
TILE = 256


def chosen_rows(flag, here_ref, there_ref):
    return jnp.where(flag != 0, here_ref[...].astype(jnp.float32), there_ref[...])


def norm_stats(values):
    average = jnp.mean(values, axis=-1, keepdims=True)
    centered = values - average
    inverse = lax.rsqrt(jnp.mean(centered * centered, axis=-1, keepdims=True) + 1e-05)
    return (centered * inverse, inverse)


def norm_pull(grad, gain, hat, inverse):
    scaled = grad * gain
    mean_scaled = jnp.mean(scaled, axis=-1, keepdims=True)
    mean_cross = jnp.mean(scaled * hat, axis=-1, keepdims=True)
    return inverse * (scaled - mean_scaled - hat * mean_cross)


def add_gain(ref, step, row, value):
    @pl.when(step == 0)
    def _():
        ref[row : row + 1, :] = value

    @pl.when(step != 0)
    def _():
        ref[row : row + 1, :] += value


def hidden_kernel(where_ref, low_ref, high_ref, w_out_ref, arrived_ref, here_ref, there_ref, gain_ref, hidden_ref, total_ref):
    group = low_ref.shape[1]
    total = jnp.dot(low_ref[...], w_out_ref[:group, :], preferred_element_type=jnp.float32) + arrived_ref[...]
    total += jnp.dot(high_ref[...], w_out_ref[group:, :], preferred_element_type=jnp.float32)
    total_ref[...] = total
    hat, _ = norm_stats(total)
    hidden_ref[...] = chosen_rows(where_ref[1], here_ref, there_ref) + hat * gain_ref[...]


def mlp_forward_kernel(hidden_ref, gain_ref, up_ref, down_ref, *refs):
    mlp_in_ref, act_ref, slope_ref, part_ref = refs[-4:]
    step = pl.program_id(0)

    @pl.when(step == 0)
    def _():
        hat, _ = norm_stats(hidden_ref[...])
        mlp_in_ref[...] = (hat * gain_ref[...]).astype(jnp.bfloat16)

    factor = math.sqrt(2.0 / math.pi)
    size = up_ref.shape[1] // PARTS
    part = None
    for number in range(PARTS):
        cols = slice(number * size, (number + 1) * size)
        pre = jnp.dot(mlp_in_ref[...], up_ref[:, cols], preferred_element_type=jnp.float32)
        squared = pre * pre
        bent = jnp.tanh(factor * pre * (1.0 + 0.044715 * squared))
        gate = 0.5 * (1.0 + bent)
        act = (pre * gate).astype(jnp.bfloat16)
        act_ref[:, cols] = act
        slope_ref[:, cols] = gate + 0.5 * pre * (1.0 - bent * bent) * (factor + (3.0 * 0.044715 * factor) * squared)
        piece = jnp.dot(act, down_ref[cols, :], preferred_element_type=jnp.float32)
        part = piece if part is None else part + piece

    @pl.when(step == 0)
    def _():
        part_ref[...] = part

    @pl.when(step != 0)
    def _():
        part_ref[...] += part


def mlp_backward_kernel(
    where_ref, hidden_ref, total_ref, here_ref, there_ref, gain_ref, down_ref, up_ref, slope_ref, *refs
):
    block_ref, low_ref, gain_sum_ref, grad_up_ref, part_ref = refs[-5:]
    step = pl.program_id(0)

    @pl.when(step == 0)
    def _():
        hat, inverse = norm_stats(total_ref[...])
        cot = chosen_rows(where_ref[1], here_ref, there_ref)
        block_ref[...] = hidden_ref[...] + hat * gain_ref[...]
        low_ref[...] = norm_pull(cot, gain_ref[...], hat, inverse).astype(jnp.bfloat16)
        gain_sum_ref[...] = jnp.broadcast_to(jnp.sum(cot * hat, axis=0, keepdims=True), gain_sum_ref.shape)

    size = up_ref.shape[1] // PARTS
    part = None
    for number in range(PARTS):
        cols = slice(number * size, (number + 1) * size)
        grad_act = contract(low_ref[...], down_ref[cols, :], 1, 1)
        grad_up = (grad_act * slope_ref[:, cols]).astype(jnp.bfloat16)
        grad_up_ref[:, cols] = grad_up
        piece = contract(grad_up, up_ref[:, cols], 1, 1)
        part = piece if part is None else part + piece

    @pl.when(step == 0)
    def _():
        part_ref[...] = part

    @pl.when(step != 0)
    def _():
        part_ref[...] += part


def residual_kernel(
    where_ref, part_ref, arrived_ref, hidden_ref, attn_ref, here_ref, there_ref, gain_mlp_ref, gain_attn_ref, *refs
):
    res_ref, attn_grad_ref, gains_ref = refs[-3:]
    step = pl.program_id(0)
    grad = part_ref[...] + arrived_ref[...]
    hat, inverse = norm_stats(hidden_ref[...])
    cot = chosen_rows(where_ref[1], here_ref, there_ref)
    res = cot + norm_pull(grad, gain_mlp_ref[...], hat, inverse)
    res_ref[...] = res
    add_gain(gains_ref, step, 0, jnp.sum(grad * hat, axis=0, keepdims=True))
    hat, inverse = norm_stats(attn_ref[...])
    attn_grad_ref[...] = norm_pull(res, gain_attn_ref[...], hat, inverse)
    add_gain(gains_ref, step, 1, jnp.sum(res * hat, axis=0, keepdims=True))


def other_kernel(where_ref, grad_ref, weight_ref, out_ref):
    piece = contract(grad_ref[...], weight_ref[...], 1, 1)

    @pl.when(pl.program_id(0) == 0)
    def _():
        out_ref[...] = piece

    @pl.when(pl.program_id(0) != 0)
    def _():
        out_ref[...] += piece


def input_kernel(
    where_ref, grad_ref, weight_ref, arrived_ref, here_ref, there_ref, res_ref, gain_ref, out_ref, gain_sum_ref, sum_ref
):
    step = pl.program_id(0)
    piece = contract(grad_ref[...], weight_ref[...], 1, 1)

    @pl.when(step == 0)
    def _():
        sum_ref[...] = piece + arrived_ref[...]

    @pl.when(step != 0)
    def _():
        sum_ref[...] += piece

    @pl.when(step == pl.num_programs(0) - 1)
    def _():
        grad = sum_ref[...]
        hat, inverse = norm_stats(chosen_rows(where_ref[1], here_ref, there_ref))
        out_ref[...] = res_ref[...] + norm_pull(grad, gain_ref[...], hat, inverse)
        gain_sum_ref[...] = jnp.broadcast_to(jnp.sum(grad * hat, axis=0, keepdims=True), gain_sum_ref.shape)


def pack_kernel(where_ref, x_ref, cot_ref, out_ref):
    step = pl.program_id(0)

    @pl.when(step < 2)
    def _():
        out_ref[...] = x_ref[...].astype(jnp.float32)

    @pl.when(step == 2)
    def _():
        out_ref[...] = cot_ref[...].astype(jnp.float32)


def call(kernel, name, steps, where, arrays, specs, outs, aliases, flops):
    moved = sum(array.size * array.dtype.itemsize for array in arrays)
    return pl.pallas_call(
        kernel,
        grid_spec=pltpu.PrefetchScalarGridSpec(
            num_scalar_prefetch=0 if where is None else 1,
            grid=(steps,),
            in_specs=specs,
            out_specs=[spec for _, spec in outs],
        ),
        out_shape=[shape for shape, _ in outs],
        input_output_aliases=aliases,
        compiler_params=pltpu.CompilerParams(vmem_limit_bytes=VMEM_LIMIT),
        cost_estimate=SMALL,
        name=name,
    )(*(() if where is None else (where,)), *arrays)


def rows_spec(rows, width, place):
    return pl.BlockSpec((rows, width), lambda step, *where: (place(step, *where), 0))


def fixed_spec(shape):
    return pl.BlockSpec(shape, lambda *args: (0,) * len(shape))


def hidden_chunk(where, number, attended, w_out, arrived, block_in, there, gain):
    row_len, group = attended[0].shape
    width = w_out.shape[1]
    rows = row_len // 4
    mine = rows_spec(rows, width, lambda step, where: where[0] * 2 + number)
    mine_attended = rows_spec(rows, group, lambda step, where: where[0] * 2 + number)
    shape = jax.ShapeDtypeStruct((rows, width), jnp.float32)
    return call(
        hidden_kernel, "hidden", 1, where,
        (*attended, w_out, arrived, block_in, there, gain[None]),
        [
            mine_attended, mine_attended, fixed_spec(w_out.shape),
            rows_spec(rows, width, lambda step, where: number), mine, mine, fixed_spec((1, width)),
        ],
        [(shape, fixed_spec((rows, width))), (shape, fixed_spec((rows, width)))],
        {}, 4 * rows * group * width,
    )


def mlp_forward(number, hidden, gain, w_up, w_down, buffers):
    rows, width = hidden.shape
    inner = w_up.shape[1]
    size = inner // FF_STEPS
    spare = [pl.BlockSpec(memory_space=pl.ANY)] * len(buffers)
    return call(
        mlp_forward_kernel, "mlp_forward", FF_STEPS, None,
        (hidden, gain[None], w_up, w_down, *buffers),
        [
            fixed_spec((rows, width)), fixed_spec((1, width)),
            pl.BlockSpec((width, size), lambda step: (0, step)),
            pl.BlockSpec((size, width), lambda step: (step, 0)),
            *spare,
        ],
        [
            (jax.ShapeDtypeStruct((4 * rows, width), jnp.bfloat16), pl.BlockSpec((rows, width), lambda step: (number, 0))),
            (jax.ShapeDtypeStruct((4 * rows, inner), jnp.bfloat16), pl.BlockSpec((rows, size), lambda step: (number, step))),
            (jax.ShapeDtypeStruct((rows, inner), jnp.float32), pl.BlockSpec((rows, size), lambda step: (0, step))),
            (jax.ShapeDtypeStruct((rows, width), jnp.float32), fixed_spec((rows, width))),
        ],
        {4 + index: index for index in range(len(buffers))}, 4 * rows * width * inner,
    )


def mlp_backward(where, number, hidden, total, cotangent, there, gain, w_down, w_up, slope, buffers):
    rows, width = hidden.shape
    inner = w_up.shape[1]
    size = inner // FF_STEPS
    part = number % 2
    spare = [pl.BlockSpec(memory_space=pl.ANY)] * len(buffers)
    return call(
        mlp_backward_kernel, "mlp_backward", FF_STEPS, where,
        (hidden, total, cotangent, there, gain[None], w_down, w_up, slope, *buffers),
        [
            fixed_spec((rows, width)), fixed_spec((rows, width)),
            rows_spec(rows, width, lambda step, where: where[0] * 2 + part),
            rows_spec(rows, width, lambda step, where: 4 + part),
            fixed_spec((1, width)),
            pl.BlockSpec((size, width), lambda step, where: (step, 0)),
            pl.BlockSpec((width, size), lambda step, where: (0, step)),
            pl.BlockSpec((rows, size), lambda step, where: (0, step)),
            *spare,
        ],
        [
            (jax.ShapeDtypeStruct((rows, width), jnp.float32), fixed_spec((rows, width))),
            (jax.ShapeDtypeStruct((4 * rows, width), jnp.bfloat16), pl.BlockSpec((rows, width), lambda step, where: (number, 0))),
            (jax.ShapeDtypeStruct((8, width), jnp.float32), fixed_spec((8, width))),
            (jax.ShapeDtypeStruct((4 * rows, inner), jnp.bfloat16), pl.BlockSpec((rows, size), lambda step, where: (number, step))),
            (jax.ShapeDtypeStruct((rows, width), jnp.float32), fixed_spec((rows, width))),
        ],
        {9 + index: 1 + 2 * index for index in range(len(buffers))}, 4 * rows * width * inner,
    )


def residual_chunk(where, number, part, arrived, hidden, attn_total, cotangent, there, gain_mlp, gain_attn, buffers):
    rows, width = part.shape
    steps = rows // TILE
    local = rows_spec(TILE, width, lambda step, where: step)
    spare = [pl.BlockSpec(memory_space=pl.ANY)] * len(buffers)
    whole_half = jax.ShapeDtypeStruct((2 * rows, width), jnp.float32)
    place = rows_spec(TILE, width, lambda step, where: number * steps + step)
    return call(
        residual_kernel, "residual", steps, where,
        (part, arrived, hidden, attn_total, cotangent, there, gain_mlp[None], gain_attn[None], *buffers),
        [
            local, local, local, local,
            rows_spec(TILE, width, lambda step, where: (where[0] * 2 + number) * steps + step),
            rows_spec(TILE, width, lambda step, where: (4 + number) * steps + step),
            fixed_spec((1, width)), fixed_spec((1, width)),
            *spare,
        ],
        [(whole_half, place), (whole_half, place), (jax.ShapeDtypeStruct((8, width), jnp.float32), fixed_spec((8, width)))],
        {9 + index: index for index in range(len(buffers))}, 20 * rows * width,
    )


def packed(where, block_in, cotangent):
    row_len, width = block_in.shape
    half = row_len // 2
    return call(
        pack_kernel, "packed", 3, where, (block_in, cotangent),
        [
            rows_spec(half, width, lambda step, where: jnp.minimum(step, 1)),
            rows_spec(half, width, lambda step, where: 1 - where[0]),
        ],
        [(jax.ShapeDtypeStruct((3 * half, width), jnp.float32), rows_spec(half, width, lambda step, where: step))],
        {}, 0,
    )[0]


def outer_kernel(where_ref, left_ref, right_ref, out_ref, turned_ref):
    @pl.when(pl.program_id(0) == 0)
    def _():
        turned_ref[...] = left_ref[...].T

    out_ref[...] = jnp.dot(turned_ref[...], right_ref[...], preferred_element_type=jnp.float32)


def outer(where, left, right, pick, columns):
    tokens, width = left.shape
    size = min(512, columns)
    steps = columns // size
    return pl.pallas_call(
        outer_kernel,
        grid_spec=pltpu.PrefetchScalarGridSpec(
            num_scalar_prefetch=1,
            grid=(steps,),
            in_specs=[
                fixed_spec((tokens, width)),
                pl.BlockSpec((tokens, size), lambda step, where: (0, pick(where) * steps + step)),
            ],
            out_specs=pl.BlockSpec((width, size), lambda step, where: (0, step)),
            scratch_shapes=[pltpu.VMEM((width, tokens), left.dtype)],
        ),
        out_shape=jax.ShapeDtypeStruct((width, columns), jnp.float32),
        compiler_params=pltpu.CompilerParams(vmem_limit_bytes=VMEM_LIMIT),
        cost_estimate=SMALL,
        name="outer",
    )(where, left, right)


def halves_kernel(count, sources, where_ref, *refs):
    stays, leaves = refs[:count], refs[count : 2 * count]
    outs = refs[-count - 1 : -1]
    leaving_ref = refs[-1]
    start = 0
    for stay_ref, leave_ref, out_ref, source in zip(stays, leaves, outs, sources):
        columns = stay_ref.shape[-1]
        stay, leave = stay_ref[0], leave_ref[0]
        if source is not None:
            number, first = source
            stay += refs[2 * count + 2 * number][0, :, first : first + columns]
            leave += refs[2 * count + 2 * number + 1][0, :, first : first + columns]
        out_ref[0] = stay
        leaving_ref[0, :, start : start + columns] = leave
        start += columns


def halves(where, step, held, arrived, sources):
    blocks, rows = held[0].shape[0] // 2, held[0].shape[1]
    widths = [part.shape[2] for part in held]

    def spec(width, stays):
        def place(index, where):
            low, bit = where[2 + 2 * step], where[3 + 2 * step]
            bit = bit if stays else 1 - bit
            high = lax.shift_right_logical(index, low)
            return (lax.shift_left(2 * high + bit, low) + index - lax.shift_left(high, low), 0, 0)

        return pl.BlockSpec((1, rows, width), place)

    arrays = list(held) * 2
    specs = [spec(width, stays) for stays in (True, False) for width in widths]
    for array in arrived:
        arrays += [array] * 2
        specs += [spec(array.shape[2], stays) for stays in (True, False)]
    outs = [*widths, sum(widths)]
    *staying, leaving = pl.pallas_call(
        partial(halves_kernel, len(held), sources),
        grid_spec=pltpu.PrefetchScalarGridSpec(
            num_scalar_prefetch=1,
            grid=(blocks,),
            in_specs=specs,
            out_specs=[pl.BlockSpec((1, rows, width), lambda index, where: (index, 0, 0)) for width in outs],
        ),
        out_shape=[jax.ShapeDtypeStruct((blocks, rows, width), jnp.float32) for width in outs],
        compiler_params=pltpu.CompilerParams(vmem_limit_bytes=VMEM_LIMIT),
        cost_estimate=SMALL,
        name="halves",
    )(where, *arrays)
    return staying, leaving


def input_specs(grads, weights, other):
    row_len, wide = grads.shape[0], grads.shape[1] // 3
    width = weights.shape[0]
    half = row_len // 2
    return [
        pl.BlockSpec((half, wide), lambda step, where: (1 - where[0] if other else where[0], step)),
        pl.BlockSpec((width, wide), lambda step, where: (0, step)),
    ], (half, width)


def input_other(where, grads, weights):
    specs, shape = input_specs(grads, weights, True)
    return call(
        other_kernel, "input_other", 3, where, (grads, weights), specs,
        [(jax.ShapeDtypeStruct(shape, jnp.float32), fixed_spec(shape))], {}, 2 * shape[0] * weights.size,
    )[0]


def input_own(where, grads, weights, arrived, block_in, there, res, gain):
    specs, shape = input_specs(grads, weights, False)
    mine = rows_spec(*shape, lambda step, where: where[0])
    moved = sum(array.size * array.dtype.itemsize for array in (grads, weights, arrived, block_in, there, res))
    return pl.pallas_call(
        input_kernel,
        grid_spec=pltpu.PrefetchScalarGridSpec(
            num_scalar_prefetch=1,
            grid=(3,),
            in_specs=specs + [fixed_spec(shape), mine, mine, fixed_spec(shape), fixed_spec((1, shape[1]))],
            out_specs=[fixed_spec(shape), fixed_spec((8, shape[1]))],
            scratch_shapes=[pltpu.VMEM(shape, jnp.float32)],
        ),
        out_shape=[jax.ShapeDtypeStruct(shape, jnp.float32), jax.ShapeDtypeStruct((8, shape[1]), jnp.float32)],
        compiler_params=pltpu.CompilerParams(vmem_limit_bytes=VMEM_LIMIT),
        cost_estimate=SMALL,
        name="input_own",
    )(where, grads, weights, arrived, block_in, there, res, gain[None])


def after(values, *others):
    return lax.optimization_barrier((values, others))[0]


def ordered(mine, other, bit, axis):
    low = jnp.where(bit == 0, mine, other)
    high = jnp.where(bit == 0, other, mine)
    return jnp.concatenate([low, high], axis=axis)


def body(
    dp_size,
    block_in,
    cotangent,
    lengths,
    pad_count,
    norm_in_attn,
    w_query,
    w_key,
    w_value,
    w_out,
    norm_out_attn,
    norm_in_mlp,
    w_up,
    w_down,
    norm_out_mlp,
):
    f32, bf16 = jnp.float32, jnp.bfloat16
    place = lax.axis_index("dp")
    core = lax.rem(place, 2)
    chip = lax.div(place, 2)
    side = lax.axis_index("tensor")
    same = core == side
    keep = same.astype(f32)
    first = (core == 0).astype(f32)
    chips = dp_size // 2
    levels = chips.bit_length() - 1
    bits = [lax.rem(lax.div(chip, 1 << level), 2) for level in range(levels)]
    swap = flat_pairs(dp_size, lambda d, c, t: (d ^ 1, 1 - t) if c != t else None)
    cross = flat_pairs(dp_size, lambda d, c, t: (d ^ 1, t))
    over = flat_pairs(dp_size, lambda d, c, t: (d, 1 - t))
    flips = [flat_pairs(dp_size, lambda d, c, t: (d ^ (2 << level), t)) for level in range(levels)]
    row_len, width = block_in.shape
    half = row_len // 2
    chunk = half // 2
    wide = w_query.shape[1]
    hidden = w_up.shape[1]

    shares = min(3, levels)
    near = flat_pairs(dp_size, lambda d, c, t: (d ^ 2, t) if c != t else None)

    orders = (list(range(levels)), [*range(1, levels), 0])
    hop_facts = []
    for step in range(levels):
        places = [sum(1 for later in order[step + 1 :] if later < order[step]) for order in orders]
        hop_facts.append(jnp.where(core == 0, places[0], places[1]))
        hop_facts.append(jnp.where(core == 0, bits[orders[0][step]], bits[orders[1][step]]))
    hops = [flat_pairs(dp_size, lambda d, c, t: (d ^ (2 << orders[c][step]), t)) for step in range(levels)]
    for bit in bits:
        hop_facts += [jnp.zeros_like(bit), bit]
    where_own = jnp.stack([core, same.astype(jnp.int32), *hop_facts])
    where_peer = jnp.stack([core, 1 - same.astype(jnp.int32)])
    out_rows = wide // 2
    weights_here = (w_query, w_key, w_value)
    part_rows = width >> shares
    which = sum(bits[level] << level for level in range(shares))
    parts_here = jnp.concatenate([half_of(weight, which, part_rows) for weight in weights_here], axis=1)
    w_out_sent = send(half_of(w_out, bits[0], out_rows).astype(f32), swap)
    attended_low, *sources = attention_forward(0, (block_in,), lengths, pad_count, norm_in_attn, w_query, w_key, w_value)
    low_sent = send(attended_low, swap)
    sources = after(sources, w_out_sent)
    w_out_sent = ordered(w_out_sent, send(w_out_sent, near), bits[0], 0)
    [attended_high] = attention_forward(1, sources, lengths, pad_count, norm_in_attn, w_query, w_key, w_value)
    high_sent = send(attended_high, swap)
    block_late, cot_late, facts = after((block_in, cotangent, jnp.pad(lengths, ((0, 0), (0, 1)))), low_sent, attended_high)
    facts = facts.astype(f32) + jnp.pad(pad_count.astype(f32)[:, None], ((0, 0), (lengths.shape[1], 0)))
    there = send(packed(where_own, block_late, cot_late), cross)
    facts_there = send(facts, cross)
    low_sent = after(low_sent, attended_high)
    attended = [(attended_low * keep + low_sent).astype(bf16), (attended_high * keep + high_sent).astype(bf16)]
    w_out_mine = (w_out.astype(f32) * keep + w_out_sent).astype(bf16)
    parts_sent = send(after(parts_here, attended[0]).astype(f32), swap)
    facts_row = jnp.where(same, facts, facts_there).astype(jnp.int32)
    docs = lengths.shape[1]
    lengths_row, pad_row = facts_row[:, :docs], facts_row[:, docs]
    part_other = sum(
        jnp.dot(half_of(values, 1 - core, half), w_out_mine[start : start + out_rows], preferred_element_type=f32)
        for values, start in zip(attended, (0, out_rows))
    )
    arrived = send(part_other, cross)
    hidden_own, attn_total, hidden_peer = [], [], []
    for number in range(2):
        one, total = hidden_chunk(where_own, number, attended, w_out_mine, arrived, block_in, there, norm_out_attn)
        hidden_own.append(one)
        attn_total.append(total)
        hidden_peer.append(send(one, over))

    gathered = 1 << shares
    groups = [
        [base + 2 * near_chip + one for near_chip in range(gathered)]
        for base in range(0, dp_size, 2 * gathered)
        for one in range(2)
    ]
    weights_sent = lax.all_gather(after(parts_sent, hidden_own[0]), "dp", axis=0, tiled=True, axis_index_groups=groups)

    buffers, slopes, parts, sums_own = (), [], [], []
    for number in range(4):
        piece = hidden_own[number] if number < 2 else hidden_peer[number - 2]
        if number > 1:
            piece = after(piece, parts[number - 1])
        *buffers, slope, part = mlp_forward(number, piece, norm_in_mlp, w_up, w_down, buffers)
        slopes.append(slope)
        parts.append(part)
        if number >= 2:
            sums_own.append(send(part, over))
    mlp_in_all, activated_all = buffers
    totals, blocks, back_parts, gain_out_mlp = [None] * 4, [None] * 4, [None] * 4, [None] * 4
    buffers = ()

    def add_up(number, gate):
        totals[number] = parts[number] + after(sums_own[number], gate)
        totals[number + 2] = send(totals[number], over)

    add_up(0, parts[3])
    gate = totals[0]
    for number in range(4):
        block, low_all, gain_sum, up_all, part = mlp_backward(
            where_own if number < 2 else where_peer,
            number,
            hidden_own[number] if number < 2 else hidden_peer[number - 2],
            after(totals[number], gate),
            cotangent,
            there,
            norm_out_mlp,
            w_down,
            w_up,
            slopes[number],
            buffers,
        )
        buffers = (low_all, up_all)
        blocks[number], back_parts[number], gain_out_mlp[number] = block, part, gain_sum[0]
        gate = part
        if number == 0:
            add_up(1, part)
            gate = totals[1]
    grad_low_all, grad_up_all = buffers
    sums_own = [send(part, over) for part in back_parts[2:]]

    def residual(number, arrived, buffers):
        return residual_chunk(
            where_own,
            number,
            back_parts[number],
            arrived,
            hidden_own[number],
            attn_total[number],
            cotangent,
            there,
            norm_in_mlp,
            norm_out_attn,
            buffers,
        )

    chip_rows = width // chips
    small = chip_rows // 2

    class Sum:
        def __init__(self, held, arrived, plain=False):
            self.plain = plain
            self.held = [part.reshape(chips, chip_rows, -1) for part in held]
            self.arrived = [] if arrived is None else [arrived.reshape(chips, chip_rows, -1)]
            self.sources = [None if arrived is None or number else (0, 0) for number in range(len(held))]
            self.step = 0

        def hop(self, *gates):
            arrived = [after(array, *gates) for array in self.arrived]
            self.held, leaving = halves(where_own, self.step + levels * self.plain, self.held, arrived, tuple(self.sources))
            self.arrived = [send(leaving, (flips if self.plain else hops)[self.step])]
            starts = np.cumsum([0, *(part.shape[2] for part in self.held)])
            self.sources = [(0, int(start)) for start in starts[:-1]]
            self.step += 1
            return leaving

        def result(self, *gates):
            while self.step < levels:
                gates = (self.hop(*gates),)
            arrived = [after(array, *gates) for array in self.arrived]
            return [
                (part + arrived[number][:, :, start : start + part.shape[2]]).reshape(chip_rows, -1)
                for part, (number, start) in zip(self.held, self.sources)
            ]

    down_other = outer(where_own, grad_low_all, activated_all, lambda where: 1 - where[0], hidden // 2)
    down_kept = outer(where_own, grad_low_all, activated_all, lambda where: where[0], hidden // 2)
    early = Sum([down_kept], send(down_other, cross))
    mlp_in_all, grad_up_all = after((mlp_in_all, grad_up_all), early.hop(down_kept))
    weight_up = outer(where_own, mlp_in_all, grad_up_all, lambda where: 0, hidden)
    grad_up = lax.psum_scatter(weight_up, "dp", scatter_dimension=0, tiled=True)
    weights_late = after(weights_sent, weight_up)
    weights_mine = (jnp.concatenate(weights_here, axis=1).astype(f32) * keep + weights_late).astype(bf16)
    ready = attention_ready(where_own, block_in, there, lengths_row, pad_row, norm_in_attn, weights_mine)
    *buffers, gain_sum = residual(0, after(sums_own[0], ready[0]), ())
    gain_sums = [gain_sum]
    *buffers, gain_sum = residual(1, after(sums_own[1], gain_sum), buffers)
    gain_sums.append(gain_sum)
    grad_res, grad_attn = buffers
    gain_in_mlp = gain_sums[0][0] + gain_sums[1][0]
    gain_out_attn = gain_sums[0][1] + gain_sums[1][1]
    gain_out_mlp = gain_out_mlp[0] + gain_out_mlp[1]

    def to_output(values_own, values_peer):
        stay = jnp.where(same, values_own, values_peer)
        leave = jnp.where(same, values_peer, values_own)
        arrived = send(leave, cross)
        low = stay * first + arrived * (1.0 - first)
        high = arrived * first + stay * (1.0 - first)
        return jnp.concatenate([low, high], axis=0)

    grad_attn_other = send(grad_attn, cross)
    gate = early.hop(gain_sum)
    grad_attn_low = jnp.concatenate(
        [
            grad_attn * first + grad_attn_other * (1.0 - first),
            grad_attn_other * first + grad_attn * (1.0 - first),
        ],
        axis=0,
    ).astype(bf16)
    grad_heads = jnp.einsum("td,ed->te", grad_attn_low, w_out_mine, preferred_element_type=f32).astype(bf16)
    grads = attention_backward(ready, lengths_row, pad_row, after(grad_heads, gate))
    grads = jnp.concatenate(after(grads, early.hop(grads)), axis=1)
    late = Sum([jnp.einsum("td,te->de", ready[4], grads, preferred_element_type=f32)], None)
    gate = late.hop()
    other = input_other(where_own, after(grads, gate), weights_mine)
    other_sent = send(other, cross)
    attended_all = after(jnp.concatenate(attended, axis=1), other)
    weight_out = jnp.einsum("td,te->de", grad_attn_low, attended_all, preferred_element_type=f32)
    weight_out_sent = send(weight_out, swap)
    gate = weight_out
    grad_in_own, gain_in_attn = input_own(
        where_own, grads, weights_mine, after(other_sent, gate), block_in, there, grad_res, norm_in_attn
    )
    grad_in_sent = send(grad_in_own, over)
    gains = jnp.stack([gain_in_attn[0], gain_out_attn, gain_in_mlp, gain_out_mlp], axis=0)
    weight_out_sent, gains = after((weight_out_sent, gains), grad_up)
    gains = jnp.pad((gains + send(gains, cross)).T, ((0, 0), (0, LANES - 4)))
    weight_out = weight_out * keep + weight_out_sent
    out_sent = send(half_columns(weight_out, 1 - core, out_rows), cross)
    extra = Sum([half_columns(weight_out, core, out_rows), gains], out_sent, plain=True)
    gate = late.hop(weight_out)
    gate = extra.hop(gate)
    gate = extra.hop(gate)
    gate = late.hop(gate)
    gate = extra.hop(gate)
    [grad_down] = early.result(gate)
    [held] = late.result(gate)
    grad_out, gains = extra.result()

    def to_core(*parts):
        leaving = jnp.concatenate([half_of(part, 1 - core, small) for part in parts], axis=1)
        arrived, start, results = send(leaving, cross), 0, []
        for part in parts:
            columns = part.shape[1]
            results.append(ordered(half_of(part, core, small), arrived[:, start : start + columns], core, 1))
            start += columns
        return results

    def to_output(values_own, values_peer):
        stay = jnp.where(same, values_own, values_peer)
        leave = jnp.where(same, values_peer, values_own)
        arrived = send(leave, cross)
        low = stay * first + arrived * (1.0 - first)
        high = arrived * first + stay * (1.0 - first)
        return jnp.concatenate([low, high], axis=0)

    grad_down, grad_out = to_core(grad_down, grad_out)
    grad_in = to_output(grad_in_own, after(grad_in_sent, gate))
    for_core = half_of(held, core, small)
    for_other = half_of(held, 1 - core, small)
    diagonal = send(for_other, swap)
    straight = send(
        jnp.where(same, for_other, for_core),
        flat_pairs(dp_size, lambda d, c, t: (d, 1 - t) if c != t else (d ^ 1, t)),
    )
    heads = straight + jnp.where(same, for_core, diagonal)
    gains = half_of(gains, core, small)[:, :4].T
    gains = gains + send(gains, over)
    block_out = to_output(jnp.concatenate(blocks[:2], axis=0), jnp.concatenate(blocks[2:], axis=0)).astype(bf16)
    return (
        block_out,
        grad_in,
        gains[0],
        heads[:, :wide],
        heads[:, wide : 2 * wide],
        heads[:, 2 * wide : 3 * wide],
        grad_out.T,
        gains[1],
        gains[2],
        grad_up,
        grad_down.T,
        gains[3],
    )


def solution(mesh):
    placed = (
        P("dp", None),
        P("dp", None),
        P("dp", None),
        P("dp"),
        P(),
        P(None, "tensor"),
        P(None, "tensor"),
        P(None, "tensor"),
        P("tensor", None),
        P(),
        P(),
        P(None, "tensor"),
        P("tensor", None),
        P(),
    )
    return jax.shard_map(
        partial(body, mesh.shape["dp"]),
        mesh=mesh,
        in_specs=placed,
        out_specs=(
            P("dp", None),
            P("dp", None),
            P("dp"),
            P("dp", "tensor"),
            P("dp", "tensor"),
            P("dp", "tensor"),
            P("tensor", "dp"),
            P("dp"),
            P("dp"),
            P("dp", "tensor"),
            P("tensor", "dp"),
            P("dp"),
        ),
        check_vma=False,
    )
```

```python
from functools import partial
import math

import jax
import jax.numpy as jnp
from jax import lax
from jax.experimental import pallas as pl
from jax.experimental.pallas import tpu as pltpu
from jax.sharding import PartitionSpec as P
import numpy as np

HEAD_DIM = 64


def half_columns(values, which, size):
    return lax.dynamic_slice_in_dim(values, which * size, size, axis=1)


def flat_pairs(count, target):
    pairs = []
    for row in range(count):
        for side in range(2):
            goal = target(row, row % 2, side)
            if goal is not None:
                pairs.append((row * 2 + side, goal[0] * 2 + goal[1]))
    return pairs


def send(values, pairs):
    return lax.ppermute(values, ("dp", "tensor"), pairs)


def half_of(values, which, size):
    return lax.dynamic_slice_in_dim(values, which * size, size, axis=0)


BLOCK = 256
LANES = 128
VMEM_LIMIT = 56 * 1024 * 1024
SMALL = pl.CostEstimate(flops=1, bytes_accessed=1, transcendentals=0)


def doc_ends(lengths_ref, docs):
    ends = [lengths_ref[0, 0]]
    for number in range(1, docs):
        ends.append(ends[-1] + lengths_ref[0, number])
    return ends


def doc_start(index, ends):
    start = jnp.zeros_like(index)
    for end in ends:
        start = jnp.where(index >= end, end, start)
    return start


def first_key(index, ends, real):
    return jnp.where(index >= real, index, doc_start(index, ends))


def rope_tables(ends, row_len, freq_ref, cos_ref, sin_ref):
    index = lax.broadcasted_iota(jnp.int32, (1, row_len), 1)
    position = (index - doc_start(index, ends)).astype(jnp.float32)
    angles = freq_ref[...] * position
    cosine, sine = jnp.cos(angles), jnp.sin(angles)
    cos_ref[...] = jnp.concatenate([cosine] * 4, axis=0).T
    sin_ref[...] = jnp.concatenate([-sine, sine] * 2, axis=0).T


def turned(values, cosine, sine, low_half):
    ahead = pltpu.roll(values, LANES - HEAD_DIM // 2, 1)
    behind = pltpu.roll(values, HEAD_DIM // 2, 1)
    return values * cosine + jnp.where(low_half, ahead, behind) * sine


def normed(values):
    average = jnp.mean(values, axis=-1, keepdims=True)
    centered = values - average
    return centered * lax.rsqrt(jnp.mean(centered * centered, axis=-1, keepdims=True) + 1e-05)


def contract(left, right, left_dim, right_dim):
    return lax.dot_general(
        left, right, (((left_dim,), (right_dim,)), ((), ())), preferred_element_type=jnp.float32
    )


def prepare(docs, lengths_ref, freq_ref, rows_of, gain_ref, attn_in_ref, cos_ref, sin_ref):
    row_len = attn_in_ref.shape[0]

    @pl.when(pl.program_id(0) == 0)
    def _():
        rope_tables(doc_ends(lengths_ref, docs), row_len, freq_ref, cos_ref, sin_ref)
        for number in range(row_len // BLOCK):
            rows = pl.ds(number * BLOCK, BLOCK)
            attn_in_ref[rows, :] = (
                normed(rows_of(rows)) * gain_ref[...]
            ).astype(jnp.bfloat16)


def head_masks():
    lane = lax.broadcasted_iota(jnp.int32, (1, LANES), 1)
    return (lax.rem(lane, HEAD_DIM) < HEAD_DIM // 2, lane < HEAD_DIM)


def forward_kernel(docs, first, lengths_ref, pad_ref, freq_ref, gain_ref, *refs):
    if first:
        x_ref, wq_ref, wk_ref, wv_ref, out_ref, attn_in_ref, cos_ref, sin_ref, q_ref, k_ref, v_ref = refs
        row_len = x_ref.shape[0]
        prepare(
            docs, lengths_ref, freq_ref, lambda rows: x_ref[rows, :].astype(jnp.float32), gain_ref, attn_in_ref, cos_ref, sin_ref
        )
    else:
        attn_in_ref, cos_ref, sin_ref, wq_ref, wk_ref, wv_ref, out_ref, q_ref, k_ref, v_ref = refs
        row_len = attn_in_ref.shape[0]
    low_half, even = head_masks()
    group = wq_ref.shape[1]
    scale = 1.0 / math.sqrt(HEAD_DIM)
    for number in range(row_len // BLOCK):
        rows = pl.ds(number * BLOCK, BLOCK)
        block = attn_in_ref[rows, :]
        query = jnp.dot(block, wq_ref[...], preferred_element_type=jnp.float32)
        key = jnp.dot(block, wk_ref[...], preferred_element_type=jnp.float32)
        v_ref[rows, :] = jnp.dot(block, wv_ref[...], preferred_element_type=jnp.float32).astype(jnp.bfloat16)
        cosine, sine = cos_ref[rows, :], sin_ref[rows, :]
        for pair in range(group // LANES):
            cols = slice(pair * LANES, (pair + 1) * LANES)
            q_ref[rows, cols] = (turned(query[:, cols], cosine, sine, low_half) * scale).astype(jnp.bfloat16)
            k_ref[rows, cols] = turned(key[:, cols], cosine, sine, low_half).astype(jnp.bfloat16)
    ends = doc_ends(lengths_ref, docs)
    real = row_len - pad_ref[0]
    for number in range(row_len // BLOCK):
        rows = pl.ds(number * BLOCK, BLOCK)
        keys = (number + 1) * BLOCK
        query_index = number * BLOCK + lax.broadcasted_iota(jnp.int32, (BLOCK, 1), 0)
        start = first_key(query_index, ends, real)
        key_index = lax.broadcasted_iota(jnp.int32, (1, keys), 1)
        allowed = (key_index >= start) & (key_index <= query_index)
        for pair in range(group // LANES):
            cols = slice(pair * LANES, (pair + 1) * LANES)
            query = q_ref[rows, cols]
            key, value = k_ref[:keys, cols], v_ref[:keys, cols]
            results = []
            for chosen in (even, jnp.logical_not(even)):
                one = query * chosen.astype(jnp.bfloat16)
                scores = jnp.where(allowed, contract(one, key, 1, 1), -1e30)
                weights = jnp.exp(scores - jnp.max(scores, axis=-1, keepdims=True))
                total = jnp.sum(weights, axis=-1, keepdims=True)
                results.append(
                    jnp.dot(weights.astype(jnp.bfloat16), value, preferred_element_type=jnp.float32) / total
                )
            out_ref[rows, cols] = jnp.where(even, results[0], results[1]).astype(jnp.bfloat16).astype(jnp.float32)


def ready_kernel(
    docs, where_ref, lengths_ref, pad_ref, freq_ref, here_ref, there_ref, gain_ref, wq_ref, wk_ref, wv_ref,
    q_ref, k_ref, v_ref, log_ref, attn_in_ref, cos_ref, sin_ref,
):
    row_len = here_ref.shape[0]
    flag = where_ref[1]
    prepare(
        docs,
        lengths_ref,
        freq_ref,
        lambda rows: jnp.where(flag != 0, here_ref[rows, :].astype(jnp.float32), there_ref[rows, :]),
        gain_ref,
        attn_in_ref,
        cos_ref,
        sin_ref,
    )
    low_half, even = head_masks()
    group = wq_ref.shape[1]
    scale = 1.0 / math.sqrt(HEAD_DIM)
    for number in range(row_len // BLOCK):
        rows = pl.ds(number * BLOCK, BLOCK)
        block = attn_in_ref[rows, :]
        query = jnp.dot(block, wq_ref[...], preferred_element_type=jnp.float32)
        key = jnp.dot(block, wk_ref[...], preferred_element_type=jnp.float32)
        v_ref[rows, :] = jnp.dot(block, wv_ref[...], preferred_element_type=jnp.float32).astype(jnp.bfloat16)
        cosine, sine = cos_ref[rows, :], sin_ref[rows, :]
        for pair in range(group // LANES):
            cols = slice(pair * LANES, (pair + 1) * LANES)
            q_ref[rows, cols] = (turned(query[:, cols], cosine, sine, low_half) * scale).astype(jnp.bfloat16)
            k_ref[rows, cols] = turned(key[:, cols], cosine, sine, low_half).astype(jnp.bfloat16)
    ends = doc_ends(lengths_ref, docs)
    real = row_len - pad_ref[0]
    for number in range(row_len // BLOCK):
        rows = pl.ds(number * BLOCK, BLOCK)
        keys = (number + 1) * BLOCK
        query_index = number * BLOCK + lax.broadcasted_iota(jnp.int32, (1, BLOCK), 1)
        start = first_key(query_index, ends, real)
        key_index = lax.broadcasted_iota(jnp.int32, (keys, 1), 0)
        allowed = (key_index >= start) & (key_index <= query_index)
        for pair in range(group // LANES):
            cols = slice(pair * LANES, (pair + 1) * LANES)
            query, key = q_ref[rows, cols], k_ref[:keys, cols]
            for side, chosen in enumerate((even, jnp.logical_not(even))):
                one = query * chosen.astype(jnp.bfloat16)
                scores = jnp.where(allowed, contract(key, one, 1, 1), -1e30)
                highest = jnp.max(scores, axis=0, keepdims=True)
                total = jnp.sum(jnp.exp(scores - highest), axis=0, keepdims=True)
                head = pair * 2 + side
                log_ref[0, head : head + 1, rows] = highest + jnp.log(total)


def backward_kernel(
    docs, lengths_ref, pad_ref, cos_ref, sin_ref, q_ref, k_ref, v_ref, log_ref, grad_ref,
    gq_ref, gk_ref, gv_ref, key_sum, value_sum,
):
    row_len = q_ref.shape[0]
    low_half, even = head_masks()
    scale = 1.0 / math.sqrt(HEAD_DIM)
    ends = doc_ends(lengths_ref, docs)
    real = row_len - pad_ref[0]
    blocks = row_len // BLOCK
    for number in range(blocks - 1, -1, -1):
        rows = pl.ds(number * BLOCK, BLOCK)
        keys = (number + 1) * BLOCK
        query_index = number * BLOCK + lax.broadcasted_iota(jnp.int32, (1, BLOCK), 1)
        start = first_key(query_index, ends, real)
        key_index = lax.broadcasted_iota(jnp.int32, (keys, 1), 0)
        allowed = (key_index >= start) & (key_index <= query_index)
        query, grad = q_ref[rows, :], grad_ref[rows, :]
        key, value = k_ref[:keys, :], v_ref[:keys, :]
        parts = []
        for side, chosen in enumerate((even, jnp.logical_not(even))):
            mask = chosen.astype(jnp.bfloat16)
            one_query, one_grad = query * mask, grad * mask
            scores = jnp.where(allowed, contract(key, one_query, 1, 1), -1e30)
            weights = jnp.exp(scores - log_ref[0, side : side + 1, rows])
            soft = contract(value, one_grad, 1, 1)
            cross = jnp.sum(soft * weights, axis=0, keepdims=True)
            grad_scores = (weights * (soft - cross)).astype(jnp.bfloat16)
            low_weights = weights.astype(jnp.bfloat16)
            parts.append((
                contract(grad_scores, key, 0, 0),
                jnp.dot(grad_scores, one_query, preferred_element_type=jnp.float32),
                jnp.dot(low_weights, one_grad, preferred_element_type=jnp.float32),
            ))
        grad_query = jnp.where(even, parts[0][0], parts[1][0]) * scale
        gq_ref[rows, :] = turned(grad_query, cos_ref[rows, :], -sin_ref[rows, :], low_half).astype(jnp.bfloat16)
        if number == blocks - 1:
            key_sum[...] = parts[0][1] + parts[1][1]
            value_sum[...] = parts[0][2] + parts[1][2]
        else:
            key_sum[:keys, :] += parts[0][1] + parts[1][1]
            value_sum[:keys, :] += parts[0][2] + parts[1][2]
    for number in range(blocks):
        rows = pl.ds(number * BLOCK, BLOCK)
        gk_ref[rows, :] = turned(
            key_sum[rows, :], cos_ref[rows, :], -sin_ref[rows, :], low_half
        ).astype(jnp.bfloat16)
        gv_ref[rows, :] = value_sum[rows, :].astype(jnp.bfloat16)


def smem():
    return pl.BlockSpec(memory_space=pltpu.SMEM)


def whole(shape):
    return pl.BlockSpec(shape, lambda step: (0,) * len(shape))


def frequencies():
    half_dim = HEAD_DIM // 2
    return (10000.0 ** (-2.0 * np.arange(half_dim) / HEAD_DIM)).astype(np.float32)[:, None]


def attention_forward(number, sources, lengths, pad_count, gain, w_query, w_key, w_value):
    row_len, width = sources[0].shape
    first = number == 0
    group = w_query.shape[1] // 2
    weight = pl.BlockSpec((width, group), lambda step: (0, number))
    table = jax.ShapeDtypeStruct((row_len, LANES), jnp.float32)
    outs = [jax.ShapeDtypeStruct((row_len, group), jnp.float32)]
    if first:
        outs += [jax.ShapeDtypeStruct((row_len, width), jnp.bfloat16), table, table]
    return pl.pallas_call(
        partial(forward_kernel, lengths.shape[1], first),
        grid=(1,),
        in_specs=[
            smem(), smem(), whole((HEAD_DIM // 2, 1)), whole((1, width)),
            *(whole(source.shape) for source in sources), weight, weight, weight,
        ],
        out_specs=[whole(out.shape) for out in outs],
        out_shape=outs,
        scratch_shapes=[pltpu.VMEM((row_len, group), jnp.bfloat16)] * 3,
        compiler_params=pltpu.CompilerParams(vmem_limit_bytes=VMEM_LIMIT),
        cost_estimate=SMALL,
        name="attention_forward",
    )(lengths, pad_count, jnp.asarray(frequencies()), gain[None], *sources, w_query, w_key, w_value)


def attention_ready(where, block_in, there, lengths, pad_count, gain, weights):
    row_len, width = block_in.shape
    wide = weights.shape[1] // 3
    group = 2 * LANES
    heads = group // HEAD_DIM
    steps = wide // group
    weight = [pl.BlockSpec((width, group), lambda step, part=part: (0, part * steps + step)) for part in range(3)]
    part = pl.BlockSpec((row_len, group), lambda step: (0, step))
    table = jax.ShapeDtypeStruct((row_len, LANES), jnp.float32)
    rows = jax.ShapeDtypeStruct((row_len, wide), jnp.bfloat16)
    return pl.pallas_call(
        partial(ready_kernel, lengths.shape[1]),
        grid=(wide // group,),
        in_specs=[
            smem(), smem(), smem(), whole((HEAD_DIM // 2, 1)), whole((row_len, width)), whole((row_len, width)), whole((1, width)), *weight,
        ],
        out_specs=[
            part, part, part,
            pl.BlockSpec((1, heads, row_len), lambda step: (step, 0, 0)),
            whole((row_len, width)), whole((row_len, LANES)), whole((row_len, LANES)),
        ],
        out_shape=[
            rows, rows, rows,
            jax.ShapeDtypeStruct((wide // group, heads, row_len), jnp.float32),
            jax.ShapeDtypeStruct((row_len, width), jnp.bfloat16), table, table,
        ],
        compiler_params=pltpu.CompilerParams(vmem_limit_bytes=VMEM_LIMIT),
        cost_estimate=SMALL,
        name="attention_ready",
    )(where, lengths, pad_count, jnp.asarray(frequencies()), block_in, there, gain[None], weights, weights, weights)


def attention_backward(ready, lengths, pad_count, grad_heads):
    query, key, value, logs, _, cosine, sine = ready
    row_len, wide = query.shape
    pairs = wide // LANES
    logs = logs.reshape(pairs, LANES // HEAD_DIM, row_len)
    part = pl.BlockSpec((row_len, LANES), lambda step: (0, step))
    rows = jax.ShapeDtypeStruct((row_len, wide), jnp.bfloat16)
    return pl.pallas_call(
        partial(backward_kernel, lengths.shape[1]),
        grid=(pairs,),
        in_specs=[
            smem(), smem(), whole((row_len, LANES)), whole((row_len, LANES)), part, part, part,
            pl.BlockSpec((1, LANES // HEAD_DIM, row_len), lambda step: (step, 0, 0)), part,
        ],
        out_specs=[part, part, part],
        out_shape=[rows, rows, rows],
        scratch_shapes=[pltpu.VMEM((row_len, LANES), jnp.float32), pltpu.VMEM((row_len, LANES), jnp.float32)],
        compiler_params=pltpu.CompilerParams(vmem_limit_bytes=VMEM_LIMIT),
        cost_estimate=SMALL,
        name="attention_backward",
    )(lengths, pad_count, cosine, sine, query, key, value, logs, grad_heads)


FF_STEPS = 4
PARTS = 2
TILE = 256


def chosen_rows(flag, here_ref, there_ref):
    return jnp.where(flag != 0, here_ref[...].astype(jnp.float32), there_ref[...])


def norm_stats(values):
    average = jnp.mean(values, axis=-1, keepdims=True)
    centered = values - average
    inverse = lax.rsqrt(jnp.mean(centered * centered, axis=-1, keepdims=True) + 1e-05)
    return (centered * inverse, inverse)


def norm_pull(grad, gain, hat, inverse):
    scaled = grad * gain
    mean_scaled = jnp.mean(scaled, axis=-1, keepdims=True)
    mean_cross = jnp.mean(scaled * hat, axis=-1, keepdims=True)
    return inverse * (scaled - mean_scaled - hat * mean_cross)


def add_gain(ref, step, row, value):
    @pl.when(step == 0)
    def _():
        ref[row : row + 1, :] = value

    @pl.when(step != 0)
    def _():
        ref[row : row + 1, :] += value


def hidden_kernel(where_ref, low_ref, high_ref, w_out_ref, arrived_ref, here_ref, there_ref, gain_ref, hidden_ref, total_ref):
    group = low_ref.shape[1]
    total = jnp.dot(low_ref[...], w_out_ref[:group, :], preferred_element_type=jnp.float32) + arrived_ref[...]
    total += jnp.dot(high_ref[...], w_out_ref[group:, :], preferred_element_type=jnp.float32)
    total_ref[...] = total
    hat, _ = norm_stats(total)
    hidden_ref[...] = chosen_rows(where_ref[1], here_ref, there_ref) + hat * gain_ref[...]


def mlp_forward_kernel(hidden_ref, gain_ref, up_ref, down_ref, *refs):
    mlp_in_ref, act_ref, slope_ref, part_ref = refs[-4:]
    step = pl.program_id(0)

    @pl.when(step == 0)
    def _():
        hat, _ = norm_stats(hidden_ref[...])
        mlp_in_ref[...] = (hat * gain_ref[...]).astype(jnp.bfloat16)

    factor = math.sqrt(2.0 / math.pi)
    size = up_ref.shape[1] // PARTS
    part = None
    for number in range(PARTS):
        cols = slice(number * size, (number + 1) * size)
        pre = jnp.dot(mlp_in_ref[...], up_ref[:, cols], preferred_element_type=jnp.float32)
        squared = pre * pre
        bent = jnp.tanh(factor * pre * (1.0 + 0.044715 * squared))
        gate = 0.5 * (1.0 + bent)
        act = (pre * gate).astype(jnp.bfloat16)
        act_ref[:, cols] = act
        slope_ref[:, cols] = gate + 0.5 * pre * (1.0 - bent * bent) * (factor + (3.0 * 0.044715 * factor) * squared)
        piece = jnp.dot(act, down_ref[cols, :], preferred_element_type=jnp.float32)
        part = piece if part is None else part + piece

    @pl.when(step == 0)
    def _():
        part_ref[...] = part

    @pl.when(step != 0)
    def _():
        part_ref[...] += part


def mlp_backward_kernel(
    where_ref, hidden_ref, total_ref, here_ref, there_ref, gain_ref, down_ref, up_ref, slope_ref, *refs
):
    block_ref, low_ref, gain_sum_ref, grad_up_ref, part_ref = refs[-5:]
    step = pl.program_id(0)

    @pl.when(step == 0)
    def _():
        hat, inverse = norm_stats(total_ref[...])
        cot = chosen_rows(where_ref[1], here_ref, there_ref)
        block_ref[...] = hidden_ref[...] + hat * gain_ref[...]
        low_ref[...] = norm_pull(cot, gain_ref[...], hat, inverse).astype(jnp.bfloat16)
        gain_sum_ref[...] = jnp.broadcast_to(jnp.sum(cot * hat, axis=0, keepdims=True), gain_sum_ref.shape)

    size = up_ref.shape[1] // PARTS
    part = None
    for number in range(PARTS):
        cols = slice(number * size, (number + 1) * size)
        grad_act = contract(low_ref[...], down_ref[cols, :], 1, 1)
        grad_up = (grad_act * slope_ref[:, cols]).astype(jnp.bfloat16)
        grad_up_ref[:, cols] = grad_up
        piece = contract(grad_up, up_ref[:, cols], 1, 1)
        part = piece if part is None else part + piece

    @pl.when(step == 0)
    def _():
        part_ref[...] = part

    @pl.when(step != 0)
    def _():
        part_ref[...] += part


def residual_kernel(
    where_ref, part_ref, arrived_ref, hidden_ref, attn_ref, here_ref, there_ref, gain_mlp_ref, gain_attn_ref, *refs
):
    res_ref, attn_grad_ref, gains_ref = refs[-3:]
    step = pl.program_id(0)
    grad = part_ref[...] + arrived_ref[...]
    hat, inverse = norm_stats(hidden_ref[...])
    cot = chosen_rows(where_ref[1], here_ref, there_ref)
    res = cot + norm_pull(grad, gain_mlp_ref[...], hat, inverse)
    res_ref[...] = res
    add_gain(gains_ref, step, 0, jnp.sum(grad * hat, axis=0, keepdims=True))
    hat, inverse = norm_stats(attn_ref[...])
    attn_grad_ref[...] = norm_pull(res, gain_attn_ref[...], hat, inverse)
    add_gain(gains_ref, step, 1, jnp.sum(res * hat, axis=0, keepdims=True))


def other_kernel(where_ref, grad_ref, weight_ref, out_ref):
    piece = contract(grad_ref[...], weight_ref[...], 1, 1)

    @pl.when(pl.program_id(0) == 0)
    def _():
        out_ref[...] = piece

    @pl.when(pl.program_id(0) != 0)
    def _():
        out_ref[...] += piece


def input_kernel(
    where_ref, grad_ref, weight_ref, arrived_ref, here_ref, there_ref, res_ref, gain_ref, out_ref, gain_sum_ref, sum_ref
):
    step = pl.program_id(0)
    piece = contract(grad_ref[...], weight_ref[...], 1, 1)

    @pl.when(step == 0)
    def _():
        sum_ref[...] = piece + arrived_ref[...]

    @pl.when(step != 0)
    def _():
        sum_ref[...] += piece

    @pl.when(step == pl.num_programs(0) - 1)
    def _():
        grad = sum_ref[...]
        hat, inverse = norm_stats(chosen_rows(where_ref[1], here_ref, there_ref))
        out_ref[...] = res_ref[...] + norm_pull(grad, gain_ref[...], hat, inverse)
        gain_sum_ref[...] = jnp.broadcast_to(jnp.sum(grad * hat, axis=0, keepdims=True), gain_sum_ref.shape)


def pack_kernel(where_ref, x_ref, cot_ref, out_ref):
    step = pl.program_id(0)

    @pl.when(step < 2)
    def _():
        out_ref[...] = x_ref[...].astype(jnp.float32)

    @pl.when(step == 2)
    def _():
        out_ref[...] = cot_ref[...].astype(jnp.float32)


def call(kernel, name, steps, where, arrays, specs, outs, aliases, flops):
    moved = sum(array.size * array.dtype.itemsize for array in arrays)
    return pl.pallas_call(
        kernel,
        grid_spec=pltpu.PrefetchScalarGridSpec(
            num_scalar_prefetch=0 if where is None else 1,
            grid=(steps,),
            in_specs=specs,
            out_specs=[spec for _, spec in outs],
        ),
        out_shape=[shape for shape, _ in outs],
        input_output_aliases=aliases,
        compiler_params=pltpu.CompilerParams(vmem_limit_bytes=VMEM_LIMIT),
        cost_estimate=SMALL,
        name=name,
    )(*(() if where is None else (where,)), *arrays)


def rows_spec(rows, width, place):
    return pl.BlockSpec((rows, width), lambda step, *where: (place(step, *where), 0))


def fixed_spec(shape):
    return pl.BlockSpec(shape, lambda *args: (0,) * len(shape))


def hidden_chunk(where, number, attended, w_out, arrived, block_in, there, gain):
    row_len, group = attended[0].shape
    width = w_out.shape[1]
    rows = row_len // 4
    mine = rows_spec(rows, width, lambda step, where: where[0] * 2 + number)
    mine_attended = rows_spec(rows, group, lambda step, where: where[0] * 2 + number)
    shape = jax.ShapeDtypeStruct((rows, width), jnp.float32)
    return call(
        hidden_kernel, "hidden", 1, where,
        (*attended, w_out, arrived, block_in, there, gain[None]),
        [
            mine_attended, mine_attended, fixed_spec(w_out.shape),
            rows_spec(rows, width, lambda step, where: number), mine, mine, fixed_spec((1, width)),
        ],
        [(shape, fixed_spec((rows, width))), (shape, fixed_spec((rows, width)))],
        {}, 4 * rows * group * width,
    )


def mlp_forward(number, hidden, gain, w_up, w_down, buffers):
    rows, width = hidden.shape
    inner = w_up.shape[1]
    size = inner // FF_STEPS
    spare = [pl.BlockSpec(memory_space=pl.ANY)] * len(buffers)
    return call(
        mlp_forward_kernel, "mlp_forward", FF_STEPS, None,
        (hidden, gain[None], w_up, w_down, *buffers),
        [
            fixed_spec((rows, width)), fixed_spec((1, width)),
            pl.BlockSpec((width, size), lambda step: (0, step)),
            pl.BlockSpec((size, width), lambda step: (step, 0)),
            *spare,
        ],
        [
            (jax.ShapeDtypeStruct((4 * rows, width), jnp.bfloat16), pl.BlockSpec((rows, width), lambda step: (number, 0))),
            (jax.ShapeDtypeStruct((4 * rows, inner), jnp.bfloat16), pl.BlockSpec((rows, size), lambda step: (number, step))),
            (jax.ShapeDtypeStruct((rows, inner), jnp.float32), pl.BlockSpec((rows, size), lambda step: (0, step))),
            (jax.ShapeDtypeStruct((rows, width), jnp.float32), fixed_spec((rows, width))),
        ],
        {4 + index: index for index in range(len(buffers))}, 4 * rows * width * inner,
    )


def mlp_backward(where, number, hidden, total, cotangent, there, gain, w_down, w_up, slope, buffers):
    rows, width = hidden.shape
    inner = w_up.shape[1]
    size = inner // FF_STEPS
    part = number % 2
    spare = [pl.BlockSpec(memory_space=pl.ANY)] * len(buffers)
    return call(
        mlp_backward_kernel, "mlp_backward", FF_STEPS, where,
        (hidden, total, cotangent, there, gain[None], w_down, w_up, slope, *buffers),
        [
            fixed_spec((rows, width)), fixed_spec((rows, width)),
            rows_spec(rows, width, lambda step, where: where[0] * 2 + part),
            rows_spec(rows, width, lambda step, where: 4 + part),
            fixed_spec((1, width)),
            pl.BlockSpec((size, width), lambda step, where: (step, 0)),
            pl.BlockSpec((width, size), lambda step, where: (0, step)),
            pl.BlockSpec((rows, size), lambda step, where: (0, step)),
            *spare,
        ],
        [
            (jax.ShapeDtypeStruct((rows, width), jnp.float32), fixed_spec((rows, width))),
            (jax.ShapeDtypeStruct((4 * rows, width), jnp.bfloat16), pl.BlockSpec((rows, width), lambda step, where: (number, 0))),
            (jax.ShapeDtypeStruct((8, width), jnp.float32), fixed_spec((8, width))),
            (jax.ShapeDtypeStruct((4 * rows, inner), jnp.bfloat16), pl.BlockSpec((rows, size), lambda step, where: (number, step))),
            (jax.ShapeDtypeStruct((rows, width), jnp.float32), fixed_spec((rows, width))),
        ],
        {9 + index: 1 + 2 * index for index in range(len(buffers))}, 4 * rows * width * inner,
    )


def residual_chunk(where, number, part, arrived, hidden, attn_total, cotangent, there, gain_mlp, gain_attn, buffers):
    rows, width = part.shape
    steps = rows // TILE
    local = rows_spec(TILE, width, lambda step, where: step)
    spare = [pl.BlockSpec(memory_space=pl.ANY)] * len(buffers)
    whole_half = jax.ShapeDtypeStruct((2 * rows, width), jnp.float32)
    place = rows_spec(TILE, width, lambda step, where: number * steps + step)
    return call(
        residual_kernel, "residual", steps, where,
        (part, arrived, hidden, attn_total, cotangent, there, gain_mlp[None], gain_attn[None], *buffers),
        [
            local, local, local, local,
            rows_spec(TILE, width, lambda step, where: (where[0] * 2 + number) * steps + step),
            rows_spec(TILE, width, lambda step, where: (4 + number) * steps + step),
            fixed_spec((1, width)), fixed_spec((1, width)),
            *spare,
        ],
        [(whole_half, place), (whole_half, place), (jax.ShapeDtypeStruct((8, width), jnp.float32), fixed_spec((8, width)))],
        {9 + index: index for index in range(len(buffers))}, 20 * rows * width,
    )


def packed(where, block_in, cotangent):
    row_len, width = block_in.shape
    half = row_len // 2
    return call(
        pack_kernel, "packed", 3, where, (block_in, cotangent),
        [
            rows_spec(half, width, lambda step, where: jnp.minimum(step, 1)),
            rows_spec(half, width, lambda step, where: 1 - where[0]),
        ],
        [(jax.ShapeDtypeStruct((3 * half, width), jnp.float32), rows_spec(half, width, lambda step, where: step))],
        {}, 0,
    )[0]


def outer_kernel(where_ref, left_ref, right_ref, out_ref, turned_ref):
    @pl.when(pl.program_id(0) == 0)
    def _():
        turned_ref[...] = left_ref[...].T

    out_ref[...] = jnp.dot(turned_ref[...], right_ref[...], preferred_element_type=jnp.float32)


def outer(where, left, right, pick, columns):
    tokens, width = left.shape
    size = min(512, columns)
    steps = columns // size
    return pl.pallas_call(
        outer_kernel,
        grid_spec=pltpu.PrefetchScalarGridSpec(
            num_scalar_prefetch=1,
            grid=(steps,),
            in_specs=[
                fixed_spec((tokens, width)),
                pl.BlockSpec((tokens, size), lambda step, where: (0, pick(where) * steps + step)),
            ],
            out_specs=pl.BlockSpec((width, size), lambda step, where: (0, step)),
            scratch_shapes=[pltpu.VMEM((width, tokens), left.dtype)],
        ),
        out_shape=jax.ShapeDtypeStruct((width, columns), jnp.float32),
        compiler_params=pltpu.CompilerParams(vmem_limit_bytes=VMEM_LIMIT),
        cost_estimate=SMALL,
        name="outer",
    )(where, left, right)


def halves_kernel(count, sources, where_ref, *refs):
    stays, leaves = refs[:count], refs[count : 2 * count]
    outs = refs[-count - 1 : -1]
    leaving_ref = refs[-1]
    start = 0
    for stay_ref, leave_ref, out_ref, source in zip(stays, leaves, outs, sources):
        columns = stay_ref.shape[-1]
        stay, leave = stay_ref[0], leave_ref[0]
        if source is not None:
            number, first = source
            stay += refs[2 * count + 2 * number][0, :, first : first + columns]
            leave += refs[2 * count + 2 * number + 1][0, :, first : first + columns]
        out_ref[0] = stay
        leaving_ref[0, :, start : start + columns] = leave
        start += columns


def halves(where, step, held, arrived, sources):
    blocks, rows = held[0].shape[0] // 2, held[0].shape[1]
    widths = [part.shape[2] for part in held]

    def spec(width, stays):
        def place(index, where):
            low, bit = where[2 + 2 * step], where[3 + 2 * step]
            bit = bit if stays else 1 - bit
            high = lax.shift_right_logical(index, low)
            return (lax.shift_left(2 * high + bit, low) + index - lax.shift_left(high, low), 0, 0)

        return pl.BlockSpec((1, rows, width), place)

    arrays = list(held) * 2
    specs = [spec(width, stays) for stays in (True, False) for width in widths]
    for array in arrived:
        arrays += [array] * 2
        specs += [spec(array.shape[2], stays) for stays in (True, False)]
    outs = [*widths, sum(widths)]
    *staying, leaving = pl.pallas_call(
        partial(halves_kernel, len(held), sources),
        grid_spec=pltpu.PrefetchScalarGridSpec(
            num_scalar_prefetch=1,
            grid=(blocks,),
            in_specs=specs,
            out_specs=[pl.BlockSpec((1, rows, width), lambda index, where: (index, 0, 0)) for width in outs],
        ),
        out_shape=[jax.ShapeDtypeStruct((blocks, rows, width), jnp.float32) for width in outs],
        compiler_params=pltpu.CompilerParams(vmem_limit_bytes=VMEM_LIMIT),
        cost_estimate=SMALL,
        name="halves",
    )(where, *arrays)
    return staying, leaving


def input_specs(grads, weights, other):
    row_len, wide = grads.shape[0], grads.shape[1] // 3
    width = weights.shape[0]
    half = row_len // 2
    return [
        pl.BlockSpec((half, wide), lambda step, where: (1 - where[0] if other else where[0], step)),
        pl.BlockSpec((width, wide), lambda step, where: (0, step)),
    ], (half, width)


def input_other(where, grads, weights):
    specs, shape = input_specs(grads, weights, True)
    return call(
        other_kernel, "input_other", 3, where, (grads, weights), specs,
        [(jax.ShapeDtypeStruct(shape, jnp.float32), fixed_spec(shape))], {}, 2 * shape[0] * weights.size,
    )[0]


def input_own(where, grads, weights, arrived, block_in, there, res, gain):
    specs, shape = input_specs(grads, weights, False)
    mine = rows_spec(*shape, lambda step, where: where[0])
    moved = sum(array.size * array.dtype.itemsize for array in (grads, weights, arrived, block_in, there, res))
    return pl.pallas_call(
        input_kernel,
        grid_spec=pltpu.PrefetchScalarGridSpec(
            num_scalar_prefetch=1,
            grid=(3,),
            in_specs=specs + [fixed_spec(shape), mine, mine, fixed_spec(shape), fixed_spec((1, shape[1]))],
            out_specs=[fixed_spec(shape), fixed_spec((8, shape[1]))],
            scratch_shapes=[pltpu.VMEM(shape, jnp.float32)],
        ),
        out_shape=[jax.ShapeDtypeStruct(shape, jnp.float32), jax.ShapeDtypeStruct((8, shape[1]), jnp.float32)],
        compiler_params=pltpu.CompilerParams(vmem_limit_bytes=VMEM_LIMIT),
        cost_estimate=SMALL,
        name="input_own",
    )(where, grads, weights, arrived, block_in, there, res, gain[None])


def after(values, *others):
    return lax.optimization_barrier((values, others))[0]


def ordered(mine, other, bit, axis):
    low = jnp.where(bit == 0, mine, other)
    high = jnp.where(bit == 0, other, mine)
    return jnp.concatenate([low, high], axis=axis)


def body(
    dp_size,
    block_in,
    cotangent,
    lengths,
    pad_count,
    norm_in_attn,
    w_query,
    w_key,
    w_value,
    w_out,
    norm_out_attn,
    norm_in_mlp,
    w_up,
    w_down,
    norm_out_mlp,
):
    f32, bf16 = jnp.float32, jnp.bfloat16
    place = lax.axis_index("dp")
    core = lax.rem(place, 2)
    chip = lax.div(place, 2)
    side = lax.axis_index("tensor")
    same = core == side
    keep = same.astype(f32)
    first = (core == 0).astype(f32)
    chips = dp_size // 2
    levels = chips.bit_length() - 1
    bits = [lax.rem(lax.div(chip, 1 << level), 2) for level in range(levels)]
    swap = flat_pairs(dp_size, lambda d, c, t: (d ^ 1, 1 - t) if c != t else None)
    cross = flat_pairs(dp_size, lambda d, c, t: (d ^ 1, t))
    over = flat_pairs(dp_size, lambda d, c, t: (d, 1 - t))
    flips = [flat_pairs(dp_size, lambda d, c, t: (d ^ (2 << level), t)) for level in range(levels)]
    row_len, width = block_in.shape
    half = row_len // 2
    chunk = half // 2
    wide = w_query.shape[1]
    hidden = w_up.shape[1]

    shares = min(3, levels)
    near = flat_pairs(dp_size, lambda d, c, t: (d ^ 2, t) if c != t else None)

    orders = (list(range(levels)), [*range(1, levels), 0])
    hop_facts = []
    for step in range(levels):
        places = [sum(1 for later in order[step + 1 :] if later < order[step]) for order in orders]
        hop_facts.append(jnp.where(core == 0, places[0], places[1]))
        hop_facts.append(jnp.where(core == 0, bits[orders[0][step]], bits[orders[1][step]]))
    hops = [flat_pairs(dp_size, lambda d, c, t: (d ^ (2 << orders[c][step]), t)) for step in range(levels)]
    for bit in bits:
        hop_facts += [jnp.zeros_like(bit), bit]
    where_own = jnp.stack([core, same.astype(jnp.int32), *hop_facts])
    where_peer = jnp.stack([core, 1 - same.astype(jnp.int32)])
    out_rows = wide // 2
    weights_here = (w_query, w_key, w_value)
    part_rows = width >> shares
    which = sum(bits[level] << level for level in range(shares))
    parts_here = jnp.concatenate([half_of(weight, which, part_rows) for weight in weights_here], axis=1)
    w_out_sent = send(half_of(w_out, bits[0], out_rows).astype(f32), swap)
    attended_low, *sources = attention_forward(0, (block_in,), lengths, pad_count, norm_in_attn, w_query, w_key, w_value)
    low_sent = send(attended_low, swap)
    sources = after(sources, w_out_sent)
    w_out_sent = ordered(w_out_sent, send(w_out_sent, near), bits[0], 0)
    [attended_high] = attention_forward(1, sources, lengths, pad_count, norm_in_attn, w_query, w_key, w_value)
    high_sent = send(attended_high, swap)
    block_late, cot_late, facts = after((block_in, cotangent, jnp.pad(lengths, ((0, 0), (0, 1)))), low_sent, attended_high)
    facts = facts.astype(f32) + jnp.pad(pad_count.astype(f32)[:, None], ((0, 0), (lengths.shape[1], 0)))
    there = send(packed(where_own, block_late, cot_late), cross)
    facts_there = send(facts, cross)
    low_sent = after(low_sent, attended_high)
    attended = [(attended_low * keep + low_sent).astype(bf16), (attended_high * keep + high_sent).astype(bf16)]
    w_out_mine = (w_out.astype(f32) * keep + w_out_sent).astype(bf16)
    parts_sent = send(after(parts_here, attended[0]).astype(f32), swap)
    facts_row = jnp.where(same, facts, facts_there).astype(jnp.int32)
    docs = lengths.shape[1]
    lengths_row, pad_row = facts_row[:, :docs], facts_row[:, docs]
    part_other = sum(
        jnp.dot(half_of(values, 1 - core, half), w_out_mine[start : start + out_rows], preferred_element_type=f32)
        for values, start in zip(attended, (0, out_rows))
    )
    arrived = send(part_other, cross)
    hidden_own, attn_total, hidden_peer = [], [], []
    for number in range(2):
        one, total = hidden_chunk(where_own, number, attended, w_out_mine, arrived, block_in, there, norm_out_attn)
        hidden_own.append(one)
        attn_total.append(total)
        hidden_peer.append(send(one, over))

    gathered = 1 << shares
    groups = [
        [base + 2 * near_chip + one for near_chip in range(gathered)]
        for base in range(0, dp_size, 2 * gathered)
        for one in range(2)
    ]
    weights_sent = lax.all_gather(after(parts_sent, hidden_own[0]), "dp", axis=0, tiled=True, axis_index_groups=groups)

    buffers, slopes, parts, sums_own = (), [], [], []
    for number in range(4):
        piece = hidden_own[number] if number < 2 else hidden_peer[number - 2]
        if number > 1:
            piece = after(piece, parts[number - 1])
        *buffers, slope, part = mlp_forward(number, piece, norm_in_mlp, w_up, w_down, buffers)
        slopes.append(slope)
        parts.append(part)
        if number >= 2:
            sums_own.append(send(part, over))
    mlp_in_all, activated_all = buffers
    totals, blocks, back_parts, gain_out_mlp = [None] * 4, [None] * 4, [None] * 4, [None] * 4
    buffers = ()

    def add_up(number, gate):
        totals[number] = parts[number] + after(sums_own[number], gate)
        totals[number + 2] = send(totals[number], over)

    add_up(0, parts[3])
    gate = totals[0]
    for number in range(4):
        block, low_all, gain_sum, up_all, part = mlp_backward(
            where_own if number < 2 else where_peer,
            number,
            hidden_own[number] if number < 2 else hidden_peer[number - 2],
            after(totals[number], gate),
            cotangent,
            there,
            norm_out_mlp,
            w_down,
            w_up,
            slopes[number],
            buffers,
        )
        buffers = (low_all, up_all)
        blocks[number], back_parts[number], gain_out_mlp[number] = block, part, gain_sum[0]
        gate = part
        if number == 0:
            add_up(1, part)
            gate = totals[1]
    grad_low_all, grad_up_all = buffers
    sums_own = [send(part, over) for part in back_parts[2:]]

    def residual(number, arrived, buffers):
        return residual_chunk(
            where_own,
            number,
            back_parts[number],
            arrived,
            hidden_own[number],
            attn_total[number],
            cotangent,
            there,
            norm_in_mlp,
            norm_out_attn,
            buffers,
        )

    chip_rows = width // chips
    small = chip_rows // 2

    class Sum:
        def __init__(self, held, arrived, plain=False):
            self.plain = plain
            self.held = [part.reshape(chips, chip_rows, -1) for part in held]
            self.arrived = [] if arrived is None else [arrived.reshape(chips, chip_rows, -1)]
            self.sources = [None if arrived is None or number else (0, 0) for number in range(len(held))]
            self.step = 0

        def hop(self, *gates):
            arrived = [after(array, *gates) for array in self.arrived]
            self.held, leaving = halves(where_own, self.step + levels * self.plain, self.held, arrived, tuple(self.sources))
            self.arrived = [send(leaving, (flips if self.plain else hops)[self.step])]
            starts = np.cumsum([0, *(part.shape[2] for part in self.held)])
            self.sources = [(0, int(start)) for start in starts[:-1]]
            self.step += 1
            return leaving

        def result(self, *gates):
            while self.step < levels:
                gates = (self.hop(*gates),)
            arrived = [after(array, *gates) for array in self.arrived]
            return [
                (part + arrived[number][:, :, start : start + part.shape[2]]).reshape(chip_rows, -1)
                for part, (number, start) in zip(self.held, self.sources)
            ]

    def weight_part(columns):
        chosen = half_columns(activated_all, columns, hidden // 2)
        return jnp.einsum("td,tf->df", grad_low_all, chosen, preferred_element_type=f32)

    down_other = weight_part(1 - core)
    down_kept = weight_part(core)
    early = Sum([down_kept], send(down_other, cross))
    mlp_in_all, grad_up_all = after((mlp_in_all, grad_up_all), early.hop(down_kept))
    weight_up = jnp.einsum("td,tf->df", mlp_in_all, grad_up_all, preferred_element_type=f32)
    grad_up = lax.psum_scatter(weight_up, "dp", scatter_dimension=0, tiled=True)
    weights_late = after(weights_sent, weight_up)
    weights_mine = (jnp.concatenate(weights_here, axis=1).astype(f32) * keep + weights_late).astype(bf16)
    ready = attention_ready(where_own, block_in, there, lengths_row, pad_row, norm_in_attn, weights_mine)
    *buffers, gain_sum = residual(0, after(sums_own[0], ready[0]), ())
    gain_sums = [gain_sum]
    *buffers, gain_sum = residual(1, after(sums_own[1], gain_sum), buffers)
    gain_sums.append(gain_sum)
    grad_res, grad_attn = buffers
    gain_in_mlp = gain_sums[0][0] + gain_sums[1][0]
    gain_out_attn = gain_sums[0][1] + gain_sums[1][1]
    gain_out_mlp = gain_out_mlp[0] + gain_out_mlp[1]

    def to_output(values_own, values_peer):
        stay = jnp.where(same, values_own, values_peer)
        leave = jnp.where(same, values_peer, values_own)
        arrived = send(leave, cross)
        low = stay * first + arrived * (1.0 - first)
        high = arrived * first + stay * (1.0 - first)
        return jnp.concatenate([low, high], axis=0)

    grad_attn_other = send(grad_attn, cross)
    gate = early.hop(gain_sum)
    grad_attn_low = jnp.concatenate(
        [
            grad_attn * first + grad_attn_other * (1.0 - first),
            grad_attn_other * first + grad_attn * (1.0 - first),
        ],
        axis=0,
    ).astype(bf16)
    grad_heads = jnp.einsum("td,ed->te", grad_attn_low, w_out_mine, preferred_element_type=f32).astype(bf16)
    grads = attention_backward(ready, lengths_row, pad_row, after(grad_heads, gate))
    grads = jnp.concatenate(after(grads, early.hop(grads)), axis=1)
    late = Sum([jnp.einsum("td,te->de", ready[4], grads, preferred_element_type=f32)], None)
    gate = late.hop()
    other = input_other(where_own, after(grads, gate), weights_mine)
    other_sent = send(other, cross)
    attended_all = after(jnp.concatenate(attended, axis=1), other)
    weight_out = jnp.einsum("td,te->de", grad_attn_low, attended_all, preferred_element_type=f32)
    weight_out_sent = send(weight_out, swap)
    gate = weight_out
    grad_in_own, gain_in_attn = input_own(
        where_own, grads, weights_mine, after(other_sent, gate), block_in, there, grad_res, norm_in_attn
    )
    grad_in_sent = send(grad_in_own, over)
    gains = jnp.stack([gain_in_attn[0], gain_out_attn, gain_in_mlp, gain_out_mlp], axis=0)
    weight_out_sent, gains = after((weight_out_sent, gains), grad_up)
    gains = jnp.pad((gains + send(gains, cross)).T, ((0, 0), (0, LANES - 4)))
    weight_out = weight_out * keep + weight_out_sent
    out_sent = send(half_columns(weight_out, 1 - core, out_rows), cross)
    extra = Sum([half_columns(weight_out, core, out_rows), gains], out_sent, plain=True)
    gate = late.hop(weight_out)
    gate = extra.hop(gate)
    gate = extra.hop(gate)
    gate = late.hop(gate)
    gate = extra.hop(gate)
    [grad_down] = early.result(gate)
    [held] = late.result(gate)
    for_core = half_of(held, core, small)
    for_other = half_of(held, 1 - core, small)
    for_other, leaving = lax.optimization_barrier((for_other, jnp.where(same, for_other, for_core)))
    diagonal = send(for_other, swap)
    straight = send(
        leaving,
        flat_pairs(dp_size, lambda d, c, t: (d, 1 - t) if c != t else (d ^ 1, t)),
    )
    grad_out, gains = extra.result(leaving)

    def to_core(*parts):
        leaving = jnp.concatenate([half_of(part, 1 - core, small) for part in parts], axis=1)
        arrived, start, results = send(leaving, cross), 0, []
        for part in parts:
            columns = part.shape[1]
            results.append(ordered(half_of(part, core, small), arrived[:, start : start + columns], core, 1))
            start += columns
        return results

    def to_output(values_own, values_peer):
        stay = jnp.where(same, values_own, values_peer)
        leave = jnp.where(same, values_peer, values_own)
        arrived = send(leave, cross)
        low = stay * first + arrived * (1.0 - first)
        high = arrived * first + stay * (1.0 - first)
        return jnp.concatenate([low, high], axis=0)

    grad_down, grad_out = to_core(grad_down, grad_out)
    grad_in = to_output(grad_in_own, after(grad_in_sent, gate))
    heads = straight + jnp.where(same, for_core, diagonal)
    gains = half_of(gains, core, small)[:, :4].T
    gains = gains + send(gains, over)
    block_out = to_output(jnp.concatenate(blocks[:2], axis=0), jnp.concatenate(blocks[2:], axis=0)).astype(bf16)
    return (
        block_out,
        grad_in,
        gains[0],
        heads[:, :wide],
        heads[:, wide : 2 * wide],
        heads[:, 2 * wide : 3 * wide],
        grad_out.T,
        gains[1],
        gains[2],
        grad_up,
        grad_down.T,
        gains[3],
    )


def solution(mesh):
    placed = (
        P("dp", None),
        P("dp", None),
        P("dp", None),
        P("dp"),
        P(),
        P(None, "tensor"),
        P(None, "tensor"),
        P(None, "tensor"),
        P("tensor", None),
        P(),
        P(),
        P(None, "tensor"),
        P("tensor", None),
        P(),
    )
    return jax.shard_map(
        partial(body, mesh.shape["dp"]),
        mesh=mesh,
        in_specs=placed,
        out_specs=(
            P("dp", None),
            P("dp", None),
            P("dp"),
            P("dp", "tensor"),
            P("dp", "tensor"),
            P("dp", "tensor"),
            P("tensor", "dp"),
            P("dp"),
            P("dp"),
            P("dp", "tensor"),
            P("tensor", "dp"),
            P("dp"),
        ),
        check_vma=False,
    )
```

```python
from functools import partial
import math

import jax
import jax.numpy as jnp
from jax import lax
from jax.experimental import pallas as pl
from jax.experimental.pallas import tpu as pltpu
from jax.sharding import PartitionSpec as P
import numpy as np

HEAD_DIM = 64


def half_columns(values, which, size):
    return lax.dynamic_slice_in_dim(values, which * size, size, axis=1)


def flat_pairs(count, target):
    pairs = []
    for row in range(count):
        for side in range(2):
            goal = target(row, row % 2, side)
            if goal is not None:
                pairs.append((row * 2 + side, goal[0] * 2 + goal[1]))
    return pairs


def send(values, pairs):
    return lax.ppermute(values, ("dp", "tensor"), pairs)


def half_of(values, which, size):
    return lax.dynamic_slice_in_dim(values, which * size, size, axis=0)


BLOCK = 256
LANES = 128
VMEM_LIMIT = 56 * 1024 * 1024
SMALL = pl.CostEstimate(flops=1, bytes_accessed=1, transcendentals=0)


def doc_ends(lengths_ref, docs):
    ends = [lengths_ref[0, 0]]
    for number in range(1, docs):
        ends.append(ends[-1] + lengths_ref[0, number])
    return ends


def doc_start(index, ends):
    start = jnp.zeros_like(index)
    for end in ends:
        start = jnp.where(index >= end, end, start)
    return start


def first_key(index, ends, real):
    return jnp.where(index >= real, index, doc_start(index, ends))


def rope_tables(ends, row_len, freq_ref, cos_ref, sin_ref):
    index = lax.broadcasted_iota(jnp.int32, (1, row_len), 1)
    position = (index - doc_start(index, ends)).astype(jnp.float32)
    angles = freq_ref[...] * position
    cosine, sine = jnp.cos(angles), jnp.sin(angles)
    cos_ref[...] = jnp.concatenate([cosine] * 4, axis=0).T
    sin_ref[...] = jnp.concatenate([-sine, sine] * 2, axis=0).T


def turned(values, cosine, sine, low_half):
    ahead = pltpu.roll(values, LANES - HEAD_DIM // 2, 1)
    behind = pltpu.roll(values, HEAD_DIM // 2, 1)
    return values * cosine + jnp.where(low_half, ahead, behind) * sine


def normed(values):
    average = jnp.mean(values, axis=-1, keepdims=True)
    centered = values - average
    return centered * lax.rsqrt(jnp.mean(centered * centered, axis=-1, keepdims=True) + 1e-05)


def contract(left, right, left_dim, right_dim):
    return lax.dot_general(
        left, right, (((left_dim,), (right_dim,)), ((), ())), preferred_element_type=jnp.float32
    )


def prepare(docs, lengths_ref, freq_ref, rows_of, gain_ref, attn_in_ref, cos_ref, sin_ref):
    row_len = attn_in_ref.shape[0]

    @pl.when(pl.program_id(0) == 0)
    def _():
        rope_tables(doc_ends(lengths_ref, docs), row_len, freq_ref, cos_ref, sin_ref)
        for number in range(row_len // BLOCK):
            rows = pl.ds(number * BLOCK, BLOCK)
            attn_in_ref[rows, :] = (
                normed(rows_of(rows)) * gain_ref[...]
            ).astype(jnp.bfloat16)


def head_masks():
    lane = lax.broadcasted_iota(jnp.int32, (1, LANES), 1)
    return (lax.rem(lane, HEAD_DIM) < HEAD_DIM // 2, lane < HEAD_DIM)


def forward_kernel(docs, first, lengths_ref, pad_ref, freq_ref, gain_ref, *refs):
    if first:
        x_ref, wq_ref, wk_ref, wv_ref, out_ref, attn_in_ref, cos_ref, sin_ref, q_ref, k_ref, v_ref = refs
        row_len = x_ref.shape[0]
        prepare(
            docs, lengths_ref, freq_ref, lambda rows: x_ref[rows, :].astype(jnp.float32), gain_ref, attn_in_ref, cos_ref, sin_ref
        )
    else:
        attn_in_ref, cos_ref, sin_ref, wq_ref, wk_ref, wv_ref, out_ref, q_ref, k_ref, v_ref = refs
        row_len = attn_in_ref.shape[0]
    low_half, even = head_masks()
    group = wq_ref.shape[1]
    scale = 1.0 / math.sqrt(HEAD_DIM)
    for number in range(row_len // BLOCK):
        rows = pl.ds(number * BLOCK, BLOCK)
        block = attn_in_ref[rows, :]
        query = jnp.dot(block, wq_ref[...], preferred_element_type=jnp.float32)
        key = jnp.dot(block, wk_ref[...], preferred_element_type=jnp.float32)
        v_ref[rows, :] = jnp.dot(block, wv_ref[...], preferred_element_type=jnp.float32).astype(jnp.bfloat16)
        cosine, sine = cos_ref[rows, :], sin_ref[rows, :]
        for pair in range(group // LANES):
            cols = slice(pair * LANES, (pair + 1) * LANES)
            q_ref[rows, cols] = (turned(query[:, cols], cosine, sine, low_half) * scale).astype(jnp.bfloat16)
            k_ref[rows, cols] = turned(key[:, cols], cosine, sine, low_half).astype(jnp.bfloat16)
    ends = doc_ends(lengths_ref, docs)
    real = row_len - pad_ref[0]
    for number in range(row_len // BLOCK):
        rows = pl.ds(number * BLOCK, BLOCK)
        keys = (number + 1) * BLOCK
        query_index = number * BLOCK + lax.broadcasted_iota(jnp.int32, (BLOCK, 1), 0)
        start = first_key(query_index, ends, real)
        key_index = lax.broadcasted_iota(jnp.int32, (1, keys), 1)
        allowed = (key_index >= start) & (key_index <= query_index)
        for pair in range(group // LANES):
            cols = slice(pair * LANES, (pair + 1) * LANES)
            query = q_ref[rows, cols]
            key, value = k_ref[:keys, cols], v_ref[:keys, cols]
            results = []
            for chosen in (even, jnp.logical_not(even)):
                one = query * chosen.astype(jnp.bfloat16)
                scores = jnp.where(allowed, contract(one, key, 1, 1), -1e30)
                weights = jnp.exp(scores - jnp.max(scores, axis=-1, keepdims=True))
                total = jnp.sum(weights, axis=-1, keepdims=True)
                results.append(
                    jnp.dot(weights.astype(jnp.bfloat16), value, preferred_element_type=jnp.float32) / total
                )
            out_ref[rows, cols] = jnp.where(even, results[0], results[1]).astype(jnp.bfloat16).astype(jnp.float32)


def ready_kernel(
    docs, where_ref, lengths_ref, pad_ref, freq_ref, here_ref, there_ref, gain_ref, wq_ref, wk_ref, wv_ref,
    q_ref, k_ref, v_ref, log_ref, attn_in_ref, cos_ref, sin_ref,
):
    row_len = here_ref.shape[0]
    flag = where_ref[1]
    prepare(
        docs,
        lengths_ref,
        freq_ref,
        lambda rows: jnp.where(flag != 0, here_ref[rows, :].astype(jnp.float32), there_ref[rows, :]),
        gain_ref,
        attn_in_ref,
        cos_ref,
        sin_ref,
    )
    low_half, even = head_masks()
    group = wq_ref.shape[1]
    scale = 1.0 / math.sqrt(HEAD_DIM)
    for number in range(row_len // BLOCK):
        rows = pl.ds(number * BLOCK, BLOCK)
        block = attn_in_ref[rows, :]
        query = jnp.dot(block, wq_ref[...], preferred_element_type=jnp.float32)
        key = jnp.dot(block, wk_ref[...], preferred_element_type=jnp.float32)
        v_ref[rows, :] = jnp.dot(block, wv_ref[...], preferred_element_type=jnp.float32).astype(jnp.bfloat16)
        cosine, sine = cos_ref[rows, :], sin_ref[rows, :]
        for pair in range(group // LANES):
            cols = slice(pair * LANES, (pair + 1) * LANES)
            q_ref[rows, cols] = (turned(query[:, cols], cosine, sine, low_half) * scale).astype(jnp.bfloat16)
            k_ref[rows, cols] = turned(key[:, cols], cosine, sine, low_half).astype(jnp.bfloat16)
    ends = doc_ends(lengths_ref, docs)
    real = row_len - pad_ref[0]
    for number in range(row_len // BLOCK):
        rows = pl.ds(number * BLOCK, BLOCK)
        keys = (number + 1) * BLOCK
        query_index = number * BLOCK + lax.broadcasted_iota(jnp.int32, (1, BLOCK), 1)
        start = first_key(query_index, ends, real)
        key_index = lax.broadcasted_iota(jnp.int32, (keys, 1), 0)
        allowed = (key_index >= start) & (key_index <= query_index)
        for pair in range(group // LANES):
            cols = slice(pair * LANES, (pair + 1) * LANES)
            query, key = q_ref[rows, cols], k_ref[:keys, cols]
            for side, chosen in enumerate((even, jnp.logical_not(even))):
                one = query * chosen.astype(jnp.bfloat16)
                scores = jnp.where(allowed, contract(key, one, 1, 1), -1e30)
                highest = jnp.max(scores, axis=0, keepdims=True)
                total = jnp.sum(jnp.exp(scores - highest), axis=0, keepdims=True)
                head = pair * 2 + side
                log_ref[0, head : head + 1, rows] = highest + jnp.log(total)


def backward_kernel(
    docs, lengths_ref, pad_ref, cos_ref, sin_ref, q_ref, k_ref, v_ref, log_ref, grad_ref,
    gq_ref, gk_ref, gv_ref, key_sum, value_sum,
):
    row_len = q_ref.shape[0]
    low_half, even = head_masks()
    scale = 1.0 / math.sqrt(HEAD_DIM)
    ends = doc_ends(lengths_ref, docs)
    real = row_len - pad_ref[0]
    blocks = row_len // BLOCK
    for number in range(blocks - 1, -1, -1):
        rows = pl.ds(number * BLOCK, BLOCK)
        keys = (number + 1) * BLOCK
        query_index = number * BLOCK + lax.broadcasted_iota(jnp.int32, (1, BLOCK), 1)
        start = first_key(query_index, ends, real)
        key_index = lax.broadcasted_iota(jnp.int32, (keys, 1), 0)
        allowed = (key_index >= start) & (key_index <= query_index)
        query, grad = q_ref[rows, :], grad_ref[rows, :]
        key, value = k_ref[:keys, :], v_ref[:keys, :]
        parts = []
        for side, chosen in enumerate((even, jnp.logical_not(even))):
            mask = chosen.astype(jnp.bfloat16)
            one_query, one_grad = query * mask, grad * mask
            scores = jnp.where(allowed, contract(key, one_query, 1, 1), -1e30)
            weights = jnp.exp(scores - log_ref[0, side : side + 1, rows])
            soft = contract(value, one_grad, 1, 1)
            cross = jnp.sum(soft * weights, axis=0, keepdims=True)
            grad_scores = (weights * (soft - cross)).astype(jnp.bfloat16)
            low_weights = weights.astype(jnp.bfloat16)
            parts.append((
                contract(grad_scores, key, 0, 0),
                jnp.dot(grad_scores, one_query, preferred_element_type=jnp.float32),
                jnp.dot(low_weights, one_grad, preferred_element_type=jnp.float32),
            ))
        grad_query = jnp.where(even, parts[0][0], parts[1][0]) * scale
        gq_ref[rows, :] = turned(grad_query, cos_ref[rows, :], -sin_ref[rows, :], low_half).astype(jnp.bfloat16)
        if number == blocks - 1:
            key_sum[...] = parts[0][1] + parts[1][1]
            value_sum[...] = parts[0][2] + parts[1][2]
        else:
            key_sum[:keys, :] += parts[0][1] + parts[1][1]
            value_sum[:keys, :] += parts[0][2] + parts[1][2]
    for number in range(blocks):
        rows = pl.ds(number * BLOCK, BLOCK)
        gk_ref[rows, :] = turned(
            key_sum[rows, :], cos_ref[rows, :], -sin_ref[rows, :], low_half
        ).astype(jnp.bfloat16)
        gv_ref[rows, :] = value_sum[rows, :].astype(jnp.bfloat16)


def smem():
    return pl.BlockSpec(memory_space=pltpu.SMEM)


def whole(shape):
    return pl.BlockSpec(shape, lambda step: (0,) * len(shape))


def frequencies():
    half_dim = HEAD_DIM // 2
    return (10000.0 ** (-2.0 * np.arange(half_dim) / HEAD_DIM)).astype(np.float32)[:, None]


def attention_forward(number, sources, lengths, pad_count, gain, w_query, w_key, w_value):
    row_len, width = sources[0].shape
    first = number == 0
    group = w_query.shape[1] // 2
    weight = pl.BlockSpec((width, group), lambda step: (0, number))
    table = jax.ShapeDtypeStruct((row_len, LANES), jnp.float32)
    outs = [jax.ShapeDtypeStruct((row_len, group), jnp.float32)]
    if first:
        outs += [jax.ShapeDtypeStruct((row_len, width), jnp.bfloat16), table, table]
    return pl.pallas_call(
        partial(forward_kernel, lengths.shape[1], first),
        grid=(1,),
        in_specs=[
            smem(), smem(), whole((HEAD_DIM // 2, 1)), whole((1, width)),
            *(whole(source.shape) for source in sources), weight, weight, weight,
        ],
        out_specs=[whole(out.shape) for out in outs],
        out_shape=outs,
        scratch_shapes=[pltpu.VMEM((row_len, group), jnp.bfloat16)] * 3,
        compiler_params=pltpu.CompilerParams(vmem_limit_bytes=VMEM_LIMIT),
        cost_estimate=SMALL,
        name="attention_forward",
    )(lengths, pad_count, jnp.asarray(frequencies()), gain[None], *sources, w_query, w_key, w_value)


def attention_ready(where, block_in, there, lengths, pad_count, gain, weights):
    row_len, width = block_in.shape
    wide = weights.shape[1] // 3
    group = 2 * LANES
    heads = group // HEAD_DIM
    steps = wide // group
    weight = [pl.BlockSpec((width, group), lambda step, part=part: (0, part * steps + step)) for part in range(3)]
    part = pl.BlockSpec((row_len, group), lambda step: (0, step))
    table = jax.ShapeDtypeStruct((row_len, LANES), jnp.float32)
    rows = jax.ShapeDtypeStruct((row_len, wide), jnp.bfloat16)
    return pl.pallas_call(
        partial(ready_kernel, lengths.shape[1]),
        grid=(wide // group,),
        in_specs=[
            smem(), smem(), smem(), whole((HEAD_DIM // 2, 1)), whole((row_len, width)), whole((row_len, width)), whole((1, width)), *weight,
        ],
        out_specs=[
            part, part, part,
            pl.BlockSpec((1, heads, row_len), lambda step: (step, 0, 0)),
            whole((row_len, width)), whole((row_len, LANES)), whole((row_len, LANES)),
        ],
        out_shape=[
            rows, rows, rows,
            jax.ShapeDtypeStruct((wide // group, heads, row_len), jnp.float32),
            jax.ShapeDtypeStruct((row_len, width), jnp.bfloat16), table, table,
        ],
        compiler_params=pltpu.CompilerParams(vmem_limit_bytes=VMEM_LIMIT),
        cost_estimate=SMALL,
        name="attention_ready",
    )(where, lengths, pad_count, jnp.asarray(frequencies()), block_in, there, gain[None], weights, weights, weights)


def attention_backward(ready, lengths, pad_count, grad_heads):
    query, key, value, logs, _, cosine, sine = ready
    row_len, wide = query.shape
    pairs = wide // LANES
    logs = logs.reshape(pairs, LANES // HEAD_DIM, row_len)
    part = pl.BlockSpec((row_len, LANES), lambda step: (0, step))
    rows = jax.ShapeDtypeStruct((row_len, wide), jnp.bfloat16)
    return pl.pallas_call(
        partial(backward_kernel, lengths.shape[1]),
        grid=(pairs,),
        in_specs=[
            smem(), smem(), whole((row_len, LANES)), whole((row_len, LANES)), part, part, part,
            pl.BlockSpec((1, LANES // HEAD_DIM, row_len), lambda step: (step, 0, 0)), part,
        ],
        out_specs=[part, part, part],
        out_shape=[rows, rows, rows],
        scratch_shapes=[pltpu.VMEM((row_len, LANES), jnp.float32), pltpu.VMEM((row_len, LANES), jnp.float32)],
        compiler_params=pltpu.CompilerParams(vmem_limit_bytes=VMEM_LIMIT),
        cost_estimate=SMALL,
        name="attention_backward",
    )(lengths, pad_count, cosine, sine, query, key, value, logs, grad_heads)


FF_STEPS = 4
PARTS = 2
TILE = 256


def chosen_rows(flag, here_ref, there_ref):
    return jnp.where(flag != 0, here_ref[...].astype(jnp.float32), there_ref[...])


def norm_stats(values):
    average = jnp.mean(values, axis=-1, keepdims=True)
    centered = values - average
    inverse = lax.rsqrt(jnp.mean(centered * centered, axis=-1, keepdims=True) + 1e-05)
    return (centered * inverse, inverse)


def norm_pull(grad, gain, hat, inverse):
    scaled = grad * gain
    mean_scaled = jnp.mean(scaled, axis=-1, keepdims=True)
    mean_cross = jnp.mean(scaled * hat, axis=-1, keepdims=True)
    return inverse * (scaled - mean_scaled - hat * mean_cross)


def add_gain(ref, step, row, value):
    @pl.when(step == 0)
    def _():
        ref[row : row + 1, :] = value

    @pl.when(step != 0)
    def _():
        ref[row : row + 1, :] += value


def hidden_kernel(where_ref, low_ref, high_ref, w_out_ref, arrived_ref, here_ref, there_ref, gain_ref, hidden_ref, total_ref):
    group = low_ref.shape[1]
    total = jnp.dot(low_ref[...], w_out_ref[:group, :], preferred_element_type=jnp.float32) + arrived_ref[...]
    total += jnp.dot(high_ref[...], w_out_ref[group:, :], preferred_element_type=jnp.float32)
    total_ref[...] = total
    hat, _ = norm_stats(total)
    hidden_ref[...] = chosen_rows(where_ref[1], here_ref, there_ref) + hat * gain_ref[...]


def mlp_forward_kernel(hidden_ref, gain_ref, up_ref, down_ref, *refs):
    mlp_in_ref, act_ref, slope_ref, part_ref = refs[-4:]
    step = pl.program_id(0)

    @pl.when(step == 0)
    def _():
        hat, _ = norm_stats(hidden_ref[...])
        mlp_in_ref[...] = (hat * gain_ref[...]).astype(jnp.bfloat16)

    factor = math.sqrt(2.0 / math.pi)
    size = up_ref.shape[1] // PARTS
    part = None
    for number in range(PARTS):
        cols = slice(number * size, (number + 1) * size)
        pre = jnp.dot(mlp_in_ref[...], up_ref[:, cols], preferred_element_type=jnp.float32)
        squared = pre * pre
        bent = jnp.tanh(factor * pre * (1.0 + 0.044715 * squared))
        gate = 0.5 * (1.0 + bent)
        act = (pre * gate).astype(jnp.bfloat16)
        act_ref[:, cols] = act
        slope_ref[:, cols] = gate + 0.5 * pre * (1.0 - bent * bent) * (factor + (3.0 * 0.044715 * factor) * squared)
        piece = jnp.dot(act, down_ref[cols, :], preferred_element_type=jnp.float32)
        part = piece if part is None else part + piece

    @pl.when(step == 0)
    def _():
        part_ref[...] = part

    @pl.when(step != 0)
    def _():
        part_ref[...] += part


def mlp_backward_kernel(
    where_ref, hidden_ref, total_ref, here_ref, there_ref, gain_ref, down_ref, up_ref, slope_ref, *refs
):
    block_ref, low_ref, gain_sum_ref, grad_up_ref, part_ref = refs[-5:]
    step = pl.program_id(0)

    @pl.when(step == 0)
    def _():
        hat, inverse = norm_stats(total_ref[...])
        cot = chosen_rows(where_ref[1], here_ref, there_ref)
        block_ref[...] = hidden_ref[...] + hat * gain_ref[...]
        low_ref[...] = norm_pull(cot, gain_ref[...], hat, inverse).astype(jnp.bfloat16)
        gain_sum_ref[...] = jnp.broadcast_to(jnp.sum(cot * hat, axis=0, keepdims=True), gain_sum_ref.shape)

    size = up_ref.shape[1] // PARTS
    part = None
    for number in range(PARTS):
        cols = slice(number * size, (number + 1) * size)
        grad_act = contract(low_ref[...], down_ref[cols, :], 1, 1)
        grad_up = (grad_act * slope_ref[:, cols]).astype(jnp.bfloat16)
        grad_up_ref[:, cols] = grad_up
        piece = contract(grad_up, up_ref[:, cols], 1, 1)
        part = piece if part is None else part + piece

    @pl.when(step == 0)
    def _():
        part_ref[...] = part

    @pl.when(step != 0)
    def _():
        part_ref[...] += part


def residual_kernel(
    where_ref, part_ref, arrived_ref, hidden_ref, attn_ref, here_ref, there_ref, gain_mlp_ref, gain_attn_ref, *refs
):
    res_ref, attn_grad_ref, gains_ref = refs[-3:]
    step = pl.program_id(0)
    grad = part_ref[...] + arrived_ref[...]
    hat, inverse = norm_stats(hidden_ref[...])
    cot = chosen_rows(where_ref[1], here_ref, there_ref)
    res = cot + norm_pull(grad, gain_mlp_ref[...], hat, inverse)
    res_ref[...] = res
    add_gain(gains_ref, step, 0, jnp.sum(grad * hat, axis=0, keepdims=True))
    hat, inverse = norm_stats(attn_ref[...])
    attn_grad_ref[...] = norm_pull(res, gain_attn_ref[...], hat, inverse)
    add_gain(gains_ref, step, 1, jnp.sum(res * hat, axis=0, keepdims=True))


def other_kernel(where_ref, grad_ref, weight_ref, out_ref):
    piece = contract(grad_ref[...], weight_ref[...], 1, 1)

    @pl.when(pl.program_id(0) == 0)
    def _():
        out_ref[...] = piece

    @pl.when(pl.program_id(0) != 0)
    def _():
        out_ref[...] += piece


def input_kernel(
    where_ref, grad_ref, weight_ref, arrived_ref, here_ref, there_ref, res_ref, gain_ref, out_ref, gain_sum_ref, sum_ref
):
    step = pl.program_id(0)
    piece = contract(grad_ref[...], weight_ref[...], 1, 1)

    @pl.when(step == 0)
    def _():
        sum_ref[...] = piece + arrived_ref[...]

    @pl.when(step != 0)
    def _():
        sum_ref[...] += piece

    @pl.when(step == pl.num_programs(0) - 1)
    def _():
        grad = sum_ref[...]
        hat, inverse = norm_stats(chosen_rows(where_ref[1], here_ref, there_ref))
        out_ref[...] = res_ref[...] + norm_pull(grad, gain_ref[...], hat, inverse)
        gain_sum_ref[...] = jnp.broadcast_to(jnp.sum(grad * hat, axis=0, keepdims=True), gain_sum_ref.shape)


def pack_kernel(where_ref, x_ref, cot_ref, out_ref):
    step = pl.program_id(0)

    @pl.when(step < 2)
    def _():
        out_ref[...] = x_ref[...].astype(jnp.float32)

    @pl.when(step == 2)
    def _():
        out_ref[...] = cot_ref[...].astype(jnp.float32)


def call(kernel, name, steps, where, arrays, specs, outs, aliases, flops):
    moved = sum(array.size * array.dtype.itemsize for array in arrays)
    return pl.pallas_call(
        kernel,
        grid_spec=pltpu.PrefetchScalarGridSpec(
            num_scalar_prefetch=0 if where is None else 1,
            grid=(steps,),
            in_specs=specs,
            out_specs=[spec for _, spec in outs],
        ),
        out_shape=[shape for shape, _ in outs],
        input_output_aliases=aliases,
        compiler_params=pltpu.CompilerParams(vmem_limit_bytes=VMEM_LIMIT),
        cost_estimate=SMALL,
        name=name,
    )(*(() if where is None else (where,)), *arrays)


def rows_spec(rows, width, place):
    return pl.BlockSpec((rows, width), lambda step, *where: (place(step, *where), 0))


def fixed_spec(shape):
    return pl.BlockSpec(shape, lambda *args: (0,) * len(shape))


def hidden_chunk(where, number, attended, w_out, arrived, block_in, there, gain):
    row_len, group = attended[0].shape
    width = w_out.shape[1]
    rows = row_len // 4
    mine = rows_spec(rows, width, lambda step, where: where[0] * 2 + number)
    mine_attended = rows_spec(rows, group, lambda step, where: where[0] * 2 + number)
    shape = jax.ShapeDtypeStruct((rows, width), jnp.float32)
    return call(
        hidden_kernel, "hidden", 1, where,
        (*attended, w_out, arrived, block_in, there, gain[None]),
        [
            mine_attended, mine_attended, fixed_spec(w_out.shape),
            rows_spec(rows, width, lambda step, where: number), mine, mine, fixed_spec((1, width)),
        ],
        [(shape, fixed_spec((rows, width))), (shape, fixed_spec((rows, width)))],
        {}, 4 * rows * group * width,
    )


def mlp_forward(number, hidden, gain, w_up, w_down, buffers):
    rows, width = hidden.shape
    inner = w_up.shape[1]
    size = inner // FF_STEPS
    spare = [pl.BlockSpec(memory_space=pl.ANY)] * len(buffers)
    return call(
        mlp_forward_kernel, "mlp_forward", FF_STEPS, None,
        (hidden, gain[None], w_up, w_down, *buffers),
        [
            fixed_spec((rows, width)), fixed_spec((1, width)),
            pl.BlockSpec((width, size), lambda step: (0, step)),
            pl.BlockSpec((size, width), lambda step: (step, 0)),
            *spare,
        ],
        [
            (jax.ShapeDtypeStruct((4 * rows, width), jnp.bfloat16), pl.BlockSpec((rows, width), lambda step: (number, 0))),
            (jax.ShapeDtypeStruct((4 * rows, inner), jnp.bfloat16), pl.BlockSpec((rows, size), lambda step: (number, step))),
            (jax.ShapeDtypeStruct((rows, inner), jnp.float32), pl.BlockSpec((rows, size), lambda step: (0, step))),
            (jax.ShapeDtypeStruct((rows, width), jnp.float32), fixed_spec((rows, width))),
        ],
        {4 + index: index for index in range(len(buffers))}, 4 * rows * width * inner,
    )


def mlp_backward(where, number, hidden, total, cotangent, there, gain, w_down, w_up, slope, buffers):
    rows, width = hidden.shape
    inner = w_up.shape[1]
    size = inner // FF_STEPS
    part = number % 2
    spare = [pl.BlockSpec(memory_space=pl.ANY)] * len(buffers)
    return call(
        mlp_backward_kernel, "mlp_backward", FF_STEPS, where,
        (hidden, total, cotangent, there, gain[None], w_down, w_up, slope, *buffers),
        [
            fixed_spec((rows, width)), fixed_spec((rows, width)),
            rows_spec(rows, width, lambda step, where: where[0] * 2 + part),
            rows_spec(rows, width, lambda step, where: 4 + part),
            fixed_spec((1, width)),
            pl.BlockSpec((size, width), lambda step, where: (step, 0)),
            pl.BlockSpec((width, size), lambda step, where: (0, step)),
            pl.BlockSpec((rows, size), lambda step, where: (0, step)),
            *spare,
        ],
        [
            (jax.ShapeDtypeStruct((rows, width), jnp.float32), fixed_spec((rows, width))),
            (jax.ShapeDtypeStruct((4 * rows, width), jnp.bfloat16), pl.BlockSpec((rows, width), lambda step, where: (number, 0))),
            (jax.ShapeDtypeStruct((8, width), jnp.float32), fixed_spec((8, width))),
            (jax.ShapeDtypeStruct((4 * rows, inner), jnp.bfloat16), pl.BlockSpec((rows, size), lambda step, where: (number, step))),
            (jax.ShapeDtypeStruct((rows, width), jnp.float32), fixed_spec((rows, width))),
        ],
        {9 + index: 1 + 2 * index for index in range(len(buffers))}, 4 * rows * width * inner,
    )


def residual_chunk(where, number, part, arrived, hidden, attn_total, cotangent, there, gain_mlp, gain_attn, buffers):
    rows, width = part.shape
    steps = rows // TILE
    local = rows_spec(TILE, width, lambda step, where: step)
    spare = [pl.BlockSpec(memory_space=pl.ANY)] * len(buffers)
    whole_half = jax.ShapeDtypeStruct((2 * rows, width), jnp.float32)
    place = rows_spec(TILE, width, lambda step, where: number * steps + step)
    return call(
        residual_kernel, "residual", steps, where,
        (part, arrived, hidden, attn_total, cotangent, there, gain_mlp[None], gain_attn[None], *buffers),
        [
            local, local, local, local,
            rows_spec(TILE, width, lambda step, where: (where[0] * 2 + number) * steps + step),
            rows_spec(TILE, width, lambda step, where: (4 + number) * steps + step),
            fixed_spec((1, width)), fixed_spec((1, width)),
            *spare,
        ],
        [(whole_half, place), (whole_half, place), (jax.ShapeDtypeStruct((8, width), jnp.float32), fixed_spec((8, width)))],
        {9 + index: index for index in range(len(buffers))}, 20 * rows * width,
    )


def packed(where, block_in, cotangent):
    row_len, width = block_in.shape
    half = row_len // 2
    return call(
        pack_kernel, "packed", 3, where, (block_in, cotangent),
        [
            rows_spec(half, width, lambda step, where: jnp.minimum(step, 1)),
            rows_spec(half, width, lambda step, where: 1 - where[0]),
        ],
        [(jax.ShapeDtypeStruct((3 * half, width), jnp.float32), rows_spec(half, width, lambda step, where: step))],
        {}, 0,
    )[0]


def outer_kernel(where_ref, left_ref, right_ref, out_ref, turned_ref):
    @pl.when(pl.program_id(0) == 0)
    def _():
        turned_ref[...] = left_ref[...].T

    out_ref[...] = jnp.dot(turned_ref[...], right_ref[...], preferred_element_type=jnp.float32)


def outer(where, left, right, pick, columns):
    tokens, width = left.shape
    size = min(512, columns)
    steps = columns // size
    return pl.pallas_call(
        outer_kernel,
        grid_spec=pltpu.PrefetchScalarGridSpec(
            num_scalar_prefetch=1,
            grid=(steps,),
            in_specs=[
                fixed_spec((tokens, width)),
                pl.BlockSpec((tokens, size), lambda step, where: (0, pick(where) * steps + step)),
            ],
            out_specs=pl.BlockSpec((width, size), lambda step, where: (0, step)),
            scratch_shapes=[pltpu.VMEM((width, tokens), left.dtype)],
        ),
        out_shape=jax.ShapeDtypeStruct((width, columns), jnp.float32),
        compiler_params=pltpu.CompilerParams(vmem_limit_bytes=VMEM_LIMIT),
        cost_estimate=SMALL,
        name="outer",
    )(where, left, right)


def halves_kernel(count, sources, where_ref, *refs):
    stays, leaves = refs[:count], refs[count : 2 * count]
    outs = refs[-count - 1 : -1]
    leaving_ref = refs[-1]
    start = 0
    for stay_ref, leave_ref, out_ref, source in zip(stays, leaves, outs, sources):
        columns = stay_ref.shape[-1]
        stay, leave = stay_ref[0], leave_ref[0]
        if source is not None:
            number, first = source
            stay += refs[2 * count + 2 * number][0, :, first : first + columns]
            leave += refs[2 * count + 2 * number + 1][0, :, first : first + columns]
        out_ref[0] = stay
        leaving_ref[0, :, start : start + columns] = leave
        start += columns


def halves(where, step, held, arrived, sources):
    blocks, rows = held[0].shape[0] // 2, held[0].shape[1]
    widths = [part.shape[2] for part in held]

    def spec(width, stays):
        def place(index, where):
            low, bit = where[2 + 2 * step], where[3 + 2 * step]
            bit = bit if stays else 1 - bit
            high = lax.shift_right_logical(index, low)
            return (lax.shift_left(2 * high + bit, low) + index - lax.shift_left(high, low), 0, 0)

        return pl.BlockSpec((1, rows, width), place)

    arrays = list(held) * 2
    specs = [spec(width, stays) for stays in (True, False) for width in widths]
    for array in arrived:
        arrays += [array] * 2
        specs += [spec(array.shape[2], stays) for stays in (True, False)]
    outs = [*widths, sum(widths)]
    *staying, leaving = pl.pallas_call(
        partial(halves_kernel, len(held), sources),
        grid_spec=pltpu.PrefetchScalarGridSpec(
            num_scalar_prefetch=1,
            grid=(blocks,),
            in_specs=specs,
            out_specs=[pl.BlockSpec((1, rows, width), lambda index, where: (index, 0, 0)) for width in outs],
        ),
        out_shape=[jax.ShapeDtypeStruct((blocks, rows, width), jnp.float32) for width in outs],
        compiler_params=pltpu.CompilerParams(vmem_limit_bytes=VMEM_LIMIT),
        cost_estimate=SMALL,
        name="halves",
    )(where, *arrays)
    return staying, leaving


def input_specs(grads, weights, other):
    row_len, wide = grads.shape[0], grads.shape[1] // 3
    width = weights.shape[0]
    half = row_len // 2
    return [
        pl.BlockSpec((half, wide), lambda step, where: (1 - where[0] if other else where[0], step)),
        pl.BlockSpec((width, wide), lambda step, where: (0, step)),
    ], (half, width)


def input_other(where, grads, weights):
    specs, shape = input_specs(grads, weights, True)
    return call(
        other_kernel, "input_other", 3, where, (grads, weights), specs,
        [(jax.ShapeDtypeStruct(shape, jnp.float32), fixed_spec(shape))], {}, 2 * shape[0] * weights.size,
    )[0]


def input_own(where, grads, weights, arrived, block_in, there, res, gain):
    specs, shape = input_specs(grads, weights, False)
    mine = rows_spec(*shape, lambda step, where: where[0])
    moved = sum(array.size * array.dtype.itemsize for array in (grads, weights, arrived, block_in, there, res))
    return pl.pallas_call(
        input_kernel,
        grid_spec=pltpu.PrefetchScalarGridSpec(
            num_scalar_prefetch=1,
            grid=(3,),
            in_specs=specs + [fixed_spec(shape), mine, mine, fixed_spec(shape), fixed_spec((1, shape[1]))],
            out_specs=[fixed_spec(shape), fixed_spec((8, shape[1]))],
            scratch_shapes=[pltpu.VMEM(shape, jnp.float32)],
        ),
        out_shape=[jax.ShapeDtypeStruct(shape, jnp.float32), jax.ShapeDtypeStruct((8, shape[1]), jnp.float32)],
        compiler_params=pltpu.CompilerParams(vmem_limit_bytes=VMEM_LIMIT),
        cost_estimate=SMALL,
        name="input_own",
    )(where, grads, weights, arrived, block_in, there, res, gain[None])


def after(values, *others):
    return lax.optimization_barrier((values, others))[0]


def ordered(mine, other, bit, axis):
    low = jnp.where(bit == 0, mine, other)
    high = jnp.where(bit == 0, other, mine)
    return jnp.concatenate([low, high], axis=axis)


def body(
    dp_size,
    block_in,
    cotangent,
    lengths,
    pad_count,
    norm_in_attn,
    w_query,
    w_key,
    w_value,
    w_out,
    norm_out_attn,
    norm_in_mlp,
    w_up,
    w_down,
    norm_out_mlp,
):
    f32, bf16 = jnp.float32, jnp.bfloat16
    place = lax.axis_index("dp")
    core = lax.rem(place, 2)
    chip = lax.div(place, 2)
    side = lax.axis_index("tensor")
    same = core == side
    keep = same.astype(f32)
    first = (core == 0).astype(f32)
    chips = dp_size // 2
    levels = chips.bit_length() - 1
    bits = [lax.rem(lax.div(chip, 1 << level), 2) for level in range(levels)]
    swap = flat_pairs(dp_size, lambda d, c, t: (d ^ 1, 1 - t) if c != t else None)
    cross = flat_pairs(dp_size, lambda d, c, t: (d ^ 1, t))
    over = flat_pairs(dp_size, lambda d, c, t: (d, 1 - t))
    flips = [flat_pairs(dp_size, lambda d, c, t: (d ^ (2 << level), t)) for level in range(levels)]
    row_len, width = block_in.shape
    half = row_len // 2
    chunk = half // 2
    wide = w_query.shape[1]
    hidden = w_up.shape[1]

    shares = min(3, levels)
    near = flat_pairs(dp_size, lambda d, c, t: (d ^ 2, t) if c != t else None)

    orders = (list(range(levels)), [*range(1, levels), 0])
    hop_facts = []
    for step in range(levels):
        places = [sum(1 for later in order[step + 1 :] if later < order[step]) for order in orders]
        hop_facts.append(jnp.where(core == 0, places[0], places[1]))
        hop_facts.append(jnp.where(core == 0, bits[orders[0][step]], bits[orders[1][step]]))
    hops = [flat_pairs(dp_size, lambda d, c, t: (d ^ (2 << orders[c][step]), t)) for step in range(levels)]
    for bit in bits:
        hop_facts += [jnp.zeros_like(bit), bit]
    where_own = jnp.stack([core, same.astype(jnp.int32), *hop_facts])
    where_peer = jnp.stack([core, 1 - same.astype(jnp.int32)])
    out_rows = wide // 2
    weights_here = (w_query, w_key, w_value)
    part_rows = width >> shares
    which = sum(bits[level] << level for level in range(shares))
    parts_here = jnp.concatenate([half_of(weight, which, part_rows) for weight in weights_here], axis=1)
    w_out_sent = send(half_of(w_out, bits[0], out_rows).astype(f32), swap)
    attended_low, *sources = attention_forward(0, (block_in,), lengths, pad_count, norm_in_attn, w_query, w_key, w_value)
    low_sent = send(attended_low, swap)
    sources = after(sources, w_out_sent)
    w_out_sent = ordered(w_out_sent, send(w_out_sent, near), bits[0], 0)
    [attended_high] = attention_forward(1, sources, lengths, pad_count, norm_in_attn, w_query, w_key, w_value)
    high_sent = send(attended_high, swap)
    block_late, cot_late, facts = after((block_in, cotangent, jnp.pad(lengths, ((0, 0), (0, 1)))), low_sent, attended_high)
    facts = facts.astype(f32) + jnp.pad(pad_count.astype(f32)[:, None], ((0, 0), (lengths.shape[1], 0)))
    there = send(packed(where_own, block_late, cot_late), cross)
    facts_there = send(facts, cross)
    low_sent = after(low_sent, attended_high)
    attended = [(attended_low * keep + low_sent).astype(bf16), (attended_high * keep + high_sent).astype(bf16)]
    w_out_mine = (w_out.astype(f32) * keep + w_out_sent).astype(bf16)
    parts_sent = send(after(parts_here, attended[0]).astype(f32), swap)
    facts_row = jnp.where(same, facts, facts_there).astype(jnp.int32)
    docs = lengths.shape[1]
    lengths_row, pad_row = facts_row[:, :docs], facts_row[:, docs]
    part_other = sum(
        jnp.dot(half_of(values, 1 - core, half), w_out_mine[start : start + out_rows], preferred_element_type=f32)
        for values, start in zip(attended, (0, out_rows))
    )
    arrived = send(part_other, cross)
    hidden_own, attn_total, hidden_peer = [], [], []
    for number in range(2):
        one, total = hidden_chunk(where_own, number, attended, w_out_mine, arrived, block_in, there, norm_out_attn)
        hidden_own.append(one)
        attn_total.append(total)
        hidden_peer.append(send(one, over))

    gathered = 1 << shares
    groups = [
        [base + 2 * near_chip + one for near_chip in range(gathered)]
        for base in range(0, dp_size, 2 * gathered)
        for one in range(2)
    ]
    weights_sent = lax.all_gather(after(parts_sent, hidden_own[0]), "dp", axis=0, tiled=True, axis_index_groups=groups)

    buffers, slopes, parts, sums_own = (), [], [], []
    for number in range(4):
        piece = hidden_own[number] if number < 2 else hidden_peer[number - 2]
        if number > 1:
            piece = after(piece, parts[number - 1])
        *buffers, slope, part = mlp_forward(number, piece, norm_in_mlp, w_up, w_down, buffers)
        slopes.append(slope)
        parts.append(part)
        if number >= 2:
            sums_own.append(send(part, over))
    mlp_in_all, activated_all = buffers
    totals, blocks, back_parts, gain_out_mlp = [None] * 4, [None] * 4, [None] * 4, [None] * 4
    buffers = ()

    def add_up(number, gate):
        totals[number] = parts[number] + after(sums_own[number], gate)
        totals[number + 2] = send(totals[number], over)

    add_up(0, parts[3])
    gate = totals[0]
    for number in range(4):
        block, low_all, gain_sum, up_all, part = mlp_backward(
            where_own if number < 2 else where_peer,
            number,
            hidden_own[number] if number < 2 else hidden_peer[number - 2],
            after(totals[number], gate),
            cotangent,
            there,
            norm_out_mlp,
            w_down,
            w_up,
            slopes[number],
            buffers,
        )
        buffers = (low_all, up_all)
        blocks[number], back_parts[number], gain_out_mlp[number] = block, part, gain_sum[0]
        gate = part
        if number == 0:
            add_up(1, part)
            gate = totals[1]
    grad_low_all, grad_up_all = buffers
    sums_own = [send(part, over) for part in back_parts[2:]]

    def residual(number, arrived, buffers):
        return residual_chunk(
            where_own,
            number,
            back_parts[number],
            arrived,
            hidden_own[number],
            attn_total[number],
            cotangent,
            there,
            norm_in_mlp,
            norm_out_attn,
            buffers,
        )

    chip_rows = width // chips
    small = chip_rows // 2

    class Sum:
        def __init__(self, held, arrived, plain=False):
            self.plain = plain
            self.held = [part.reshape(chips, chip_rows, -1) for part in held]
            self.arrived = [] if arrived is None else [arrived.reshape(chips, chip_rows, -1)]
            self.sources = [None if arrived is None or number else (0, 0) for number in range(len(held))]
            self.step = 0

        def hop(self, *gates):
            arrived = [after(array, *gates) for array in self.arrived]
            self.held, leaving = halves(where_own, self.step + levels * self.plain, self.held, arrived, tuple(self.sources))
            self.arrived = [send(leaving, (flips if self.plain else hops)[self.step])]
            starts = np.cumsum([0, *(part.shape[2] for part in self.held)])
            self.sources = [(0, int(start)) for start in starts[:-1]]
            self.step += 1
            return leaving

        def result(self, *gates):
            while self.step < levels:
                gates = (self.hop(*gates),)
            arrived = [after(array, *gates) for array in self.arrived]
            return [
                (part + arrived[number][:, :, start : start + part.shape[2]]).reshape(chip_rows, -1)
                for part, (number, start) in zip(self.held, self.sources)
            ]

    def weight_part(columns):
        chosen = half_columns(activated_all, columns, hidden // 2)
        return jnp.einsum("td,tf->df", grad_low_all, chosen, preferred_element_type=f32)

    down_other = weight_part(1 - core)
    down_kept = weight_part(core)
    early = Sum([down_kept], send(down_other, cross))
    mlp_in_all, grad_up_all = after((mlp_in_all, grad_up_all), early.hop(down_kept))
    weight_up = jnp.einsum("td,tf->df", mlp_in_all, grad_up_all, preferred_element_type=f32)
    grad_up = lax.psum_scatter(weight_up, "dp", scatter_dimension=0, tiled=True)
    weights_late = after(weights_sent, weight_up)
    weights_mine = (jnp.concatenate(weights_here, axis=1).astype(f32) * keep + weights_late).astype(bf16)
    ready = attention_ready(where_own, block_in, there, lengths_row, pad_row, norm_in_attn, weights_mine)
    *buffers, gain_sum = residual(0, after(sums_own[0], ready[0]), ())
    gain_sums = [gain_sum]
    *buffers, gain_sum = residual(1, after(sums_own[1], gain_sum), buffers)
    gain_sums.append(gain_sum)
    grad_res, grad_attn = buffers
    gain_in_mlp = gain_sums[0][0] + gain_sums[1][0]
    gain_out_attn = gain_sums[0][1] + gain_sums[1][1]
    gain_out_mlp = gain_out_mlp[0] + gain_out_mlp[1]

    def to_output(values_own, values_peer):
        stay = jnp.where(same, values_own, values_peer)
        leave = jnp.where(same, values_peer, values_own)
        arrived = send(leave, cross)
        low = stay * first + arrived * (1.0 - first)
        high = arrived * first + stay * (1.0 - first)
        return jnp.concatenate([low, high], axis=0)

    grad_attn_other = send(grad_attn, cross)
    gate = early.hop(gain_sum)
    grad_attn_low = jnp.concatenate(
        [
            grad_attn * first + grad_attn_other * (1.0 - first),
            grad_attn_other * first + grad_attn * (1.0 - first),
        ],
        axis=0,
    ).astype(bf16)
    grad_heads = jnp.einsum("td,ed->te", grad_attn_low, w_out_mine, preferred_element_type=f32).astype(bf16)
    grads = attention_backward(ready, lengths_row, pad_row, after(grad_heads, gate))
    grads = jnp.concatenate(after(grads, early.hop(grads)), axis=1)
    late = Sum([jnp.einsum("td,te->de", ready[4], grads, preferred_element_type=f32)], None)
    gate = late.hop()
    other = input_other(where_own, after(grads, gate), weights_mine)
    other_sent = send(other, cross)
    attended_all = after(jnp.concatenate(attended, axis=1), other)
    weight_out = jnp.einsum("td,te->de", grad_attn_low, attended_all, preferred_element_type=f32)
    weight_out_sent = send(weight_out, swap)
    gate = weight_out
    grad_in_own, gain_in_attn = input_own(
        where_own, grads, weights_mine, after(other_sent, gate), block_in, there, grad_res, norm_in_attn
    )
    grad_in_sent = send(grad_in_own, over)
    gains = jnp.stack([gain_in_attn[0], gain_out_attn, gain_in_mlp, gain_out_mlp], axis=0)
    gate = late.hop(grad_in_own)
    weight_out_sent, gains = after((weight_out_sent, gains), grad_up, gate)
    gains = jnp.pad((gains + send(gains, cross)).T, ((0, 0), (0, LANES - 4)))
    weight_out = weight_out * keep + weight_out_sent
    out_sent = send(half_columns(weight_out, 1 - core, out_rows), cross)
    extra = Sum([half_columns(weight_out, core, out_rows), gains], out_sent, plain=True)
    gate = extra.hop(gate)
    gate = extra.hop(gate)
    gate = late.hop(gate)
    gate = extra.hop(gate)
    [grad_down] = early.result(gate)
    [held] = late.result(gate)
    for_core = half_of(held, core, small)
    for_other = half_of(held, 1 - core, small)
    for_other, leaving = lax.optimization_barrier((for_other, jnp.where(same, for_other, for_core)))
    diagonal = send(for_other, swap)
    straight = send(
        leaving,
        flat_pairs(dp_size, lambda d, c, t: (d, 1 - t) if c != t else (d ^ 1, t)),
    )
    grad_out, gains = extra.result(leaving)

    def to_core(*parts):
        leaving = jnp.concatenate([half_of(part, 1 - core, small) for part in parts], axis=1)
        arrived, start, results = send(leaving, cross), 0, []
        for part in parts:
            columns = part.shape[1]
            results.append(ordered(half_of(part, core, small), arrived[:, start : start + columns], core, 1))
            start += columns
        return results

    def to_output(values_own, values_peer):
        stay = jnp.where(same, values_own, values_peer)
        leave = jnp.where(same, values_peer, values_own)
        arrived = send(leave, cross)
        low = stay * first + arrived * (1.0 - first)
        high = arrived * first + stay * (1.0 - first)
        return jnp.concatenate([low, high], axis=0)

    grad_down, grad_out = to_core(grad_down, grad_out)
    grad_in = to_output(grad_in_own, after(grad_in_sent, gate))
    heads = straight + jnp.where(same, for_core, diagonal)
    gains = half_of(gains, core, small)[:, :4].T
    gains = gains + send(gains, over)
    block_out = to_output(jnp.concatenate(blocks[:2], axis=0), jnp.concatenate(blocks[2:], axis=0)).astype(bf16)
    return (
        block_out,
        grad_in,
        gains[0],
        heads[:, :wide],
        heads[:, wide : 2 * wide],
        heads[:, 2 * wide : 3 * wide],
        grad_out.T,
        gains[1],
        gains[2],
        grad_up,
        grad_down.T,
        gains[3],
    )


def solution(mesh):
    placed = (
        P("dp", None),
        P("dp", None),
        P("dp", None),
        P("dp"),
        P(),
        P(None, "tensor"),
        P(None, "tensor"),
        P(None, "tensor"),
        P("tensor", None),
        P(),
        P(),
        P(None, "tensor"),
        P("tensor", None),
        P(),
    )
    return jax.shard_map(
        partial(body, mesh.shape["dp"]),
        mesh=mesh,
        in_specs=placed,
        out_specs=(
            P("dp", None),
            P("dp", None),
            P("dp"),
            P("dp", "tensor"),
            P("dp", "tensor"),
            P("dp", "tensor"),
            P("tensor", "dp"),
            P("dp"),
            P("dp"),
            P("dp", "tensor"),
            P("tensor", "dp"),
            P("dp"),
        ),
        check_vma=False,
    )
```

```python
from functools import partial
import math

import jax
import jax.numpy as jnp
from jax import lax
from jax.experimental import pallas as pl
from jax.experimental.pallas import tpu as pltpu
from jax.sharding import PartitionSpec as P
import numpy as np

HEAD_DIM = 64


def half_columns(values, which, size):
    return lax.dynamic_slice_in_dim(values, which * size, size, axis=1)


def flat_pairs(count, target):
    pairs = []
    for row in range(count):
        for side in range(2):
            goal = target(row, row % 2, side)
            if goal is not None:
                pairs.append((row * 2 + side, goal[0] * 2 + goal[1]))
    return pairs


def send(values, pairs):
    return lax.ppermute(values, ("dp", "tensor"), pairs)


def half_of(values, which, size):
    return lax.dynamic_slice_in_dim(values, which * size, size, axis=0)


BLOCK = 256
LANES = 128
VMEM_LIMIT = 56 * 1024 * 1024
SMALL = pl.CostEstimate(flops=1, bytes_accessed=1, transcendentals=0)


def doc_ends(lengths_ref, docs):
    ends = [lengths_ref[0, 0]]
    for number in range(1, docs):
        ends.append(ends[-1] + lengths_ref[0, number])
    return ends


def doc_start(index, ends):
    start = jnp.zeros_like(index)
    for end in ends:
        start = jnp.where(index >= end, end, start)
    return start


def first_key(index, ends, real):
    return jnp.where(index >= real, index, doc_start(index, ends))


def rope_tables(ends, row_len, freq_ref, cos_ref, sin_ref):
    index = lax.broadcasted_iota(jnp.int32, (1, row_len), 1)
    position = (index - doc_start(index, ends)).astype(jnp.float32)
    angles = freq_ref[...] * position
    cosine, sine = jnp.cos(angles), jnp.sin(angles)
    cos_ref[...] = jnp.concatenate([cosine] * 4, axis=0).T
    sin_ref[...] = jnp.concatenate([-sine, sine] * 2, axis=0).T


def turned(values, cosine, sine, low_half):
    ahead = pltpu.roll(values, LANES - HEAD_DIM // 2, 1)
    behind = pltpu.roll(values, HEAD_DIM // 2, 1)
    return values * cosine + jnp.where(low_half, ahead, behind) * sine


def normed(values):
    average = jnp.mean(values, axis=-1, keepdims=True)
    centered = values - average
    return centered * lax.rsqrt(jnp.mean(centered * centered, axis=-1, keepdims=True) + 1e-05)


def contract(left, right, left_dim, right_dim):
    return lax.dot_general(
        left, right, (((left_dim,), (right_dim,)), ((), ())), preferred_element_type=jnp.float32
    )


def prepare(docs, lengths_ref, freq_ref, rows_of, gain_ref, attn_in_ref, cos_ref, sin_ref):
    row_len = attn_in_ref.shape[0]

    @pl.when(pl.program_id(0) == 0)
    def _():
        rope_tables(doc_ends(lengths_ref, docs), row_len, freq_ref, cos_ref, sin_ref)
        for number in range(row_len // BLOCK):
            rows = pl.ds(number * BLOCK, BLOCK)
            attn_in_ref[rows, :] = (
                normed(rows_of(rows)) * gain_ref[...]
            ).astype(jnp.bfloat16)


def head_masks():
    lane = lax.broadcasted_iota(jnp.int32, (1, LANES), 1)
    return (lax.rem(lane, HEAD_DIM) < HEAD_DIM // 2, lane < HEAD_DIM)


def forward_kernel(docs, first, lengths_ref, pad_ref, freq_ref, gain_ref, *refs):
    if first:
        x_ref, wq_ref, wk_ref, wv_ref, out_ref, attn_in_ref, cos_ref, sin_ref, q_ref, k_ref, v_ref = refs
        row_len = x_ref.shape[0]
        prepare(
            docs, lengths_ref, freq_ref, lambda rows: x_ref[rows, :].astype(jnp.float32), gain_ref, attn_in_ref, cos_ref, sin_ref
        )
    else:
        attn_in_ref, cos_ref, sin_ref, wq_ref, wk_ref, wv_ref, out_ref, q_ref, k_ref, v_ref = refs
        row_len = attn_in_ref.shape[0]
    low_half, even = head_masks()
    group = wq_ref.shape[1]
    scale = 1.0 / math.sqrt(HEAD_DIM)
    for number in range(row_len // BLOCK):
        rows = pl.ds(number * BLOCK, BLOCK)
        block = attn_in_ref[rows, :]
        query = jnp.dot(block, wq_ref[...], preferred_element_type=jnp.float32)
        key = jnp.dot(block, wk_ref[...], preferred_element_type=jnp.float32)
        v_ref[rows, :] = jnp.dot(block, wv_ref[...], preferred_element_type=jnp.float32).astype(jnp.bfloat16)
        cosine, sine = cos_ref[rows, :], sin_ref[rows, :]
        for pair in range(group // LANES):
            cols = slice(pair * LANES, (pair + 1) * LANES)
            q_ref[rows, cols] = (turned(query[:, cols], cosine, sine, low_half) * scale).astype(jnp.bfloat16)
            k_ref[rows, cols] = turned(key[:, cols], cosine, sine, low_half).astype(jnp.bfloat16)
    ends = doc_ends(lengths_ref, docs)
    real = row_len - pad_ref[0]
    for number in range(row_len // BLOCK):
        rows = pl.ds(number * BLOCK, BLOCK)
        keys = (number + 1) * BLOCK
        query_index = number * BLOCK + lax.broadcasted_iota(jnp.int32, (BLOCK, 1), 0)
        start = first_key(query_index, ends, real)
        key_index = lax.broadcasted_iota(jnp.int32, (1, keys), 1)
        allowed = (key_index >= start) & (key_index <= query_index)
        for pair in range(group // LANES):
            cols = slice(pair * LANES, (pair + 1) * LANES)
            query = q_ref[rows, cols]
            key, value = k_ref[:keys, cols], v_ref[:keys, cols]
            results = []
            for chosen in (even, jnp.logical_not(even)):
                one = query * chosen.astype(jnp.bfloat16)
                scores = jnp.where(allowed, contract(one, key, 1, 1), -1e30)
                weights = jnp.exp(scores - jnp.max(scores, axis=-1, keepdims=True))
                total = jnp.sum(weights, axis=-1, keepdims=True)
                results.append(
                    jnp.dot(weights.astype(jnp.bfloat16), value, preferred_element_type=jnp.float32) / total
                )
            out_ref[rows, cols] = jnp.where(even, results[0], results[1]).astype(jnp.bfloat16).astype(jnp.float32)


def ready_kernel(
    docs, where_ref, lengths_ref, pad_ref, freq_ref, here_ref, there_ref, gain_ref, wq_ref, wk_ref, wv_ref,
    q_ref, k_ref, v_ref, log_ref, attn_in_ref, cos_ref, sin_ref,
):
    row_len = here_ref.shape[0]
    flag = where_ref[1]
    prepare(
        docs,
        lengths_ref,
        freq_ref,
        lambda rows: jnp.where(flag != 0, here_ref[rows, :].astype(jnp.float32), there_ref[rows, :]),
        gain_ref,
        attn_in_ref,
        cos_ref,
        sin_ref,
    )
    low_half, even = head_masks()
    group = wq_ref.shape[1]
    scale = 1.0 / math.sqrt(HEAD_DIM)
    for number in range(row_len // BLOCK):
        rows = pl.ds(number * BLOCK, BLOCK)
        block = attn_in_ref[rows, :]
        query = jnp.dot(block, wq_ref[...], preferred_element_type=jnp.float32)
        key = jnp.dot(block, wk_ref[...], preferred_element_type=jnp.float32)
        v_ref[rows, :] = jnp.dot(block, wv_ref[...], preferred_element_type=jnp.float32).astype(jnp.bfloat16)
        cosine, sine = cos_ref[rows, :], sin_ref[rows, :]
        for pair in range(group // LANES):
            cols = slice(pair * LANES, (pair + 1) * LANES)
            q_ref[rows, cols] = (turned(query[:, cols], cosine, sine, low_half) * scale).astype(jnp.bfloat16)
            k_ref[rows, cols] = turned(key[:, cols], cosine, sine, low_half).astype(jnp.bfloat16)
    ends = doc_ends(lengths_ref, docs)
    real = row_len - pad_ref[0]
    for number in range(row_len // BLOCK):
        rows = pl.ds(number * BLOCK, BLOCK)
        keys = (number + 1) * BLOCK
        query_index = number * BLOCK + lax.broadcasted_iota(jnp.int32, (1, BLOCK), 1)
        start = first_key(query_index, ends, real)
        key_index = lax.broadcasted_iota(jnp.int32, (keys, 1), 0)
        allowed = (key_index >= start) & (key_index <= query_index)
        for pair in range(group // LANES):
            cols = slice(pair * LANES, (pair + 1) * LANES)
            query, key = q_ref[rows, cols], k_ref[:keys, cols]
            for side, chosen in enumerate((even, jnp.logical_not(even))):
                one = query * chosen.astype(jnp.bfloat16)
                scores = jnp.where(allowed, contract(key, one, 1, 1), -1e30)
                highest = jnp.max(scores, axis=0, keepdims=True)
                total = jnp.sum(jnp.exp(scores - highest), axis=0, keepdims=True)
                head = pair * 2 + side
                log_ref[0, head : head + 1, rows] = highest + jnp.log(total)


def backward_kernel(
    docs, lengths_ref, pad_ref, cos_ref, sin_ref, q_ref, k_ref, v_ref, log_ref, grad_ref,
    gq_ref, gk_ref, gv_ref, key_sum, value_sum,
):
    row_len = q_ref.shape[0]
    low_half, even = head_masks()
    scale = 1.0 / math.sqrt(HEAD_DIM)
    ends = doc_ends(lengths_ref, docs)
    real = row_len - pad_ref[0]
    blocks = row_len // BLOCK
    for number in range(blocks - 1, -1, -1):
        rows = pl.ds(number * BLOCK, BLOCK)
        keys = (number + 1) * BLOCK
        query_index = number * BLOCK + lax.broadcasted_iota(jnp.int32, (1, BLOCK), 1)
        start = first_key(query_index, ends, real)
        key_index = lax.broadcasted_iota(jnp.int32, (keys, 1), 0)
        allowed = (key_index >= start) & (key_index <= query_index)
        query, grad = q_ref[rows, :], grad_ref[rows, :]
        key, value = k_ref[:keys, :], v_ref[:keys, :]
        parts = []
        for side, chosen in enumerate((even, jnp.logical_not(even))):
            mask = chosen.astype(jnp.bfloat16)
            one_query, one_grad = query * mask, grad * mask
            scores = jnp.where(allowed, contract(key, one_query, 1, 1), -1e30)
            weights = jnp.exp(scores - log_ref[0, side : side + 1, rows])
            soft = contract(value, one_grad, 1, 1)
            cross = jnp.sum(soft * weights, axis=0, keepdims=True)
            grad_scores = (weights * (soft - cross)).astype(jnp.bfloat16)
            low_weights = weights.astype(jnp.bfloat16)
            parts.append((
                contract(grad_scores, key, 0, 0),
                jnp.dot(grad_scores, one_query, preferred_element_type=jnp.float32),
                jnp.dot(low_weights, one_grad, preferred_element_type=jnp.float32),
            ))
        grad_query = jnp.where(even, parts[0][0], parts[1][0]) * scale
        gq_ref[rows, :] = turned(grad_query, cos_ref[rows, :], -sin_ref[rows, :], low_half).astype(jnp.bfloat16)
        if number == blocks - 1:
            key_sum[...] = parts[0][1] + parts[1][1]
            value_sum[...] = parts[0][2] + parts[1][2]
        else:
            key_sum[:keys, :] += parts[0][1] + parts[1][1]
            value_sum[:keys, :] += parts[0][2] + parts[1][2]
    for number in range(blocks):
        rows = pl.ds(number * BLOCK, BLOCK)
        gk_ref[rows, :] = turned(
            key_sum[rows, :], cos_ref[rows, :], -sin_ref[rows, :], low_half
        ).astype(jnp.bfloat16)
        gv_ref[rows, :] = value_sum[rows, :].astype(jnp.bfloat16)


def smem():
    return pl.BlockSpec(memory_space=pltpu.SMEM)


def whole(shape):
    return pl.BlockSpec(shape, lambda step: (0,) * len(shape))


def frequencies():
    half_dim = HEAD_DIM // 2
    return (10000.0 ** (-2.0 * np.arange(half_dim) / HEAD_DIM)).astype(np.float32)[:, None]


def attention_forward(number, sources, lengths, pad_count, gain, w_query, w_key, w_value):
    row_len, width = sources[0].shape
    first = number == 0
    group = w_query.shape[1] // 2
    weight = pl.BlockSpec((width, group), lambda step: (0, number))
    table = jax.ShapeDtypeStruct((row_len, LANES), jnp.float32)
    outs = [jax.ShapeDtypeStruct((row_len, group), jnp.float32)]
    if first:
        outs += [jax.ShapeDtypeStruct((row_len, width), jnp.bfloat16), table, table]
    return pl.pallas_call(
        partial(forward_kernel, lengths.shape[1], first),
        grid=(1,),
        in_specs=[
            smem(), smem(), whole((HEAD_DIM // 2, 1)), whole((1, width)),
            *(whole(source.shape) for source in sources), weight, weight, weight,
        ],
        out_specs=[whole(out.shape) for out in outs],
        out_shape=outs,
        scratch_shapes=[pltpu.VMEM((row_len, group), jnp.bfloat16)] * 3,
        compiler_params=pltpu.CompilerParams(vmem_limit_bytes=VMEM_LIMIT),
        cost_estimate=SMALL,
        name="attention_forward",
    )(lengths, pad_count, jnp.asarray(frequencies()), gain[None], *sources, w_query, w_key, w_value)


def attention_ready(where, block_in, there, lengths, pad_count, gain, weights):
    row_len, width = block_in.shape
    wide = weights.shape[1] // 3
    group = 2 * LANES
    heads = group // HEAD_DIM
    steps = wide // group
    weight = [pl.BlockSpec((width, group), lambda step, part=part: (0, part * steps + step)) for part in range(3)]
    part = pl.BlockSpec((row_len, group), lambda step: (0, step))
    table = jax.ShapeDtypeStruct((row_len, LANES), jnp.float32)
    rows = jax.ShapeDtypeStruct((row_len, wide), jnp.bfloat16)
    return pl.pallas_call(
        partial(ready_kernel, lengths.shape[1]),
        grid=(wide // group,),
        in_specs=[
            smem(), smem(), smem(), whole((HEAD_DIM // 2, 1)), whole((row_len, width)), whole((row_len, width)), whole((1, width)), *weight,
        ],
        out_specs=[
            part, part, part,
            pl.BlockSpec((1, heads, row_len), lambda step: (step, 0, 0)),
            whole((row_len, width)), whole((row_len, LANES)), whole((row_len, LANES)),
        ],
        out_shape=[
            rows, rows, rows,
            jax.ShapeDtypeStruct((wide // group, heads, row_len), jnp.float32),
            jax.ShapeDtypeStruct((row_len, width), jnp.bfloat16), table, table,
        ],
        compiler_params=pltpu.CompilerParams(vmem_limit_bytes=VMEM_LIMIT),
        cost_estimate=SMALL,
        name="attention_ready",
    )(where, lengths, pad_count, jnp.asarray(frequencies()), block_in, there, gain[None], weights, weights, weights)


def attention_backward(ready, lengths, pad_count, grad_heads):
    query, key, value, logs, _, cosine, sine = ready
    row_len, wide = query.shape
    pairs = wide // LANES
    logs = logs.reshape(pairs, LANES // HEAD_DIM, row_len)
    part = pl.BlockSpec((row_len, LANES), lambda step: (0, step))
    rows = jax.ShapeDtypeStruct((row_len, wide), jnp.bfloat16)
    return pl.pallas_call(
        partial(backward_kernel, lengths.shape[1]),
        grid=(pairs,),
        in_specs=[
            smem(), smem(), whole((row_len, LANES)), whole((row_len, LANES)), part, part, part,
            pl.BlockSpec((1, LANES // HEAD_DIM, row_len), lambda step: (step, 0, 0)), part,
        ],
        out_specs=[part, part, part],
        out_shape=[rows, rows, rows],
        scratch_shapes=[pltpu.VMEM((row_len, LANES), jnp.float32), pltpu.VMEM((row_len, LANES), jnp.float32)],
        compiler_params=pltpu.CompilerParams(vmem_limit_bytes=VMEM_LIMIT),
        cost_estimate=SMALL,
        name="attention_backward",
    )(lengths, pad_count, cosine, sine, query, key, value, logs, grad_heads)


FF_STEPS = 4
PARTS = 2
TILE = 256


def chosen_rows(flag, here_ref, there_ref):
    return jnp.where(flag != 0, here_ref[...].astype(jnp.float32), there_ref[...])


def norm_stats(values):
    average = jnp.mean(values, axis=-1, keepdims=True)
    centered = values - average
    inverse = lax.rsqrt(jnp.mean(centered * centered, axis=-1, keepdims=True) + 1e-05)
    return (centered * inverse, inverse)


def norm_pull(grad, gain, hat, inverse):
    scaled = grad * gain
    mean_scaled = jnp.mean(scaled, axis=-1, keepdims=True)
    mean_cross = jnp.mean(scaled * hat, axis=-1, keepdims=True)
    return inverse * (scaled - mean_scaled - hat * mean_cross)


def add_gain(ref, step, row, value):
    @pl.when(step == 0)
    def _():
        ref[row : row + 1, :] = value

    @pl.when(step != 0)
    def _():
        ref[row : row + 1, :] += value


def hidden_kernel(where_ref, low_ref, high_ref, w_out_ref, arrived_ref, here_ref, there_ref, gain_ref, hidden_ref, total_ref):
    group = low_ref.shape[1]
    total = jnp.dot(low_ref[...], w_out_ref[:group, :], preferred_element_type=jnp.float32) + arrived_ref[...]
    total += jnp.dot(high_ref[...], w_out_ref[group:, :], preferred_element_type=jnp.float32)
    total_ref[...] = total
    hat, _ = norm_stats(total)
    hidden_ref[...] = chosen_rows(where_ref[1], here_ref, there_ref) + hat * gain_ref[...]


def mlp_forward_kernel(hidden_ref, gain_ref, up_ref, down_ref, *refs):
    mlp_in_ref, act_ref, slope_ref, part_ref = refs[-4:]
    step = pl.program_id(0)

    @pl.when(step == 0)
    def _():
        hat, _ = norm_stats(hidden_ref[...])
        mlp_in_ref[...] = (hat * gain_ref[...]).astype(jnp.bfloat16)

    factor = math.sqrt(2.0 / math.pi)
    size = up_ref.shape[1] // PARTS
    part = None
    for number in range(PARTS):
        cols = slice(number * size, (number + 1) * size)
        pre = jnp.dot(mlp_in_ref[...], up_ref[:, cols], preferred_element_type=jnp.float32)
        squared = pre * pre
        bent = jnp.tanh(factor * pre * (1.0 + 0.044715 * squared))
        gate = 0.5 * (1.0 + bent)
        act = (pre * gate).astype(jnp.bfloat16)
        act_ref[:, cols] = act
        slope_ref[:, cols] = gate + 0.5 * pre * (1.0 - bent * bent) * (factor + (3.0 * 0.044715 * factor) * squared)
        piece = jnp.dot(act, down_ref[cols, :], preferred_element_type=jnp.float32)
        part = piece if part is None else part + piece

    @pl.when(step == 0)
    def _():
        part_ref[...] = part

    @pl.when(step != 0)
    def _():
        part_ref[...] += part


def mlp_backward_kernel(
    where_ref, hidden_ref, total_ref, here_ref, there_ref, gain_ref, down_ref, up_ref, slope_ref, *refs
):
    block_ref, low_ref, gain_sum_ref, grad_up_ref, part_ref = refs[-5:]
    step = pl.program_id(0)

    @pl.when(step == 0)
    def _():
        hat, inverse = norm_stats(total_ref[...])
        cot = chosen_rows(where_ref[1], here_ref, there_ref)
        block_ref[...] = hidden_ref[...] + hat * gain_ref[...]
        low_ref[...] = norm_pull(cot, gain_ref[...], hat, inverse).astype(jnp.bfloat16)
        gain_sum_ref[...] = jnp.broadcast_to(jnp.sum(cot * hat, axis=0, keepdims=True), gain_sum_ref.shape)

    size = up_ref.shape[1] // PARTS
    part = None
    for number in range(PARTS):
        cols = slice(number * size, (number + 1) * size)
        grad_act = contract(low_ref[...], down_ref[cols, :], 1, 1)
        grad_up = (grad_act * slope_ref[:, cols]).astype(jnp.bfloat16)
        grad_up_ref[:, cols] = grad_up
        piece = contract(grad_up, up_ref[:, cols], 1, 1)
        part = piece if part is None else part + piece

    @pl.when(step == 0)
    def _():
        part_ref[...] = part

    @pl.when(step != 0)
    def _():
        part_ref[...] += part


def residual_kernel(
    where_ref, part_ref, arrived_ref, hidden_ref, attn_ref, here_ref, there_ref, gain_mlp_ref, gain_attn_ref, *refs
):
    res_ref, attn_grad_ref, gains_ref = refs[-3:]
    step = pl.program_id(0)
    grad = part_ref[...] + arrived_ref[...]
    hat, inverse = norm_stats(hidden_ref[...])
    cot = chosen_rows(where_ref[1], here_ref, there_ref)
    res = cot + norm_pull(grad, gain_mlp_ref[...], hat, inverse)
    res_ref[...] = res
    add_gain(gains_ref, step, 0, jnp.sum(grad * hat, axis=0, keepdims=True))
    hat, inverse = norm_stats(attn_ref[...])
    attn_grad_ref[...] = norm_pull(res, gain_attn_ref[...], hat, inverse)
    add_gain(gains_ref, step, 1, jnp.sum(res * hat, axis=0, keepdims=True))


def other_kernel(where_ref, grad_ref, weight_ref, out_ref):
    piece = contract(grad_ref[...], weight_ref[...], 1, 1)

    @pl.when(pl.program_id(0) == 0)
    def _():
        out_ref[...] = piece

    @pl.when(pl.program_id(0) != 0)
    def _():
        out_ref[...] += piece


def input_kernel(
    where_ref, grad_ref, weight_ref, arrived_ref, here_ref, there_ref, res_ref, gain_ref, out_ref, gain_sum_ref, sum_ref
):
    step = pl.program_id(0)
    piece = contract(grad_ref[...], weight_ref[...], 1, 1)

    @pl.when(step == 0)
    def _():
        sum_ref[...] = piece + arrived_ref[...]

    @pl.when(step != 0)
    def _():
        sum_ref[...] += piece

    @pl.when(step == pl.num_programs(0) - 1)
    def _():
        grad = sum_ref[...]
        hat, inverse = norm_stats(chosen_rows(where_ref[1], here_ref, there_ref))
        out_ref[...] = res_ref[...] + norm_pull(grad, gain_ref[...], hat, inverse)
        gain_sum_ref[...] = jnp.broadcast_to(jnp.sum(grad * hat, axis=0, keepdims=True), gain_sum_ref.shape)


def pack_kernel(where_ref, x_ref, cot_ref, out_ref):
    step = pl.program_id(0)

    @pl.when(step < 2)
    def _():
        out_ref[...] = x_ref[...].astype(jnp.float32)

    @pl.when(step == 2)
    def _():
        out_ref[...] = cot_ref[...].astype(jnp.float32)


def call(kernel, name, steps, where, arrays, specs, outs, aliases, flops):
    moved = sum(array.size * array.dtype.itemsize for array in arrays)
    return pl.pallas_call(
        kernel,
        grid_spec=pltpu.PrefetchScalarGridSpec(
            num_scalar_prefetch=0 if where is None else 1,
            grid=(steps,),
            in_specs=specs,
            out_specs=[spec for _, spec in outs],
        ),
        out_shape=[shape for shape, _ in outs],
        input_output_aliases=aliases,
        compiler_params=pltpu.CompilerParams(vmem_limit_bytes=VMEM_LIMIT),
        cost_estimate=SMALL,
        name=name,
    )(*(() if where is None else (where,)), *arrays)


def rows_spec(rows, width, place):
    return pl.BlockSpec((rows, width), lambda step, *where: (place(step, *where), 0))


def fixed_spec(shape):
    return pl.BlockSpec(shape, lambda *args: (0,) * len(shape))


def hidden_chunk(where, number, attended, w_out, arrived, block_in, there, gain):
    row_len, group = attended[0].shape
    width = w_out.shape[1]
    rows = row_len // 4
    mine = rows_spec(rows, width, lambda step, where: where[0] * 2 + number)
    mine_attended = rows_spec(rows, group, lambda step, where: where[0] * 2 + number)
    shape = jax.ShapeDtypeStruct((rows, width), jnp.float32)
    return call(
        hidden_kernel, "hidden", 1, where,
        (*attended, w_out, arrived, block_in, there, gain[None]),
        [
            mine_attended, mine_attended, fixed_spec(w_out.shape),
            rows_spec(rows, width, lambda step, where: number), mine, mine, fixed_spec((1, width)),
        ],
        [(shape, fixed_spec((rows, width))), (shape, fixed_spec((rows, width)))],
        {}, 4 * rows * group * width,
    )


def mlp_forward(number, hidden, gain, w_up, w_down, buffers):
    rows, width = hidden.shape
    inner = w_up.shape[1]
    size = inner // FF_STEPS
    spare = [pl.BlockSpec(memory_space=pl.ANY)] * len(buffers)
    return call(
        mlp_forward_kernel, "mlp_forward", FF_STEPS, None,
        (hidden, gain[None], w_up, w_down, *buffers),
        [
            fixed_spec((rows, width)), fixed_spec((1, width)),
            pl.BlockSpec((width, size), lambda step: (0, step)),
            pl.BlockSpec((size, width), lambda step: (step, 0)),
            *spare,
        ],
        [
            (jax.ShapeDtypeStruct((4 * rows, width), jnp.bfloat16), pl.BlockSpec((rows, width), lambda step: (number, 0))),
            (jax.ShapeDtypeStruct((4 * rows, inner), jnp.bfloat16), pl.BlockSpec((rows, size), lambda step: (number, step))),
            (jax.ShapeDtypeStruct((rows, inner), jnp.float32), pl.BlockSpec((rows, size), lambda step: (0, step))),
            (jax.ShapeDtypeStruct((rows, width), jnp.float32), fixed_spec((rows, width))),
        ],
        {4 + index: index for index in range(len(buffers))}, 4 * rows * width * inner,
    )


def mlp_backward(where, number, hidden, total, cotangent, there, gain, w_down, w_up, slope, buffers):
    rows, width = hidden.shape
    inner = w_up.shape[1]
    size = inner // FF_STEPS
    part = number % 2
    spare = [pl.BlockSpec(memory_space=pl.ANY)] * len(buffers)
    return call(
        mlp_backward_kernel, "mlp_backward", FF_STEPS, where,
        (hidden, total, cotangent, there, gain[None], w_down, w_up, slope, *buffers),
        [
            fixed_spec((rows, width)), fixed_spec((rows, width)),
            rows_spec(rows, width, lambda step, where: where[0] * 2 + part),
            rows_spec(rows, width, lambda step, where: 4 + part),
            fixed_spec((1, width)),
            pl.BlockSpec((size, width), lambda step, where: (step, 0)),
            pl.BlockSpec((width, size), lambda step, where: (0, step)),
            pl.BlockSpec((rows, size), lambda step, where: (0, step)),
            *spare,
        ],
        [
            (jax.ShapeDtypeStruct((rows, width), jnp.float32), fixed_spec((rows, width))),
            (jax.ShapeDtypeStruct((4 * rows, width), jnp.bfloat16), pl.BlockSpec((rows, width), lambda step, where: (number, 0))),
            (jax.ShapeDtypeStruct((8, width), jnp.float32), fixed_spec((8, width))),
            (jax.ShapeDtypeStruct((4 * rows, inner), jnp.bfloat16), pl.BlockSpec((rows, size), lambda step, where: (number, step))),
            (jax.ShapeDtypeStruct((rows, width), jnp.float32), fixed_spec((rows, width))),
        ],
        {9 + index: 1 + 2 * index for index in range(len(buffers))}, 4 * rows * width * inner,
    )


def residual_chunk(where, number, part, arrived, hidden, attn_total, cotangent, there, gain_mlp, gain_attn, buffers):
    rows, width = part.shape
    steps = rows // TILE
    local = rows_spec(TILE, width, lambda step, where: step)
    spare = [pl.BlockSpec(memory_space=pl.ANY)] * len(buffers)
    whole_half = jax.ShapeDtypeStruct((2 * rows, width), jnp.float32)
    place = rows_spec(TILE, width, lambda step, where: number * steps + step)
    return call(
        residual_kernel, "residual", steps, where,
        (part, arrived, hidden, attn_total, cotangent, there, gain_mlp[None], gain_attn[None], *buffers),
        [
            local, local, local, local,
            rows_spec(TILE, width, lambda step, where: (where[0] * 2 + number) * steps + step),
            rows_spec(TILE, width, lambda step, where: (4 + number) * steps + step),
            fixed_spec((1, width)), fixed_spec((1, width)),
            *spare,
        ],
        [(whole_half, place), (whole_half, place), (jax.ShapeDtypeStruct((8, width), jnp.float32), fixed_spec((8, width)))],
        {9 + index: index for index in range(len(buffers))}, 20 * rows * width,
    )


def packed(where, block_in, cotangent):
    row_len, width = block_in.shape
    half = row_len // 2
    return call(
        pack_kernel, "packed", 3, where, (block_in, cotangent),
        [
            rows_spec(half, width, lambda step, where: jnp.minimum(step, 1)),
            rows_spec(half, width, lambda step, where: 1 - where[0]),
        ],
        [(jax.ShapeDtypeStruct((3 * half, width), jnp.float32), rows_spec(half, width, lambda step, where: step))],
        {}, 0,
    )[0]


def outer_kernel(where_ref, left_ref, right_ref, out_ref, turned_ref):
    @pl.when(pl.program_id(0) == 0)
    def _():
        turned_ref[...] = left_ref[...].T

    out_ref[...] = jnp.dot(turned_ref[...], right_ref[...], preferred_element_type=jnp.float32)


def outer(where, left, right, pick, columns):
    tokens, width = left.shape
    size = min(512, columns)
    steps = columns // size
    return pl.pallas_call(
        outer_kernel,
        grid_spec=pltpu.PrefetchScalarGridSpec(
            num_scalar_prefetch=1,
            grid=(steps,),
            in_specs=[
                fixed_spec((tokens, width)),
                pl.BlockSpec((tokens, size), lambda step, where: (0, pick(where) * steps + step)),
            ],
            out_specs=pl.BlockSpec((width, size), lambda step, where: (0, step)),
            scratch_shapes=[pltpu.VMEM((width, tokens), left.dtype)],
        ),
        out_shape=jax.ShapeDtypeStruct((width, columns), jnp.float32),
        compiler_params=pltpu.CompilerParams(vmem_limit_bytes=VMEM_LIMIT),
        cost_estimate=SMALL,
        name="outer",
    )(where, left, right)


def halves_kernel(count, sources, where_ref, *refs):
    stays, leaves = refs[:count], refs[count : 2 * count]
    outs = refs[-count - 1 : -1]
    leaving_ref = refs[-1]
    start = 0
    for stay_ref, leave_ref, out_ref, source in zip(stays, leaves, outs, sources):
        columns = stay_ref.shape[-1]
        stay, leave = stay_ref[0], leave_ref[0]
        if source is not None:
            number, first = source
            stay += refs[2 * count + 2 * number][0, :, first : first + columns]
            leave += refs[2 * count + 2 * number + 1][0, :, first : first + columns]
        out_ref[0] = stay
        leaving_ref[0, :, start : start + columns] = leave
        start += columns


def halves(where, step, held, arrived, sources):
    blocks, rows = held[0].shape[0] // 2, held[0].shape[1]
    widths = [part.shape[2] for part in held]

    def spec(width, stays):
        def place(index, where):
            low, bit = where[2 + 2 * step], where[3 + 2 * step]
            bit = bit if stays else 1 - bit
            high = lax.shift_right_logical(index, low)
            return (lax.shift_left(2 * high + bit, low) + index - lax.shift_left(high, low), 0, 0)

        return pl.BlockSpec((1, rows, width), place)

    arrays = list(held) * 2
    specs = [spec(width, stays) for stays in (True, False) for width in widths]
    for array in arrived:
        arrays += [array] * 2
        specs += [spec(array.shape[2], stays) for stays in (True, False)]
    outs = [*widths, sum(widths)]
    *staying, leaving = pl.pallas_call(
        partial(halves_kernel, len(held), sources),
        grid_spec=pltpu.PrefetchScalarGridSpec(
            num_scalar_prefetch=1,
            grid=(blocks,),
            in_specs=specs,
            out_specs=[pl.BlockSpec((1, rows, width), lambda index, where: (index, 0, 0)) for width in outs],
        ),
        out_shape=[jax.ShapeDtypeStruct((blocks, rows, width), jnp.float32) for width in outs],
        compiler_params=pltpu.CompilerParams(vmem_limit_bytes=VMEM_LIMIT),
        cost_estimate=SMALL,
        name="halves",
    )(where, *arrays)
    return staying, leaving


def input_specs(grads, weights, other):
    row_len, wide = grads.shape[0], grads.shape[1] // 3
    width = weights.shape[0]
    half = row_len // 2
    return [
        pl.BlockSpec((half, wide), lambda step, where: (1 - where[0] if other else where[0], step)),
        pl.BlockSpec((width, wide), lambda step, where: (0, step)),
    ], (half, width)


def input_other(where, grads, weights):
    specs, shape = input_specs(grads, weights, True)
    return call(
        other_kernel, "input_other", 3, where, (grads, weights), specs,
        [(jax.ShapeDtypeStruct(shape, jnp.float32), fixed_spec(shape))], {}, 2 * shape[0] * weights.size,
    )[0]


def input_own(where, grads, weights, arrived, block_in, there, res, gain):
    specs, shape = input_specs(grads, weights, False)
    mine = rows_spec(*shape, lambda step, where: where[0])
    moved = sum(array.size * array.dtype.itemsize for array in (grads, weights, arrived, block_in, there, res))
    return pl.pallas_call(
        input_kernel,
        grid_spec=pltpu.PrefetchScalarGridSpec(
            num_scalar_prefetch=1,
            grid=(3,),
            in_specs=specs + [fixed_spec(shape), mine, mine, fixed_spec(shape), fixed_spec((1, shape[1]))],
            out_specs=[fixed_spec(shape), fixed_spec((8, shape[1]))],
            scratch_shapes=[pltpu.VMEM(shape, jnp.float32)],
        ),
        out_shape=[jax.ShapeDtypeStruct(shape, jnp.float32), jax.ShapeDtypeStruct((8, shape[1]), jnp.float32)],
        compiler_params=pltpu.CompilerParams(vmem_limit_bytes=VMEM_LIMIT),
        cost_estimate=SMALL,
        name="input_own",
    )(where, grads, weights, arrived, block_in, there, res, gain[None])


def after(values, *others):
    return lax.optimization_barrier((values, others))[0]


def ordered(mine, other, bit, axis):
    low = jnp.where(bit == 0, mine, other)
    high = jnp.where(bit == 0, other, mine)
    return jnp.concatenate([low, high], axis=axis)


def body(
    dp_size,
    block_in,
    cotangent,
    lengths,
    pad_count,
    norm_in_attn,
    w_query,
    w_key,
    w_value,
    w_out,
    norm_out_attn,
    norm_in_mlp,
    w_up,
    w_down,
    norm_out_mlp,
):
    f32, bf16 = jnp.float32, jnp.bfloat16
    place = lax.axis_index("dp")
    core = lax.rem(place, 2)
    chip = lax.div(place, 2)
    side = lax.axis_index("tensor")
    same = core == side
    keep = same.astype(f32)
    first = (core == 0).astype(f32)
    chips = dp_size // 2
    levels = chips.bit_length() - 1
    bits = [lax.rem(lax.div(chip, 1 << level), 2) for level in range(levels)]
    swap = flat_pairs(dp_size, lambda d, c, t: (d ^ 1, 1 - t) if c != t else None)
    cross = flat_pairs(dp_size, lambda d, c, t: (d ^ 1, t))
    over = flat_pairs(dp_size, lambda d, c, t: (d, 1 - t))
    flips = [flat_pairs(dp_size, lambda d, c, t: (d ^ (2 << level), t)) for level in range(levels)]
    row_len, width = block_in.shape
    half = row_len // 2
    chunk = half // 2
    wide = w_query.shape[1]
    hidden = w_up.shape[1]

    shares = min(3, levels)
    near = flat_pairs(dp_size, lambda d, c, t: (d ^ 2, t) if c != t else None)

    orders = (list(range(levels)), [*range(1, levels), 0])
    hop_facts = []
    for step in range(levels):
        places = [sum(1 for later in order[step + 1 :] if later < order[step]) for order in orders]
        hop_facts.append(jnp.where(core == 0, places[0], places[1]))
        hop_facts.append(jnp.where(core == 0, bits[orders[0][step]], bits[orders[1][step]]))
    hops = [flat_pairs(dp_size, lambda d, c, t: (d ^ (2 << orders[c][step]), t)) for step in range(levels)]
    for bit in bits:
        hop_facts += [jnp.zeros_like(bit), bit]
    where_own = jnp.stack([core, same.astype(jnp.int32), *hop_facts])
    where_peer = jnp.stack([core, 1 - same.astype(jnp.int32)])
    out_rows = wide // 2
    weights_here = (w_query, w_key, w_value)
    part_rows = width >> shares
    which = sum(bits[level] << level for level in range(shares))
    parts_here = jnp.concatenate([half_of(weight, which, part_rows) for weight in weights_here], axis=1)
    w_out_sent = send(half_of(w_out, bits[0], out_rows).astype(f32), swap)
    attended_low, *sources = attention_forward(0, (block_in,), lengths, pad_count, norm_in_attn, w_query, w_key, w_value)
    low_sent = send(attended_low, swap)
    sources = after(sources, w_out_sent)
    w_out_sent = ordered(w_out_sent, send(w_out_sent, near), bits[0], 0)
    [attended_high] = attention_forward(1, sources, lengths, pad_count, norm_in_attn, w_query, w_key, w_value)
    high_sent = send(attended_high, swap)
    block_late, cot_late, facts = after((block_in, cotangent, jnp.pad(lengths, ((0, 0), (0, 1)))), low_sent, attended_high)
    facts = facts.astype(f32) + jnp.pad(pad_count.astype(f32)[:, None], ((0, 0), (lengths.shape[1], 0)))
    there = send(packed(where_own, block_late, cot_late), cross)
    facts_there = send(facts, cross)
    low_sent = after(low_sent, attended_high)
    attended = [(attended_low * keep + low_sent).astype(bf16), (attended_high * keep + high_sent).astype(bf16)]
    w_out_mine = (w_out.astype(f32) * keep + w_out_sent).astype(bf16)
    parts_sent = send(after(parts_here, attended[0]).astype(f32), swap)
    facts_row = jnp.where(same, facts, facts_there).astype(jnp.int32)
    docs = lengths.shape[1]
    lengths_row, pad_row = facts_row[:, :docs], facts_row[:, docs]
    part_other = sum(
        jnp.dot(half_of(values, 1 - core, half), w_out_mine[start : start + out_rows], preferred_element_type=f32)
        for values, start in zip(attended, (0, out_rows))
    )
    arrived = send(part_other, cross)
    hidden_own, attn_total, hidden_peer = [], [], []
    for number in range(2):
        one, total = hidden_chunk(where_own, number, attended, w_out_mine, arrived, block_in, there, norm_out_attn)
        hidden_own.append(one)
        attn_total.append(total)
        hidden_peer.append(send(one, over))

    gathered = 1 << shares
    groups = [
        [base + 2 * near_chip + one for near_chip in range(gathered)]
        for base in range(0, dp_size, 2 * gathered)
        for one in range(2)
    ]
    weights_sent = lax.all_gather(after(parts_sent, hidden_own[0]), "dp", axis=0, tiled=True, axis_index_groups=groups)

    buffers, slopes, parts, sums_own = (), [], [], []
    for number in range(4):
        piece = hidden_own[number] if number < 2 else hidden_peer[number - 2]
        if number > 1:
            piece = after(piece, parts[number - 1])
        *buffers, slope, part = mlp_forward(number, piece, norm_in_mlp, w_up, w_down, buffers)
        slopes.append(slope)
        parts.append(part)
        if number >= 2:
            sums_own.append(send(part, over))
    mlp_in_all, activated_all = buffers
    totals, blocks, back_parts, gain_out_mlp = [None] * 4, [None] * 4, [None] * 4, [None] * 4
    buffers = ()

    def add_up(number, gate):
        totals[number] = parts[number] + after(sums_own[number], gate)
        totals[number + 2] = send(totals[number], over)

    add_up(0, parts[3])
    gate = totals[0]
    for number in range(4):
        block, low_all, gain_sum, up_all, part = mlp_backward(
            where_own if number < 2 else where_peer,
            number,
            hidden_own[number] if number < 2 else hidden_peer[number - 2],
            after(totals[number], gate),
            cotangent,
            there,
            norm_out_mlp,
            w_down,
            w_up,
            slopes[number],
            buffers,
        )
        buffers = (low_all, up_all)
        blocks[number], back_parts[number], gain_out_mlp[number] = block, part, gain_sum[0]
        gate = part
        if number == 0:
            add_up(1, part)
            gate = totals[1]
    grad_low_all, grad_up_all = buffers
    sums_own = [send(part, over) for part in back_parts[2:]]

    def residual(number, arrived, buffers):
        return residual_chunk(
            where_own,
            number,
            back_parts[number],
            arrived,
            hidden_own[number],
            attn_total[number],
            cotangent,
            there,
            norm_in_mlp,
            norm_out_attn,
            buffers,
        )

    chip_rows = width // chips
    small = chip_rows // 2

    class Sum:
        def __init__(self, held, arrived, plain=False):
            self.plain = plain
            self.held = [part.reshape(chips, chip_rows, -1) for part in held]
            self.arrived = [] if arrived is None else [arrived.reshape(chips, chip_rows, -1)]
            self.sources = [None if arrived is None or number else (0, 0) for number in range(len(held))]
            self.step = 0

        def hop(self, *gates):
            arrived = [after(array, *gates) for array in self.arrived]
            self.held, leaving = halves(where_own, self.step + levels * self.plain, self.held, arrived, tuple(self.sources))
            self.arrived = [send(leaving, (flips if self.plain else hops)[self.step])]
            starts = np.cumsum([0, *(part.shape[2] for part in self.held)])
            self.sources = [(0, int(start)) for start in starts[:-1]]
            self.step += 1
            return leaving

        def result(self, *gates):
            while self.step < levels:
                gates = (self.hop(*gates),)
            arrived = [after(array, *gates) for array in self.arrived]
            return [
                (part + arrived[number][:, :, start : start + part.shape[2]]).reshape(chip_rows, -1)
                for part, (number, start) in zip(self.held, self.sources)
            ]

    def weight_part(columns):
        chosen = half_columns(activated_all, columns, hidden // 2)
        return jnp.einsum("td,tf->df", grad_low_all, chosen, preferred_element_type=f32)

    down_other = weight_part(1 - core)
    down_kept = weight_part(core)
    early = Sum([down_kept], send(down_other, cross))
    mlp_in_all, grad_up_all = after((mlp_in_all, grad_up_all), early.hop(down_kept))
    weight_up = jnp.einsum("td,tf->df", mlp_in_all, grad_up_all, preferred_element_type=f32)
    grad_up = lax.psum_scatter(weight_up, "dp", scatter_dimension=0, tiled=True)
    weights_late = after(weights_sent, weight_up)
    weights_mine = (jnp.concatenate(weights_here, axis=1).astype(f32) * keep + weights_late).astype(bf16)
    ready = attention_ready(where_own, block_in, there, lengths_row, pad_row, norm_in_attn, weights_mine)
    *buffers, gain_sum = residual(0, after(sums_own[0], ready[0]), ())
    gain_sums = [gain_sum]
    *buffers, gain_sum = residual(1, after(sums_own[1], gain_sum), buffers)
    gain_sums.append(gain_sum)
    grad_res, grad_attn = buffers
    gain_in_mlp = gain_sums[0][0] + gain_sums[1][0]
    gain_out_attn = gain_sums[0][1] + gain_sums[1][1]
    gain_out_mlp = gain_out_mlp[0] + gain_out_mlp[1]

    def to_output(values_own, values_peer):
        stay = jnp.where(same, values_own, values_peer)
        leave = jnp.where(same, values_peer, values_own)
        arrived = send(leave, cross)
        low = stay * first + arrived * (1.0 - first)
        high = arrived * first + stay * (1.0 - first)
        return jnp.concatenate([low, high], axis=0)

    grad_attn_other = send(grad_attn, cross)
    gate = early.hop(gain_sum)
    grad_attn_low = jnp.concatenate(
        [
            grad_attn * first + grad_attn_other * (1.0 - first),
            grad_attn_other * first + grad_attn * (1.0 - first),
        ],
        axis=0,
    ).astype(bf16)
    grad_heads = jnp.einsum("td,ed->te", grad_attn_low, w_out_mine, preferred_element_type=f32).astype(bf16)
    grads = attention_backward(ready, lengths_row, pad_row, after(grad_heads, gate))
    grads = jnp.concatenate(after(grads, early.hop(grads)), axis=1)
    late = Sum([jnp.einsum("td,te->de", ready[4], grads, preferred_element_type=f32)], None)
    gate = late.hop()
    other = input_other(where_own, after(grads, gate), weights_mine)
    other_sent = send(other, cross)
    attended_all = after(jnp.concatenate(attended, axis=1), other)
    weight_out = jnp.einsum("td,te->de", grad_attn_low, attended_all, preferred_element_type=f32)
    weight_out_sent = send(weight_out, swap)
    gate = weight_out
    grad_in_own, gain_in_attn = input_own(
        where_own, grads, weights_mine, after(other_sent, gate), block_in, there, grad_res, norm_in_attn
    )
    gains = jnp.stack([gain_in_attn[0], gain_out_attn, gain_in_mlp, gain_out_mlp], axis=0)
    gains = gains + send(gains, over)
    grad_in_sent = send(after(grad_in_own, gains), over)
    gate = late.hop(grad_in_own)
    weight_out_sent, gains = after((weight_out_sent, gains), grad_up, gate)
    gains = jnp.pad((gains + send(gains, cross)).T, ((0, 0), (0, LANES - 4)))
    weight_out = weight_out * keep + weight_out_sent
    out_sent = send(half_columns(weight_out, 1 - core, out_rows), cross)
    extra = Sum([half_columns(weight_out, core, out_rows), gains], out_sent, plain=True)
    gate = extra.hop(gate)
    gate = extra.hop(gate)
    gate = late.hop(gate)
    gate = extra.hop(gate)
    [grad_down] = early.result(gate)
    [held] = late.result(gate)
    for_core = half_of(held, core, small)
    for_other = half_of(held, 1 - core, small)
    for_other, leaving = lax.optimization_barrier((for_other, jnp.where(same, for_other, for_core)))
    diagonal = send(for_other, swap)
    straight = send(
        leaving,
        flat_pairs(dp_size, lambda d, c, t: (d, 1 - t) if c != t else (d ^ 1, t)),
    )
    grad_out, gains = extra.result(leaving)

    def to_core(*parts):
        leaving = jnp.concatenate([half_of(part, 1 - core, small) for part in parts], axis=1)
        arrived, start, results = send(leaving, cross), 0, []
        for part in parts:
            columns = part.shape[1]
            results.append(ordered(half_of(part, core, small), arrived[:, start : start + columns], core, 1))
            start += columns
        return results

    def to_output(values_own, values_peer):
        stay = jnp.where(same, values_own, values_peer)
        leave = jnp.where(same, values_peer, values_own)
        arrived = send(leave, cross)
        low = stay * first + arrived * (1.0 - first)
        high = arrived * first + stay * (1.0 - first)
        return jnp.concatenate([low, high], axis=0)

    grad_down, grad_out = to_core(grad_down, grad_out)
    grad_in = to_output(grad_in_own, after(grad_in_sent, gate))
    heads = straight + jnp.where(same, for_core, diagonal)
    gains = half_of(gains, core, small)[:, :4].T
    block_out = to_output(jnp.concatenate(blocks[:2], axis=0), jnp.concatenate(blocks[2:], axis=0)).astype(bf16)
    return (
        block_out,
        grad_in,
        gains[0],
        heads[:, :wide],
        heads[:, wide : 2 * wide],
        heads[:, 2 * wide : 3 * wide],
        grad_out.T,
        gains[1],
        gains[2],
        grad_up,
        grad_down.T,
        gains[3],
    )


def solution(mesh):
    placed = (
        P("dp", None),
        P("dp", None),
        P("dp", None),
        P("dp"),
        P(),
        P(None, "tensor"),
        P(None, "tensor"),
        P(None, "tensor"),
        P("tensor", None),
        P(),
        P(),
        P(None, "tensor"),
        P("tensor", None),
        P(),
    )
    return jax.shard_map(
        partial(body, mesh.shape["dp"]),
        mesh=mesh,
        in_specs=placed,
        out_specs=(
            P("dp", None),
            P("dp", None),
            P("dp"),
            P("dp", "tensor"),
            P("dp", "tensor"),
            P("dp", "tensor"),
            P("tensor", "dp"),
            P("dp"),
            P("dp"),
            P("dp", "tensor"),
            P("tensor", "dp"),
            P("dp"),
        ),
        check_vma=False,
    )
```
